32 devices in a mesh: lat: 4 (over y, core), lon: 8 (over z, x).
Axes of the slice: x: 2, y: 2, z: 4, core: 2. Of those that a mesh axis runs over, the one named last changes fastest.
Arguments:
- tracers: float32 [128, 768, 128], P('lat', 'lon'), may hold values from -6 to 6
- owners: int32 [4, 8, 3072, 1], P('lat', 'lon'), may hold values from 0 to 7; in each aligned block of 3072 rows (0 to 3071, 3072 to 6143, ..., all dimensions but the last counted through in order) at most 1152 rows name the same one
- columns: int32 [128, 768], P('lat', 'lon'), may hold values from 0 to 95
- lat_shift: int32 [128, 768], P('lat', 'lon'), may hold values from 0 to 2
- fractions: float32 [2, 128, 768], P(None, 'lat', 'lon'), may hold values from 0 to 1
Outputs:
- advected: float32 [128, 768, 128], P('lat', 'lon')
The draws below stay inside these ranges and needn't reach their ends.
Inputs may be any that keep to these rules, and one draw needn't show every extreme that they name: `owners`: among the 3072 cells of one device no sector is named more than 1152 times, a bound that some block reaches.
All inputs are finite; a program needn't handle non-finite values.
Results may differ from the reference program's by a relative error of at most 0.0003.
Values sent between devices are 32-bit elements; how exact they have to be, the bound alone decides.
No kernel may reach another device: no remote copies, remote signals or barrier semaphores. Data moves between devices by JAX's collectives and lax.ppermute only.
A program may use at most 192 MiB of HBM per device.

```python
import math
import jax
import jax.numpy as jnp
import numpy as np
from jax import lax

LAT_DEV = 32
LON_DEV = 96
C = 128
BANDS = 4
SECTORS = 8
NLAT = 128
NLON = 768
CELLS = 3072
CAP = 1152


def touch_ends(result, own_key, low, top_value):
    shape = result.shape
    spot = [jax.random.randint(jax.random.fold_in(own_key, axis), (), 0, shape[axis]) for axis in range(len(shape))]
    result = result.at[tuple(spot)].set(low)
    longest = shape.index(max(shape))
    spot[longest] = (spot[longest] + 1) % shape[longest]
    return result.at[tuple(spot)].set(top_value)


def level_of(rng, shape, pieces, least, high):
    gain = 1.0
    for axis_at, blocks in pieces:
        heights = jax.random.uniform(jax.random.fold_in(jax.random.fold_in(rng, 6), axis_at), (blocks,), jnp.float32, least / len(pieces), high / len(pieces))
        gain = gain * jnp.repeat(jnp.exp(heights), shape[axis_at] // blocks).reshape((-1,) + (1,) * (len(shape) - 1 - axis_at))
    return gain


def shared_out(own_key, own, number, rows, count, top, most, lean):
    ranking = jax.random.permutation(own_key, count)
    crowded, usual = portions_of(count, rows * top, most, lean, True), portions_of(count, rows * top, most, lean, False)
    places = jnp.arange(count)

    def named(tallies, offset_by):
        used = int((tallies > 0).sum())
        fixed = max(1, used // 4)
        shifted = fixed + (places - fixed + offset_by * (used - fixed)) % max(1, count - fixed)
        return jnp.zeros((count,), jnp.int32).at[ranking[jnp.where(places < fixed, places, shifted)]].set(jnp.asarray(tallies, jnp.int32))

    tallies = jnp.where(number % 4 == 0, named(crowded, number // 4), named(usual, number - number // 4 - 1))
    mixed = jax.random.permutation(jax.random.fold_in(own, 3), count)
    giver, sink = mixed[0:count // 2 * 2:2], mixed[1:count // 2 * 2:2]
    room = jnp.minimum(tallies[giver] - 1, most - tallies[sink]) // 2
    room = jnp.where((giver == ranking[0]) | (sink == ranking[0]) | (tallies[sink] == 0), 0, jnp.maximum(room, 0))
    shifted = jax.random.randint(jax.random.fold_in(own, 4), (count // 2,), 0, 1 << 20) % (room + 1)
    tallies = tallies.at[giver].add(-shifted).at[sink].add(shifted)
    items = jnp.searchsorted(jnp.cumsum(tallies), jnp.arange(rows * top), side="right").astype(jnp.int32)
    table = items.reshape(top, rows).T
    table = table[jax.random.permutation(jax.random.fold_in(own, 1), rows)]
    offset_by = jax.random.randint(jax.random.fold_in(own, 2), (rows, 1), 0, top)
    return jnp.take_along_axis(table, (jnp.arange(top)[None, :] + offset_by) % top, axis=1)


def portions_of(amount, total, bound, lean, full):
    weights = [(1 << 20) // math.isqrt(rank ** lean) + 1 for rank in range(1, amount + 1)]
    largest = bound if full else min(bound, max(-(-total // amount), total * weights[0] // sum(weights)))
    least = 1 if total - largest >= amount - 1 else 0
    given, spare = [largest] + [least] * (amount - 1), total - largest - least * (amount - 1)
    while spare > 0:
        movable = [i for i in range(1, amount) if given[i] < largest] or [i for i in range(1, amount) if given[i] < bound]
        whole, left = sum([weights[i] for i in movable]), spare
        for i in movable:
            addition = min(bound - given[i], max(1, left * weights[i] // whole), spare)
            given[i] = given[i] + addition
            spare = spare - addition
    return np.array(given)


def bell_draw(own_key, shape, spread, limit, pieces=(), held_as=jnp.bfloat16):
    values = jax.random.normal(own_key, shape, jnp.float32) * spread
    if len(pieces) > 0:
        values = level_of(own_key, shape, pieces, -0.22, 0.18) * values
    return jnp.clip(values, min=-limit, max=limit).astype(held_as)


def setup_inputs(seed: int = 0) -> dict:
    key_list = jax.random.split(jax.random.key(seed), 6)
    tracers = bell_draw(key_list[0], (NLAT, NLON, C), 1.0, 6.0, ((0, 4), (1, 8)), jnp.float32)
    owners_keys = jax.random.split(jax.random.fold_in(key_list[1], 1), BANDS * SECTORS * CELLS // CELLS)
    owners_turns = jax.random.permutation(jax.random.fold_in(key_list[1], 3), BANDS * SECTORS * CELLS // CELLS)
    owners = jax.vmap(lambda own, number: shared_out(jax.random.fold_in(key_list[1], 2), own, number, CELLS, SECTORS, 1, CAP, 2))(owners_keys, owners_turns).reshape((BANDS, SECTORS, CELLS, 1))
    columns = touch_ends(jax.random.randint(key_list[2], (NLAT, NLON), 0, LON_DEV), jax.random.fold_in(key_list[2], 1), 0, LON_DEV - 1).astype(jnp.int32)
    lat_shift = touch_ends(jax.random.randint(key_list[3], (NLAT, NLON), 0, 3), jax.random.fold_in(key_list[3], 1), 0, 2).astype(jnp.int32)
    fractions = jnp.clip(1.0 * jax.random.uniform(key_list[4], (2, NLAT, NLON), jnp.float32) ** level_of(key_list[4], (2, NLAT, NLON), ((1, 4), (2, 8)), -0.2, 0.2), 0.0, 1.0)
    return {"tracers": tracers, "owners": owners, "columns": columns, "lat_shift": lat_shift, "fractions": fractions}


def spline_weights(shift):
    rest = 1.0 - shift
    cube = shift * shift * shift
    return [rest * rest * rest / 6.0, (3.0 * cube - 6.0 * shift * shift + 4.0) / 6.0, (-3.0 * cube + 3.0 * shift * shift + 3.0 * shift + 1.0) / 6.0, cube / 6.0]

def reference(tracers, owners, columns, lat_shift, fractions):
    lat_total, lon_total, channels = tracers.shape
    dtype = tracers.dtype
    row_ids = jnp.arange(lat_total, dtype=jnp.int32)
    fixed_row = (row_ids == 0) | (row_ids == lat_total - 1)
    diagonal = jnp.where(fixed_row, 1.0, 4.0 / 6.0).astype(dtype)
    off_diag = jnp.where(fixed_row, 0.0, 1.0 / 6.0).astype(dtype)
    solved = lax.linalg.tridiagonal_solve(off_diag, diagonal, off_diag, tracers.reshape(lat_total, lon_total * channels))
    solved = solved.reshape(lat_total, lon_total, channels)
    spectrum = jnp.fft.rfft(solved, axis=1)
    freqs = jnp.arange(lon_total // 2 + 1).astype(dtype)
    symbol = (4.0 + 2.0 * jnp.cos(2.0 * math.pi * freqs / lon_total)) / 6.0
    coeffs = jnp.fft.irfft(spectrum / symbol[None, :, None], n=lon_total, axis=1).astype(dtype)
    sector = owners.reshape(BANDS, SECTORS, LAT_DEV, LON_DEV).transpose(0, 2, 1, 3).reshape(lat_total, lon_total)
    lon_dep = (sector * LON_DEV + columns).astype(jnp.int32)
    lat_dep = jnp.clip(row_ids[:, None] - 1 + lat_shift, 1, lat_total - 3).astype(jnp.int32)
    lat_weights = jnp.stack(spline_weights(fractions[0]), axis=1)
    lon_weights = jnp.stack(spline_weights(fractions[1]), axis=1)

    def one_row(items):
        lat_row, lon_row, lat_w, lon_w = items
        total = jnp.zeros((lon_total, channels), dtype)
        for lat_tap in range(4):
            for lon_tap in range(4):
                picked = coeffs[lat_row - 1 + lat_tap, (lon_row - 1 + lon_tap) % lon_total]
                total = total + (lat_w[lat_tap] * lon_w[lon_tap])[:, None] * picked
        return total
    return lax.map(one_row, (lat_dep, lon_dep, lat_weights, lon_weights))
```

```python
import functools
import math

import jax
import jax.numpy as jnp
import numpy as np
from jax import lax
from jax.experimental import pallas as pl
from jax.experimental.pallas import tpu as pltpu
from jax.sharding import PartitionSpec as P

POLE = math.sqrt(3.0) - 2.0
GAIN = math.sqrt(3.0)
LANES = 128
TAPS = 6
UP, DOWN = 2, 3
LEFT, RIGHT = 1, 2
BF = jnp.bfloat16
F32 = jnp.float32
VMEM_LIMIT = 60 * 1024 * 1024


def split(x):
    high = x.astype(BF)
    return high, (x - high.astype(F32)).astype(BF)


def dot(a, b):
    return lax.dot_general(a, b, (((1,), (0,)), ((), ())), preferred_element_type=F32)


def spline_weights(shift):
    rest = 1.0 - shift
    cube = shift * shift * shift
    return [
        rest * rest * rest / 6.0,
        (3.0 * cube - 6.0 * shift * shift + 4.0) / 6.0,
        (-3.0 * cube + 3.0 * shift * shift + 3.0 * shift + 1.0) / 6.0,
        cube / 6.0,
    ]


def edge_kernel(s_ref, down_ref, up_ref, top_ref, bottom_ref):
    rows = s_ref.shape[0]
    first, last = s_ref[0], s_ref[rows - 1]
    far = 1.0 / (1.0 - POLE)

    acc = s_ref[0]
    for r in range(1, rows - UP):
        acc = s_ref[r] + POLE * acc
        if r == rows - 2 - DOWN:
            bottom_ref[DOWN] = 2.0 * far * last - acc
    down_ref[0] = acc
    for k in range(UP):
        down_ref[1 + k] = s_ref[rows - UP + k]
    for k in range(DOWN):
        bottom_ref[k] = 2.0 * last - s_ref[rows - 2 - k]

    acc = s_ref[rows - 1]
    for r in range(rows - 2, DOWN - 1, -1):
        acc = s_ref[r] + POLE * acc
    up_ref[DOWN] = acc
    for k in range(DOWN):
        up_ref[k] = s_ref[k]
    low = s_ref[rows - 1]
    for r in range(rows - 2, UP, -1):
        low = s_ref[r] + POLE * low
    top_ref[0] = 2.0 * far * first - low
    for k in range(UP):
        top_ref[1 + k] = 2.0 * first - s_ref[UP - k]


def edges(s):
    rows, cols, ch = s.shape
    shape = lambda n: jax.ShapeDtypeStruct((n, cols, ch), F32)
    return pl.pallas_call(
        edge_kernel,
        out_shape=(shape(UP + 1), shape(DOWN + 1), shape(UP + 1), shape(DOWN + 1)),
        cost_estimate=pl.CostEstimate(flops=6 * s.size, bytes_accessed=6 * s.size, transcendentals=0),
        compiler_params=pltpu.CompilerParams(vmem_limit_bytes=VMEM_LIMIT),
        name="edges",
    )(s)


def lat_kernel(s_ref, above_ref, below_ref, top_ref, bottom_ref, wr_ref, wl_ref, out_ref, right_ref, left_ref):
    rows, cols, _ = s_ref.shape
    band = lax.axis_index("lat")
    at_top = band == 0
    at_bottom = band == lax.axis_size("lat") - 1
    total = rows + UP + DOWN

    def row(e):
        if e < UP:
            return jnp.where(at_top, top_ref[1 + e], above_ref[1 + e])
        if e >= UP + rows:
            return jnp.where(at_bottom, bottom_ref[e - UP - rows], below_ref[e - UP - rows])
        return s_ref[e - UP]

    acc = jnp.where(at_bottom, bottom_ref[DOWN], below_ref[DOWN])
    for e in range(total - 1, -1, -1):
        acc = POLE * acc
        out_ref[e] = acc
        acc = acc + row(e)
    acc = jnp.where(at_top, top_ref[0], above_ref[0])
    for e in range(total):
        acc = row(e) + POLE * acc
        value = GAIN * (out_ref[e] + acc)
        out_ref[e] = value
        right_ref[0, pl.ds(e, 1)] = jnp.sum(value * wr_ref[...], axis=0, keepdims=True)
        for k in range(LEFT):
            right_ref[1 + k, pl.ds(e, 1)] = value[cols - LEFT + k : cols - LEFT + k + 1]
        for k in range(RIGHT):
            left_ref[k, pl.ds(e, 1)] = value[k : k + 1]
        left_ref[RIGHT, pl.ds(e, 1)] = jnp.sum(value * wl_ref[...], axis=0, keepdims=True)


def lat_solve(s, above, below, top, bottom):
    rows, cols, ch = s.shape
    total = rows + UP + DOWN
    place = np.arange(cols)
    wr = np.where(place < cols - LEFT, POLE ** np.maximum(cols - LEFT - 1 - place, 0), 0.0)
    wl = np.where(place >= RIGHT, POLE ** np.maximum(place - RIGHT, 0), 0.0)
    wide = lambda w: jnp.asarray(np.broadcast_to(w[:, None], (cols, ch)).astype(np.float32))
    return pl.pallas_call(
        lat_kernel,
        out_shape=(
            jax.ShapeDtypeStruct((total, cols, ch), F32),
            jax.ShapeDtypeStruct((LEFT + 1, total, ch), F32),
            jax.ShapeDtypeStruct((RIGHT + 1, total, ch), F32),
        ),
        cost_estimate=pl.CostEstimate(flops=10 * s.size, bytes_accessed=10 * s.size, transcendentals=0),
        compiler_params=pltpu.CompilerParams(vmem_limit_bytes=VMEM_LIMIT),
        name="lat_solve",
    )(s, above, below, top, bottom, wide(wr), wide(wl))


def lon_kernel(x_ref, west_ref, east_ref, gh_ref, gl_ref, out_ref):
    total, cols, ch = x_ref.shape
    pad = LANES - cols - (LEFT + RIGHT + 2)
    for e in range(total):
        parts = [x_ref[e]]
        parts += [west_ref[k, pl.ds(e, 1)] for k in range(LEFT + 1)]
        parts += [east_ref[k, pl.ds(e, 1)] for k in range(RIGHT + 1)]
        parts += [jnp.zeros((pad, ch), F32)]
        turned = jnp.concatenate(parts, axis=0).T
        high, low = split(turned)
        both = jnp.concatenate([high, low], axis=0)
        main = dot(both, gh_ref[...])
        value = main[:ch] + main[ch:] + dot(high, gl_ref[...])
        high, low = split(value)
        out_ref[:ch, e * LANES : (e + 1) * LANES] = high
        out_ref[ch:, e * LANES : (e + 1) * LANES] = low


def lon_solve(x, west, east):
    total, cols, ch = x.shape
    width = cols + LEFT + RIGHT
    j = np.arange(width) - LEFT
    green = np.zeros((LANES, LANES))
    green[:cols, :width] = POLE ** np.abs(np.arange(cols)[:, None] - j[None, :])
    green[cols, :width] = POLE ** (j + LEFT + 1)
    for k in range(LEFT):
        green[cols + 1 + k, :width] = POLE ** np.abs(j - (k - LEFT))
    for k in range(RIGHT):
        green[cols + LEFT + 1 + k, :width] = POLE ** np.abs(j - (cols + k))
    green[cols + LEFT + 1 + RIGHT, :width] = POLE ** (cols + RIGHT - j)
    green = jnp.asarray((GAIN * green).astype(np.float32))
    high, low = split(green)
    return pl.pallas_call(
        lon_kernel,
        out_shape=jax.ShapeDtypeStruct((2 * ch, total * LANES), BF),
        cost_estimate=pl.CostEstimate(
            flops=6 * total * LANES * LANES * ch, bytes_accessed=8 * x.size, transcendentals=0
        ),
        compiler_params=pltpu.CompilerParams(vmem_limit_bytes=VMEM_LIMIT),
        name="lon_solve",
    )(x, west, east, high, low)


def tap_kernel(dest_ref, base_ref, ct_ref, cells_ref, tri_ref, out_ref, rank, wh, wl, packed, sem, *, cap, span):
    rows = cells_ref.shape[2]
    ch = ct_ref.shape[0] // 2
    me = lax.axis_index("lon").astype(F32)
    band = lax.axis_index("lat")
    lat_total = rows * lax.axis_size("lat")
    wh[...] = jnp.zeros_like(wh)
    wl[...] = jnp.zeros_like(wl)
    mine = cells_ref[0, 0] == me
    before = dot(jnp.where(mine, 1.0, 0.0).astype(BF), tri_ref[...])
    rank[...] = jnp.where(mine, before, -1000.0)
    column = lax.broadcasted_iota(jnp.int32, (span, LANES), 0).astype(F32)
    step = lax.broadcasted_iota(jnp.int32, (8, LANES), 0)
    first = dest_ref[0] * rows

    @pl.loop(0, rows)
    def _(i):
        here = pl.ds(i, 1)
        one = jnp.where(cells_ref[0, 0, here] == me, 1.0, 0.0)
        a = spline_weights(cells_ref[0, 3, here])
        b = [w * one for w in spline_weights(cells_ref[0, 4, here])]
        glob = band * rows + i
        start = i - jnp.where(glob == lat_total - 1, 1, 0)
        dep = jnp.clip(glob.astype(F32) - 1.0 + cells_ref[0, 2, here], 1.0, lat_total - 3.0)
        turn = dep - (glob - i + start - 1).astype(F32)
        far = column - cells_ref[0, 1, here]
        basis = jnp.where(
            far == 0.0, b[0], jnp.where(far == 1.0, b[1], jnp.where(far == 2.0, b[2], jnp.where(far == 3.0, b[3], 0.0)))
        )
        zero = jnp.zeros_like(one)
        for e in range(TAPS):
            lat_w = zero
            for t in range(3):
                if 0 <= e - t < 4:
                    lat_w = jnp.where(turn == float(t), a[e - t], lat_w)
            high, low = split(basis * lat_w)
            wh[e * LANES : e * LANES + span] = high
            wl[e * LANES : e * LANES + span] = low
        window = pl.ds(pl.multiple_of(start * LANES, LANES), TAPS * LANES)
        main = dot(ct_ref[:, window], wh[...])
        value = main[:ch] + main[ch:] + dot(ct_ref[:ch, window], wl[...])
        high, low = split(value)
        base = base_ref[first + i]
        odd = lax.rem(base, 8)
        spot = rank[here] + odd.astype(F32)
        pick = jnp.where(column == spot, 1.0, 0.0).astype(BF)
        got = lax.dot_general(
            jnp.concatenate([pick, pick], axis=1),
            jnp.concatenate([high, low], axis=1),
            (((1,), (1,)), ((), ())),
            preferred_element_type=F32,
        )
        at = pl.multiple_of(base - odd, 8)
        packed[pl.ds(at, 8)] = jnp.where(step < odd, packed[pl.ds(at, 8)], got[:8])
        packed[pl.ds(pl.multiple_of(at + 8, 8), span - 8)] = got[8:]

    copy = pltpu.make_async_copy(packed.at[pl.ds(0, cap)], out_ref, sem)
    copy.start()
    copy.wait()


def taps(dest, base, ct, cells, cap):
    count, words, rows, lanes = cells.shape
    ch = ct.shape[0] // 2
    span = 104
    tri = jnp.asarray(np.triu(np.ones((lanes, lanes)), 1), BF)
    return pl.pallas_call(
        functools.partial(tap_kernel, cap=cap, span=span),
        out_shape=jax.ShapeDtypeStruct((cap, ch), F32),
        grid_spec=pltpu.PrefetchScalarGridSpec(
            num_scalar_prefetch=2,
            grid=(1,),
            in_specs=[
                pl.BlockSpec(ct.shape, lambda g, d, b: (0, 0)),
                pl.BlockSpec((1, words, rows, lanes), lambda g, d, b: (d[0], 0, 0, 0)),
                pl.BlockSpec(tri.shape, lambda g, d, b: (0, 0)),
            ],
            out_specs=pl.BlockSpec(memory_space=pl.ANY),
            scratch_shapes=[
                pltpu.VMEM((rows, lanes), F32),
                pltpu.VMEM((TAPS * LANES, lanes), BF),
                pltpu.VMEM((TAPS * LANES, lanes), BF),
                pltpu.VMEM((cap + span + 8, ch), F32),
                pltpu.SemaphoreType.DMA,
            ],
        ),
        cost_estimate=pl.CostEstimate(
            flops=6 * rows * TAPS * LANES * ch * LANES, bytes_accessed=2 * ct.size, transcendentals=0
        ),
        compiler_params=pltpu.CompilerParams(vmem_limit_bytes=VMEM_LIMIT),
        name="taps",
    )(dest, base, ct, cells, tri)


def place_kernel(target_ref, *refs, cap):
    *parts, out_ref, gathered, sems = refs
    copies = [
        pltpu.make_async_copy(part, gathered.at[pl.ds(k * cap, cap)], sems.at[k]) for k, part in enumerate(parts)
    ]
    for copy in copies:
        copy.start()
    for copy in copies:
        copy.wait()

    @pl.loop(0, out_ref.shape[0] // 8)
    def _(group):
        at = pl.multiple_of(group * 8, 8)
        lines = [gathered[pl.ds(target_ref[at + k], 1)] for k in range(8)]
        out_ref[pl.ds(at, 8)] = jnp.concatenate(lines, axis=0)


def place(target, parts):
    cap, ch = parts[0].shape
    cells = target.shape[0]
    count = len(parts)
    return pl.pallas_call(
        functools.partial(place_kernel, cap=cap),
        out_shape=jax.ShapeDtypeStruct((cells, ch), F32),
        grid_spec=pltpu.PrefetchScalarGridSpec(
            num_scalar_prefetch=1,
            grid=(1,),
            in_specs=[pl.BlockSpec(memory_space=pl.ANY)] * count,
            out_specs=pl.BlockSpec((cells, ch), lambda g, t: (0, 0)),
            scratch_shapes=[pltpu.VMEM((count * cap, ch), F32), pltpu.SemaphoreType.DMA((count,))],
        ),
        cost_estimate=pl.CostEstimate(flops=0, bytes_accessed=8 * count * cap * ch, transcendentals=0),
        compiler_params=pltpu.CompilerParams(vmem_limit_bytes=VMEM_LIMIT),
        name="place",
    )(target, *parts)


def earlier(mask):
    rows, cols = mask.shape[1:]
    ones = mask.astype(F32)
    before = lax.dot_general(
        mask.astype(BF),
        jnp.asarray(np.triu(np.ones((cols, cols)), 1), BF),
        (((2,), (0,)), ((), ())),
        preferred_element_type=F32,
    )
    return before, bases(ones)


def bases(ones):
    rows = ones.shape[1]
    totals = jnp.sum(ones, axis=2)
    return jnp.dot(totals, jnp.asarray(np.triu(np.ones((rows, rows)), 1), F32), precision=lax.Precision.HIGHEST)


def body(tracers, owners, columns, lat_shift, fractions):
    rows, cols, ch = tracers.shape
    bands = lax.axis_size("lat")
    sectors = lax.axis_size("lon")
    me = lax.axis_index("lon")
    cells = rows * cols
    cap = 3 * cells // sectors

    down, up, top, bottom = edges(tracers)
    above = lax.ppermute(down, "lat", [(i, i + 1) for i in range(bands - 1)])
    below = lax.ppermute(up, "lat", [(i + 1, i) for i in range(bands - 1)])

    owner = owners.reshape(rows, cols)
    words = jnp.stack(
        [owner.astype(F32), columns.astype(F32), lat_shift.astype(F32), fractions[0], fractions[1]], axis=0
    )
    words = jnp.pad(words, ((0, 0), (0, 0), (0, LANES - cols)), constant_values=-1.0)
    asked = lax.all_to_all(
        jnp.broadcast_to(words[None], (sectors,) + words.shape), "lon", split_axis=0, concat_axis=0, tiled=True
    )

    x, right, left = lat_solve(tracers, above, below, top, bottom)
    west = lax.ppermute(right, "lon", [(i, (i + 1) % sectors) for i in range(sectors)])
    east = lax.ppermute(left, "lon", [((i + 1) % sectors, i) for i in range(sectors)])

    base = bases((asked[:, 0] == me.astype(F32)).astype(F32)).astype(jnp.int32).reshape(-1)
    every = jnp.arange(sectors, dtype=jnp.int32)
    mask = owner[None] == every[:, None, None]
    before, own_base = earlier(mask)
    slot = jnp.sum(jnp.where(mask, before + own_base[:, :, None], 0.0), axis=0).astype(jnp.int32)
    target = ((me - owner) % sectors * cap + slot).reshape(cells)

    ct = lon_solve(x, west, east)
    parts = [None] * sectors
    for k in sorted(range(sectors), key=lambda k: (k == 0, abs(2 * k - sectors))):
        dest = ((me + k) % sectors).reshape(1)
        value = taps(dest, base, ct, asked, cap)
        if k:
            value = lax.ppermute(value, "lon", [(i, (i + k) % sectors) for i in range(sectors)])
        parts[k] = value
    return place(target, parts).reshape(rows, cols, ch)


def solution(mesh):
    in_specs = (
        P("lat", "lon", None),
        P("lat", "lon", None, None),
        P("lat", "lon"),
        P("lat", "lon"),
        P(None, "lat", "lon"),
    )
    out_specs = P("lat", "lon", None)
    return jax.shard_map(body, mesh=mesh, in_specs=in_specs, out_specs=out_specs, check_vma=False)
```

```python
import functools
import math

import jax
import jax.numpy as jnp
import numpy as np
from jax import lax
from jax.experimental import pallas as pl
from jax.experimental.pallas import tpu as pltpu
from jax.sharding import PartitionSpec as P

POLE = math.sqrt(3.0) - 2.0
GAIN = math.sqrt(3.0)
LANES = 128
TAPS = 6
UP, DOWN = 2, 3
LEFT, RIGHT = 1, 2
BF = jnp.bfloat16
F32 = jnp.float32
VMEM_LIMIT = 60 * 1024 * 1024


def split(x):
    high = x.astype(BF)
    return high, (x - high.astype(F32)).astype(BF)


def thirds(x):
    high, low = split(x)
    return jnp.concatenate([high, low, high], axis=1)


def dot(a, b):
    return lax.dot_general(a, b, (((1,), (0,)), ((), ())), preferred_element_type=F32)


def spline_weights(shift):
    rest = 1.0 - shift
    cube = shift * shift * shift
    return [
        rest * rest * rest / 6.0,
        (3.0 * cube - 6.0 * shift * shift + 4.0) / 6.0,
        (-3.0 * cube + 3.0 * shift * shift + 3.0 * shift + 1.0) / 6.0,
        cube / 6.0,
    ]


def edge_kernel(
    s_ref, owner_ref, column_ref, shift_ref, frac_ref, down_ref, up_ref, top_ref, bottom_ref, words_ref
):
    rows, cols = s_ref.shape[:2]
    top_row = lax.axis_index("lat") * rows
    lat_total = rows * lax.axis_size("lat")
    arrival = lax.broadcasted_iota(jnp.int32, (rows, cols), 0) + top_row
    row = jnp.clip(arrival - 1 + shift_ref[...], 1, lat_total - 3).astype(F32)
    column = (owner_ref[...] * cols + column_ref[...]).astype(F32)
    for k in range(words_ref.shape[0]):
        for w, word in enumerate((column, row, frac_ref[0], frac_ref[1])):
            words_ref[k, w] = jnp.full((rows, LANES), -1.0, F32)
            words_ref[k, w, :, :cols] = word
    first, last = s_ref[0], s_ref[rows - 1]
    far = 1.0 / (1.0 - POLE)

    acc = s_ref[0]
    for r in range(1, rows - UP):
        acc = s_ref[r] + POLE * acc
        if r == rows - 2 - DOWN:
            bottom_ref[DOWN] = 2.0 * far * last - acc
    down_ref[0] = acc
    for k in range(UP):
        down_ref[1 + k] = s_ref[rows - UP + k]
    for k in range(DOWN):
        bottom_ref[k] = 2.0 * last - s_ref[rows - 2 - k]

    acc = s_ref[rows - 1]
    for r in range(rows - 2, DOWN - 1, -1):
        acc = s_ref[r] + POLE * acc
    up_ref[DOWN] = acc
    for k in range(DOWN):
        up_ref[k] = s_ref[k]
    low = s_ref[rows - 1]
    for r in range(rows - 2, UP, -1):
        low = s_ref[r] + POLE * low
    top_ref[0] = 2.0 * far * first - low
    for k in range(UP):
        top_ref[1 + k] = 2.0 * first - s_ref[UP - k]


def edges(s, owner, columns, lat_shift, fractions):
    rows, cols, ch = s.shape
    shape = lambda n: jax.ShapeDtypeStruct((n, cols, ch), F32)
    words = jax.ShapeDtypeStruct((lax.axis_size("lon"), 4, rows, LANES), F32)
    return pl.pallas_call(
        edge_kernel,
        out_shape=(shape(UP + 1), shape(DOWN + 1), shape(UP + 1), shape(DOWN + 1), words),
        cost_estimate=pl.CostEstimate(flops=6 * s.size, bytes_accessed=6 * s.size, transcendentals=0),
        compiler_params=pltpu.CompilerParams(vmem_limit_bytes=VMEM_LIMIT),
        name="edges",
    )(s, owner, columns, lat_shift, fractions)


def lat_kernel(s_ref, above_ref, below_ref, top_ref, bottom_ref, wr_ref, wl_ref, out_ref, right_ref, left_ref):
    rows, cols, _ = s_ref.shape
    band = lax.axis_index("lat")
    at_top = band == 0
    at_bottom = band == lax.axis_size("lat") - 1
    total = rows + UP + DOWN

    def row(e):
        if e < UP:
            return jnp.where(at_top, top_ref[1 + e], above_ref[1 + e])
        if e >= UP + rows:
            return jnp.where(at_bottom, bottom_ref[e - UP - rows], below_ref[e - UP - rows])
        return s_ref[e - UP]

    acc = jnp.where(at_bottom, bottom_ref[DOWN], below_ref[DOWN])
    for e in range(total - 1, -1, -1):
        acc = POLE * acc
        out_ref[e] = acc
        acc = acc + row(e)
    acc = jnp.where(at_top, top_ref[0], above_ref[0])
    for e in range(total):
        acc = row(e) + POLE * acc
        value = GAIN * (out_ref[e] + acc)
        out_ref[e] = value
        right_ref[0, pl.ds(e, 1)] = jnp.sum(value * wr_ref[...], axis=0, keepdims=True)
        for k in range(LEFT):
            right_ref[1 + k, pl.ds(e, 1)] = value[cols - LEFT + k : cols - LEFT + k + 1]
        for k in range(RIGHT):
            left_ref[k, pl.ds(e, 1)] = value[k : k + 1]
        left_ref[RIGHT, pl.ds(e, 1)] = jnp.sum(value * wl_ref[...], axis=0, keepdims=True)


def lat_solve(s, above, below, top, bottom):
    rows, cols, ch = s.shape
    total = rows + UP + DOWN
    place = np.arange(cols)
    wr = np.where(place < cols - LEFT, POLE ** np.maximum(cols - LEFT - 1 - place, 0), 0.0)
    wl = np.where(place >= RIGHT, POLE ** np.maximum(place - RIGHT, 0), 0.0)
    wide = lambda w: jnp.asarray(np.broadcast_to(w[:, None], (cols, ch)).astype(np.float32))
    return pl.pallas_call(
        lat_kernel,
        out_shape=(
            jax.ShapeDtypeStruct((total, cols, ch), F32),
            jax.ShapeDtypeStruct((LEFT + 1, total, ch), F32),
            jax.ShapeDtypeStruct((RIGHT + 1, total, ch), F32),
        ),
        cost_estimate=pl.CostEstimate(flops=10 * s.size, bytes_accessed=10 * s.size, transcendentals=0),
        compiler_params=pltpu.CompilerParams(vmem_limit_bytes=VMEM_LIMIT),
        name="lat_solve",
    )(s, above, below, top, bottom, wide(wr), wide(wl))


def lon_kernel(x_ref, west_ref, east_ref, green_ref, out_ref):
    total, cols, ch = x_ref.shape
    pad = LANES - cols - (LEFT + RIGHT + 2)
    for e in range(total):
        parts = [x_ref[e]]
        parts += [west_ref[k, pl.ds(e, 1)] for k in range(LEFT + 1)]
        parts += [east_ref[k, pl.ds(e, 1)] for k in range(RIGHT + 1)]
        parts += [jnp.zeros((pad, ch), F32)]
        turned = jnp.concatenate(parts, axis=0).T
        value = dot(thirds(turned), green_ref[...])
        out_ref[e * ch : (e + 1) * ch] = thirds(value)


def lon_solve(x, west, east):
    total, cols, ch = x.shape
    width = cols + LEFT + RIGHT
    j = np.arange(width) - LEFT
    green = np.zeros((LANES, LANES))
    green[:cols, :width] = POLE ** np.abs(np.arange(cols)[:, None] - j[None, :])
    green[cols, :width] = POLE ** (j + LEFT + 1)
    for k in range(LEFT):
        green[cols + 1 + k, :width] = POLE ** np.abs(j - (k - LEFT))
    for k in range(RIGHT):
        green[cols + LEFT + 1 + k, :width] = POLE ** np.abs(j - (cols + k))
    green[cols + LEFT + 1 + RIGHT, :width] = POLE ** (cols + RIGHT - j)
    green = jnp.asarray((GAIN * green).astype(np.float32))
    high, low = split(green)
    return pl.pallas_call(
        lon_kernel,
        out_shape=jax.ShapeDtypeStruct((total * ch, 3 * LANES), BF),
        cost_estimate=pl.CostEstimate(
            flops=6 * total * LANES * LANES * ch, bytes_accessed=8 * x.size, transcendentals=0
        ),
        compiler_params=pltpu.CompilerParams(vmem_limit_bytes=VMEM_LIMIT),
        name="lon_solve",
    )(x, west, east, jnp.concatenate([high, high, low], axis=0))


def tap_kernel(dest_ref, base_ref, ct_ref, *refs, count, cols, cap, span):
    cells_refs, tri_ref = refs[:count], refs[count]
    out_refs = refs[count + 1 : 2 * count + 1]
    rank, place, lon_w, lat_w, near, later, packed, sems = refs[2 * count + 1 :]
    rows = rank.shape[1]
    ch = packed.shape[2]
    band = lax.axis_index("lat")
    lat_total = rows * lax.axis_size("lat")
    origin = (dest_ref[count] * cols).astype(F32)

    def window_of(i):
        return i - jnp.where(band * rows + i == lat_total - 1, 1, 0)

    glob = lax.broadcasted_iota(jnp.int32, (rows, LANES), 0) + band * rows
    first = (glob - jnp.where(glob == lat_total - 1, 1, 0) - 1).astype(F32)
    for d in range(count):
        local = cells_refs[d][0, 0] - origin
        mine = (local >= 0.0) & (local < float(cols))
        one = jnp.where(mine, 1.0, 0.0)
        rank[d] = jnp.where(mine, dot(one.astype(BF), tri_ref[...]), -1000.0)
        place[d] = local
        turn = cells_refs[d][0, 1] - first
        a = spline_weights(cells_refs[d][0, 2])
        for n, w in enumerate(spline_weights(cells_refs[d][0, 3])):
            lon_w[d, n] = w * one
        for e in range(TAPS):
            total = jnp.zeros_like(one)
            for t in range(3):
                if 0 <= e - t < 4:
                    total = jnp.where(turn == float(t), a[e - t], total)
            lat_w[d, e] = total
    for buffer in (near, later):
        for k in range(3):
            buffer[k * LANES + span : (k + 1) * LANES] = jnp.zeros((LANES - span, count * LANES), BF)
    column = lax.broadcasted_iota(jnp.int32, (span, LANES), 0).astype(F32)
    step = lax.broadcasted_iota(jnp.int32, (8, LANES), 0)

    def build(i, buffer):
        here = pl.ds(i, 1)
        for d in range(count):
            far = column - place[d, here]
            basis = jnp.where(far == 0.0, lon_w[d, 0, here], 0.0)
            for n in range(1, 4):
                basis = jnp.where(far == float(n), lon_w[d, n, here], basis)
            high, low = split(basis)
            lanes = pl.ds(d * LANES, LANES)
            buffer[0:span, lanes] = high
            buffer[LANES : LANES + span, lanes] = high
            buffer[2 * LANES : 2 * LANES + span, lanes] = low

    def emit(i, buffer):
        half = TAPS // 2
        lines = []
        for part in range(2):
            at = pl.multiple_of((window_of(i) + part * half) * ch, ch)
            lines.append(dot(ct_ref[pl.ds(at, half * ch)], buffer[...]))
        for d in range(count):
            terms = []
            for e in range(TAPS):
                block = lines[e // half][e % half * ch : (e % half + 1) * ch, d * LANES : (d + 1) * LANES]
                terms.append(block * lat_w[d, e, pl.ds(i, 1)])
            value = ((terms[0] + terms[1]) + terms[2]) + ((terms[3] + terms[4]) + terms[5])
            high, low = split(value)
            base = base_ref[dest_ref[d] * rows + i]
            odd = lax.rem(base, 8)
            spot = rank[d, pl.ds(i, 1)] + odd.astype(F32)
            pick = jnp.where(column == spot, 1.0, 0.0).astype(BF)
            got = lax.dot_general(
                jnp.concatenate([pick, pick], axis=1),
                jnp.concatenate([high, low], axis=1),
                (((1,), (1,)), ((), ())),
                preferred_element_type=F32,
            )
            at = pl.multiple_of(base - odd, 8)
            packed[d, pl.ds(at, 8)] = jnp.where(step < odd, packed[d, pl.ds(at, 8)], got[:8])
            packed[d, pl.ds(pl.multiple_of(at + 8, 8), span - 8)] = got[8:]

    build(0, near)

    @pl.loop(0, rows // 2)
    def _(pair):
        i = 2 * pair
        emit(i, near)
        build(i + 1, later)
        emit(i + 1, later)
        build(jnp.minimum(i + 2, rows - 1), near)

    copies = [
        pltpu.make_async_copy(packed.at[d, pl.ds(0, cap)], out_refs[d], sems.at[d]) for d in range(count)
    ]
    for copy in copies:
        copy.start()
    for copy in copies:
        copy.wait()


def taps(dests, sector, base, ct, cells, cols, cap):
    _, words, rows, lanes = cells.shape
    count = len(dests)
    ch = ct.shape[0] // (rows + UP + DOWN)
    span = 112
    tri = jnp.asarray(np.triu(np.ones((lanes, lanes)), 1), BF)
    weights = pltpu.VMEM((3 * LANES, count * lanes), BF)
    meta = jnp.stack([*dests, sector]).astype(jnp.int32)
    return pl.pallas_call(
        functools.partial(tap_kernel, count=count, cols=cols, cap=cap, span=span),
        out_shape=[jax.ShapeDtypeStruct((cap, ch), F32)] * count,
        grid_spec=pltpu.PrefetchScalarGridSpec(
            num_scalar_prefetch=2,
            grid=(1,),
            in_specs=[pl.BlockSpec(ct.shape, lambda g, d, b: (0, 0))]
            + [
                pl.BlockSpec((1, words, rows, lanes), functools.partial(lambda g, d, b, k: (d[k], 0, 0, 0), k=k))
                for k in range(count)
            ]
            + [pl.BlockSpec(tri.shape, lambda g, d, b: (0, 0))],
            out_specs=[pl.BlockSpec(memory_space=pl.ANY)] * count,
            scratch_shapes=[
                pltpu.VMEM((count, rows, lanes), F32),
                pltpu.VMEM((count, rows, lanes), F32),
                pltpu.VMEM((count, 4, rows, lanes), F32),
                pltpu.VMEM((count, TAPS, rows, lanes), F32),
                weights,
                weights,
                pltpu.VMEM((count, cap + span + 8, ch), F32),
                pltpu.SemaphoreType.DMA((count,)),
            ],
        ),
        cost_estimate=pl.CostEstimate(
            flops=6 * count * rows * TAPS * LANES * ch * LANES, bytes_accessed=2 * ct.size, transcendentals=0
        ),
        compiler_params=pltpu.CompilerParams(vmem_limit_bytes=VMEM_LIMIT),
        name="taps",
    )(meta, base, ct, *([cells] * count), tri)


def place_kernel(target_ref, *refs, cap):
    *parts, out_ref, gathered, sems = refs
    copies = [
        pltpu.make_async_copy(part, gathered.at[pl.ds(k * cap, cap)], sems.at[k]) for k, part in enumerate(parts)
    ]
    for copy in copies:
        copy.start()
    for copy in copies:
        copy.wait()

    @pl.loop(0, out_ref.shape[0] // 8)
    def _(group):
        at = pl.multiple_of(group * 8, 8)
        lines = [gathered[pl.ds(target_ref[at + k], 1)] for k in range(8)]
        out_ref[pl.ds(at, 8)] = jnp.concatenate(lines, axis=0)


def place(target, parts):
    cap, ch = parts[0].shape
    cells = target.shape[0]
    count = len(parts)
    return pl.pallas_call(
        functools.partial(place_kernel, cap=cap),
        out_shape=jax.ShapeDtypeStruct((cells, ch), F32),
        grid_spec=pltpu.PrefetchScalarGridSpec(
            num_scalar_prefetch=1,
            grid=(1,),
            in_specs=[pl.BlockSpec(memory_space=pl.ANY)] * count,
            out_specs=pl.BlockSpec((cells, ch), lambda g, t: (0, 0)),
            scratch_shapes=[pltpu.VMEM((count * cap, ch), F32), pltpu.SemaphoreType.DMA((count,))],
        ),
        cost_estimate=pl.CostEstimate(flops=0, bytes_accessed=8 * count * cap * ch, transcendentals=0),
        compiler_params=pltpu.CompilerParams(vmem_limit_bytes=VMEM_LIMIT),
        name="place",
    )(target, *parts)


def earlier(mask):
    rows, cols = mask.shape[1:]
    ones = mask.astype(F32)
    before = lax.dot_general(
        mask.astype(BF),
        jnp.asarray(np.triu(np.ones((cols, cols)), 1), BF),
        (((2,), (0,)), ((), ())),
        preferred_element_type=F32,
    )
    return before, bases(ones)


def bases(ones):
    rows = ones.shape[1]
    totals = jnp.sum(ones, axis=2)
    return jnp.dot(totals, jnp.asarray(np.triu(np.ones((rows, rows)), 1), F32), precision=lax.Precision.HIGHEST)


def body(tracers, owners, columns, lat_shift, fractions):
    rows, cols, ch = tracers.shape
    bands = lax.axis_size("lat")
    sectors = lax.axis_size("lon")
    me = lax.axis_index("lon")
    cells = rows * cols
    cap = 3 * cells // sectors

    owner = owners.reshape(rows, cols)
    down, up, top, bottom, words = edges(tracers, owner, columns, lat_shift, fractions)
    above = lax.ppermute(down, "lat", [(i, i + 1) for i in range(bands - 1)])
    below = lax.ppermute(up, "lat", [(i + 1, i) for i in range(bands - 1)])
    asked = lax.all_to_all(words, "lon", split_axis=0, concat_axis=0, tiled=True)

    x, right, left = lat_solve(tracers, above, below, top, bottom)
    west = lax.ppermute(right, "lon", [(i, (i + 1) % sectors) for i in range(sectors)])
    east = lax.ppermute(left, "lon", [((i + 1) % sectors, i) for i in range(sectors)])

    local = asked[:, 0] - (me * cols).astype(F32)
    base = bases(((local >= 0.0) & (local < float(cols))).astype(F32)).astype(jnp.int32).reshape(-1)
    every = jnp.arange(sectors, dtype=jnp.int32)
    mask = owner[None] == every[:, None, None]
    before, own_base = earlier(mask)
    slot = jnp.sum(jnp.where(mask, before + own_base[:, :, None], 0.0), axis=0).astype(jnp.int32)
    target = ((me - owner) % sectors * cap + slot).reshape(cells)

    ct = lon_solve(x, west, east)
    parts = [None] * sectors
    order = sorted(range(sectors), key=lambda k: (k == 0, abs(2 * k - sectors)))
    for pair in [order[n : n + 2] for n in range(0, sectors, 2)]:
        values = taps([(me + k) % sectors for k in pair], me, base, ct, asked, cols, cap)
        for k, value in zip(pair, values):
            if k:
                value = lax.ppermute(value, "lon", [(i, (i + k) % sectors) for i in range(sectors)])
            parts[k] = value
    return place(target, parts).reshape(rows, cols, ch)


def solution(mesh):
    in_specs = (
        P("lat", "lon", None),
        P("lat", "lon", None, None),
        P("lat", "lon"),
        P("lat", "lon"),
        P(None, "lat", "lon"),
    )
    out_specs = P("lat", "lon", None)
    return jax.shard_map(body, mesh=mesh, in_specs=in_specs, out_specs=out_specs, check_vma=False)
```

```python
import functools
import math

import jax
import jax.numpy as jnp
import numpy as np
from jax import lax
from jax.experimental import pallas as pl
from jax.experimental.pallas import tpu as pltpu
from jax.sharding import PartitionSpec as P


POLE = math.sqrt(3.0) - 2.0
GAIN = math.sqrt(3.0)
LANES = 128
TAPS = 6
UP, DOWN = 2, 3
LEFT, RIGHT = 1, 2
BF = jnp.bfloat16
F32 = jnp.float32
VMEM_LIMIT = 60 * 1024 * 1024


def split(x):
    high = x.astype(BF)
    return high, (x - high.astype(F32)).astype(BF)


def thirds(x):
    high, low = split(x)
    return jnp.concatenate([high, low, high], axis=1)


def dot(a, b):
    return lax.dot_general(a, b, (((1,), (0,)), ((), ())), preferred_element_type=F32)


def spline_weights(shift):
    rest = 1.0 - shift
    cube = shift * shift * shift
    return [
        rest * rest * rest / 6.0,
        (3.0 * cube - 6.0 * shift * shift + 4.0) / 6.0,
        (-3.0 * cube + 3.0 * shift * shift + 3.0 * shift + 1.0) / 6.0,
        cube / 6.0,
    ]


def edge_kernel(
    s_ref, owner_ref, column_ref, shift_ref, frac_ref, down_ref, up_ref, top_ref, bottom_ref, words_ref
):
    rows, cols = s_ref.shape[:2]
    top_row = lax.axis_index("lat") * rows
    lat_total = rows * lax.axis_size("lat")
    arrival = lax.broadcasted_iota(jnp.int32, (rows, cols), 0) + top_row
    row = jnp.clip(arrival - 1 + shift_ref[...], 1, lat_total - 3).astype(F32)
    column = (owner_ref[...] * cols + column_ref[...]).astype(F32)
    for k in range(words_ref.shape[0]):
        for w, word in enumerate((column, row, frac_ref[0], frac_ref[1])):
            words_ref[k, w] = jnp.full((rows, LANES), -1.0, F32)
            words_ref[k, w, :, :cols] = word
    first, last = s_ref[0], s_ref[rows - 1]
    far = 1.0 / (1.0 - POLE)

    acc = s_ref[0]
    for r in range(1, rows - UP):
        acc = s_ref[r] + POLE * acc
        if r == rows - 2 - DOWN:
            bottom_ref[DOWN] = 2.0 * far * last - acc
    down_ref[0] = acc
    for k in range(UP):
        down_ref[1 + k] = s_ref[rows - UP + k]
    for k in range(DOWN):
        bottom_ref[k] = 2.0 * last - s_ref[rows - 2 - k]

    acc = s_ref[rows - 1]
    for r in range(rows - 2, DOWN - 1, -1):
        acc = s_ref[r] + POLE * acc
    up_ref[DOWN] = acc
    for k in range(DOWN):
        up_ref[k] = s_ref[k]
    low = s_ref[rows - 1]
    for r in range(rows - 2, UP, -1):
        low = s_ref[r] + POLE * low
    top_ref[0] = 2.0 * far * first - low
    for k in range(UP):
        top_ref[1 + k] = 2.0 * first - s_ref[UP - k]


def edges(s, owner, columns, lat_shift, fractions):
    rows, cols, ch = s.shape
    shape = lambda n: jax.ShapeDtypeStruct((n, cols, ch), F32)
    words = jax.ShapeDtypeStruct((lax.axis_size("lon"), 4, rows, LANES), F32)
    return pl.pallas_call(
        edge_kernel,
        out_shape=(shape(UP + 1), shape(DOWN + 1), shape(UP + 1), shape(DOWN + 1), words),
        cost_estimate=pl.CostEstimate(flops=6 * s.size, bytes_accessed=6 * s.size, transcendentals=0),
        compiler_params=pltpu.CompilerParams(vmem_limit_bytes=VMEM_LIMIT),
        name="edges",
    )(s, owner, columns, lat_shift, fractions)


def lat_kernel(s_ref, above_ref, below_ref, top_ref, bottom_ref, wr_ref, wl_ref, out_ref, right_ref, left_ref):
    rows, cols, _ = s_ref.shape
    band = lax.axis_index("lat")
    at_top = band == 0
    at_bottom = band == lax.axis_size("lat") - 1
    total = rows + UP + DOWN

    def row(e):
        if e < UP:
            return jnp.where(at_top, top_ref[1 + e], above_ref[1 + e])
        if e >= UP + rows:
            return jnp.where(at_bottom, bottom_ref[e - UP - rows], below_ref[e - UP - rows])
        return s_ref[e - UP]

    acc = jnp.where(at_bottom, bottom_ref[DOWN], below_ref[DOWN])
    for e in range(total - 1, -1, -1):
        acc = POLE * acc
        out_ref[e] = acc
        acc = acc + row(e)
    acc = jnp.where(at_top, top_ref[0], above_ref[0])
    for e in range(total):
        acc = row(e) + POLE * acc
        value = GAIN * (out_ref[e] + acc)
        out_ref[e] = value
        right_ref[0, pl.ds(e, 1)] = jnp.sum(value * wr_ref[...], axis=0, keepdims=True)
        for k in range(LEFT):
            right_ref[1 + k, pl.ds(e, 1)] = value[cols - LEFT + k : cols - LEFT + k + 1]
        for k in range(RIGHT):
            left_ref[k, pl.ds(e, 1)] = value[k : k + 1]
        left_ref[RIGHT, pl.ds(e, 1)] = jnp.sum(value * wl_ref[...], axis=0, keepdims=True)


def lat_solve(s, above, below, top, bottom):
    rows, cols, ch = s.shape
    total = rows + UP + DOWN
    place = np.arange(cols)
    wr = np.where(place < cols - LEFT, POLE ** np.maximum(cols - LEFT - 1 - place, 0), 0.0)
    wl = np.where(place >= RIGHT, POLE ** np.maximum(place - RIGHT, 0), 0.0)
    wide = lambda w: jnp.asarray(np.broadcast_to(w[:, None], (cols, ch)).astype(np.float32))
    return pl.pallas_call(
        lat_kernel,
        out_shape=(
            jax.ShapeDtypeStruct((total, cols, ch), F32),
            jax.ShapeDtypeStruct((LEFT + 1, total, ch), F32),
            jax.ShapeDtypeStruct((RIGHT + 1, total, ch), F32),
        ),
        cost_estimate=pl.CostEstimate(flops=10 * s.size, bytes_accessed=10 * s.size, transcendentals=0),
        compiler_params=pltpu.CompilerParams(vmem_limit_bytes=VMEM_LIMIT),
        name="lat_solve",
    )(s, above, below, top, bottom, wide(wr), wide(wl))


def lon_kernel(x_ref, west_ref, east_ref, green_ref, out_ref):
    total, cols, ch = x_ref.shape
    pad = LANES - cols - (LEFT + RIGHT + 2)
    for e in range(total):
        parts = [x_ref[e]]
        parts += [west_ref[k, pl.ds(e, 1)] for k in range(LEFT + 1)]
        parts += [east_ref[k, pl.ds(e, 1)] for k in range(RIGHT + 1)]
        parts += [jnp.zeros((pad, ch), F32)]
        turned = jnp.concatenate(parts, axis=0).T
        value = dot(thirds(turned), green_ref[...])
        out_ref[e * ch : (e + 1) * ch] = thirds(value)


def lon_solve(x, west, east):
    total, cols, ch = x.shape
    width = cols + LEFT + RIGHT
    j = np.arange(width) - LEFT
    green = np.zeros((LANES, LANES))
    green[:cols, :width] = POLE ** np.abs(np.arange(cols)[:, None] - j[None, :])
    green[cols, :width] = POLE ** (j + LEFT + 1)
    for k in range(LEFT):
        green[cols + 1 + k, :width] = POLE ** np.abs(j - (k - LEFT))
    for k in range(RIGHT):
        green[cols + LEFT + 1 + k, :width] = POLE ** np.abs(j - (cols + k))
    green[cols + LEFT + 1 + RIGHT, :width] = POLE ** (cols + RIGHT - j)
    green = jnp.asarray((GAIN * green).astype(np.float32))
    high, low = split(green)
    return pl.pallas_call(
        lon_kernel,
        out_shape=jax.ShapeDtypeStruct((total * ch, 3 * LANES), BF),
        cost_estimate=pl.CostEstimate(
            flops=6 * total * LANES * LANES * ch, bytes_accessed=8 * x.size, transcendentals=0
        ),
        compiler_params=pltpu.CompilerParams(vmem_limit_bytes=VMEM_LIMIT),
        name="lon_solve",
    )(x, west, east, jnp.concatenate([high, high, low], axis=0))


def tap_kernel(meta_ref, base_ref, *refs, tables, count, cols, cap, span, at):
    meta = lambda k: meta_ref[at + k]
    table_refs, refs = refs[:tables], refs[tables:]
    cells_refs, tri_ref = refs[:count], refs[count]
    out_refs = refs[count + 1 : 2 * count + 1]
    rank, place, lon_w, lat_w, near, later, packed, ct_ref, sems, table_sem = refs[2 * count + 1 :]
    for n, table_ref in enumerate(table_refs):

        @pl.when(meta(count + 1) == n)
        def _(table_ref=table_ref):
            pltpu.make_async_copy(table_ref, ct_ref, table_sem).start()

    rows = rank.shape[1]
    ch = packed.shape[2]
    band = lax.axis_index("lat")
    lat_total = rows * lax.axis_size("lat")
    origin = (meta(count) * cols).astype(F32)

    def window_of(i):
        return i - jnp.where(band * rows + i == lat_total - 1, 1, 0)

    glob = lax.broadcasted_iota(jnp.int32, (rows, LANES), 0) + band * rows
    first = (glob - jnp.where(glob == lat_total - 1, 1, 0) - 1).astype(F32)
    for d in range(count):
        local = cells_refs[d][0, 0] - origin
        mine = (local >= 0.0) & (local < float(cols))
        one = jnp.where(mine, 1.0, 0.0)
        rank[d] = jnp.where(mine, dot(one.astype(BF), tri_ref[...]), -1000.0)
        place[d] = local
        turn = cells_refs[d][0, 1] - first
        a = spline_weights(cells_refs[d][0, 2])
        for n, w in enumerate(spline_weights(cells_refs[d][0, 3])):
            lon_w[d, n] = w * one
        for e in range(TAPS):
            total = jnp.zeros_like(one)
            for t in range(3):
                if 0 <= e - t < 4:
                    total = jnp.where(turn == float(t), a[e - t], total)
            lat_w[d, e] = total
    for buffer in (near, later):
        for k in range(3):
            buffer[k * LANES + span : (k + 1) * LANES] = jnp.zeros((LANES - span, count * LANES), BF)
    column = lax.broadcasted_iota(jnp.int32, (span, LANES), 0).astype(F32)
    step = lax.broadcasted_iota(jnp.int32, (8, LANES), 0)

    def build(i, buffer):
        here = pl.ds(i, 1)
        for d in range(count):
            far = column - place[d, here]
            basis = jnp.where(far == 0.0, lon_w[d, 0, here], 0.0)
            for n in range(1, 4):
                basis = jnp.where(far == float(n), lon_w[d, n, here], basis)
            high, low = split(basis)
            lanes = pl.ds(d * LANES, LANES)
            buffer[0:span, lanes] = high
            buffer[LANES : LANES + span, lanes] = high
            buffer[2 * LANES : 2 * LANES + span, lanes] = low

    def emit(i, buffer):
        half = TAPS // 2
        lines = []
        for part in range(2):
            at = pl.multiple_of((window_of(i) + part * half) * ch, ch)
            lines.append(dot(ct_ref[pl.ds(at, half * ch)], buffer[...]))
        for d in range(count):
            terms = []
            for e in range(TAPS):
                block = lines[e // half][e % half * ch : (e % half + 1) * ch, d * LANES : (d + 1) * LANES]
                terms.append(block * lat_w[d, e, pl.ds(i, 1)])
            value = ((terms[0] + terms[1]) + terms[2]) + ((terms[3] + terms[4]) + terms[5])
            high, low = split(value)
            base = base_ref[meta(count + 2 + d) + i]
            odd = lax.rem(base, 8)
            spot = rank[d, pl.ds(i, 1)] + odd.astype(F32)
            pick = jnp.where(column == spot, 1.0, 0.0).astype(BF)
            got = lax.dot_general(
                jnp.concatenate([pick, pick], axis=1),
                jnp.concatenate([high, low], axis=1),
                (((1,), (1,)), ((), ())),
                preferred_element_type=F32,
            )
            at = pl.multiple_of(base - odd, 8)
            packed[d, pl.ds(at, 8)] = jnp.where(step < odd, packed[d, pl.ds(at, 8)], got[:8])
            packed[d, pl.ds(pl.multiple_of(at + 8, 8), span - 8)] = got[8:]

    build(0, near)
    pltpu.make_async_copy(table_refs[0], ct_ref, table_sem).wait()

    @pl.loop(0, rows // 2)
    def _(pair):
        i = 2 * pair
        emit(i, near)
        build(i + 1, later)
        emit(i + 1, later)
        build(jnp.minimum(i + 2, rows - 1), near)

    copies = [
        pltpu.make_async_copy(packed.at[d, pl.ds(0, cap)], out_refs[d], sems.at[d]) for d in range(count)
    ]
    for copy in copies:
        copy.start()
    for copy in copies:
        copy.wait()


def taps(meta, at, count, base, tables, cells, cols, cap):
    _, words, rows, lanes = cells.shape
    ch = tables[0].shape[0] // (rows + UP + DOWN)
    span = 112
    tri = jnp.asarray(np.triu(np.ones((lanes, lanes)), 1), BF)
    weights = pltpu.VMEM((3 * LANES, count * lanes), BF)
    return pl.pallas_call(
        functools.partial(tap_kernel, tables=len(tables), count=count, cols=cols, cap=cap, span=span, at=at),
        out_shape=[jax.ShapeDtypeStruct((cap, ch), F32)] * count,
        grid_spec=pltpu.PrefetchScalarGridSpec(
            num_scalar_prefetch=2,
            grid=(1,),
            in_specs=[pl.BlockSpec(memory_space=pl.ANY)] * len(tables)
            + [
                pl.BlockSpec((1, words, rows, lanes), functools.partial(lambda g, m, b, k: (m[k], 0, 0, 0), k=at + k))
                for k in range(count)
            ]
            + [pl.BlockSpec(tri.shape, lambda g, m, b: (0, 0))],
            out_specs=[pl.BlockSpec(memory_space=pl.ANY)] * count,
            scratch_shapes=[
                pltpu.VMEM((count, rows, lanes), F32),
                pltpu.VMEM((count, rows, lanes), F32),
                pltpu.VMEM((count, 4, rows, lanes), F32),
                pltpu.VMEM((count, TAPS, rows, lanes), F32),
                weights,
                weights,
                pltpu.VMEM((count, cap + span + 8, ch), F32),
                pltpu.VMEM(tables[0].shape, BF),
                pltpu.SemaphoreType.DMA((count,)),
                pltpu.SemaphoreType.DMA,
            ],
        ),
        cost_estimate=pl.CostEstimate(
            flops=6 * count * rows * TAPS * LANES * ch * LANES, bytes_accessed=2 * tables[0].size, transcendentals=0
        ),
        compiler_params=pltpu.CompilerParams(vmem_limit_bytes=VMEM_LIMIT),
        name="taps",
    )(meta, base, *tables, *([cells] * count), tri)


def place_kernel(target_ref, *refs, cap):
    *parts, out_ref, gathered, sems = refs
    copies = [
        pltpu.make_async_copy(part, gathered.at[pl.ds(k * cap, cap)], sems.at[k]) for k, part in enumerate(parts)
    ]
    for copy in copies:
        copy.start()
    for copy in copies:
        copy.wait()

    @pl.loop(0, out_ref.shape[0] // 8)
    def _(group):
        at = pl.multiple_of(group * 8, 8)
        lines = [gathered[pl.ds(target_ref[at + k], 1)] for k in range(8)]
        out_ref[pl.ds(at, 8)] = jnp.concatenate(lines, axis=0)


def place(target, parts):
    cap, ch = parts[0].shape
    cells = target.shape[0]
    count = len(parts)
    return pl.pallas_call(
        functools.partial(place_kernel, cap=cap),
        out_shape=jax.ShapeDtypeStruct((cells, ch), F32),
        grid_spec=pltpu.PrefetchScalarGridSpec(
            num_scalar_prefetch=1,
            grid=(1,),
            in_specs=[pl.BlockSpec(memory_space=pl.ANY)] * count,
            out_specs=pl.BlockSpec((cells, ch), lambda g, t: (0, 0)),
            scratch_shapes=[pltpu.VMEM((count * cap, ch), F32), pltpu.SemaphoreType.DMA((count,))],
        ),
        cost_estimate=pl.CostEstimate(flops=0, bytes_accessed=8 * count * cap * ch, transcendentals=0),
        compiler_params=pltpu.CompilerParams(vmem_limit_bytes=VMEM_LIMIT),
        name="place",
    )(target, *parts)


def earlier(mask):
    _, cols = mask.shape[1:]
    ones = mask.astype(F32)
    before = lax.dot_general(
        mask.astype(BF),
        jnp.asarray(np.triu(np.ones((cols, cols)), 1), BF),
        (((2,), (0,)), ((), ())),
        preferred_element_type=F32,
    )
    return before, bases(ones)


def bases(ones):
    rows = ones.shape[1]
    totals = jnp.sum(ones, axis=2)
    return jnp.dot(totals, jnp.asarray(np.triu(np.ones((rows, rows)), 1), F32), precision=lax.Precision.HIGHEST)


def transport(tracers, owners, columns, lat_shift, fractions):
    rows, cols, ch = tracers.shape
    bands = lax.axis_size("lat")
    sectors = lax.axis_size("lon")
    band = lax.axis_index("lat")
    me = lax.axis_index("lon")
    cells = rows * cols
    cap = 3 * cells // sectors
    quarter = sectors // 4
    at = lambda q, o: q * quarter + o
    mirror = [(at(q, o), at((0, 2, 1, 3)[q], o)) for q in (1, 2) for o in range(quarter)]
    mine, offset = me // quarter, me % quarter
    middle = (mine == 1) | (mine == 2)

    mirrored = lax.ppermute(tracers, "lon", mirror)
    owner = owners.reshape(rows, cols)
    down, up, top, bottom, words = edges(tracers, owner, columns, lat_shift, fractions)
    above = lax.ppermute(down, "lat", [(i, i + 1) for i in range(bands - 1)])
    below = lax.ppermute(up, "lat", [(i + 1, i) for i in range(bands - 1)])
    asked = lax.all_to_all(words, "lon", split_axis=0, concat_axis=0, tiled=True)

    x, right, left = lat_solve(tracers, above, below, top, bottom)
    west = lax.ppermute(right, "lon", [(i, (i + 1) % sectors) for i in range(sectors)])
    east = lax.ppermute(left, "lon", [((i + 1) % sectors, i) for i in range(sectors)])
    above, below, right = lax.optimization_barrier((above, below, right))
    rim = jnp.concatenate(
        [jnp.where(band == 0, top, above), jnp.where(band == bands - 1, bottom, below)], axis=0
    )
    rim = lax.ppermute(rim, "lon", mirror)
    sides = lax.ppermute(jnp.concatenate([west, east], axis=0), "lon", mirror)

    origins = np.array([[s * cols, dict(mirror).get(s, s) * cols] for s in range(sectors)], np.float32)
    local = asked[None, :, 0] - jnp.asarray(origins)[me][:, None, None, None]
    inside = ((local >= 0.0) & (local < float(cols))).astype(F32).reshape(2 * sectors, rows, -1)
    base = bases(inside).astype(jnp.int32).reshape(-1)

    own = lon_solve(x, west, east)
    late_owner, x = lax.optimization_barrier((owner, x))
    every = jnp.arange(sectors, dtype=jnp.int32)
    mask = late_owner[None] == every[:, None, None]
    before, own_base = earlier(mask)
    slot = jnp.sum(jnp.where(mask, before + own_base[:, :, None], 0.0), axis=0).astype(jnp.int32)
    q = late_owner // quarter
    alike = ((q == 1) | (q == 2)) == middle
    early = ((q == 1) | (q == 2)) == (q // 2 == mine // 2)
    part = jnp.where(early, jnp.where(alike, 1, 0), jnp.where(alike, 3, 2)) * quarter
    target = ((part + (offset - late_owner) % quarter) * cap + slot).reshape(cells)

    goals = ((2, 0, 3, 1), (3, 1, 2, 0), (1, 0, 3, 2), (0, 1, 2, 3))
    shifts = list(range(quarter))[::-1]
    calls = [(group, shifts[n : n + 2]) for group in range(4) for n in range(0, quarter, 2)]
    plan = []
    for s in range(sectors):
        k, o = s // quarter, s % quarter
        row = []
        for group, pair in calls:
            which = int(group >= 2 and k in (1, 2))
            dests = [at(goals[group][k], (o + a) % quarter) for a in pair]
            row += dests + [dict(mirror).get(s, s) if which else s, which]
            row += [(which * sectors + dest) * rows for dest in dests]
        plan.append(row)
    meta = jnp.asarray(np.array(plan, np.int32))[me]

    parts = [None] * sectors
    tables, done = [own], 0
    for group, pair in calls:
        if group == 2 and len(tables) == 1:
            other, _, _ = lat_solve(mirrored, rim[: UP + 1], rim[UP + 1 :], rim[: UP + 1], rim[UP + 1 :])
            tables = [own, lon_solve(other, sides[: LEFT + 1], sides[LEFT + 1 :])]
        values = taps(meta, done, len(pair), base, tables, asked, cols, cap)
        done += 2 * len(pair) + 2
        for a, value in zip(pair, values):
            moves = [(at(k, o), at(goals[group][k], (o + a) % quarter)) for k in range(4) for o in range(quarter)]
            if any(i != j for i, j in moves):
                value = lax.ppermute(value, "lon", moves)
            parts[group * quarter + a] = value
    return place(target, parts).reshape(rows, cols, ch)


def solution(mesh):
    in_specs = (
        P("lat", "lon", None),
        P("lat", "lon", None, None),
        P("lat", "lon"),
        P("lat", "lon"),
        P(None, "lat", "lon"),
    )
    out_specs = P("lat", "lon", None)
    return jax.shard_map(transport, mesh=mesh, in_specs=in_specs, out_specs=out_specs, check_vma=False)
```

```python
import functools
import math

import jax
import jax.numpy as jnp
import numpy as np
from jax import lax
from jax.experimental import pallas as pl
from jax.experimental.pallas import tpu as pltpu
from jax.sharding import PartitionSpec as P


POLE = math.sqrt(3.0) - 2.0
GAIN = math.sqrt(3.0)
LANES = 128
TAPS = 6
UP, DOWN = 2, 3
LEFT, RIGHT = 1, 2
BF = jnp.bfloat16
F32 = jnp.float32
VMEM_LIMIT = 60 * 1024 * 1024


def split(x):
    high = x.astype(BF)
    return high, (x - high.astype(F32)).astype(BF)


def thirds(x):
    high, low = split(x)
    return jnp.concatenate([high, low, high], axis=1)


def dot(a, b):
    return lax.dot_general(a, b, (((1,), (0,)), ((), ())), preferred_element_type=F32)


def spline_weights(shift):
    rest = 1.0 - shift
    cube = shift * shift * shift
    return [
        rest * rest * rest / 6.0,
        (3.0 * cube - 6.0 * shift * shift + 4.0) / 6.0,
        (-3.0 * cube + 3.0 * shift * shift + 3.0 * shift + 1.0) / 6.0,
        cube / 6.0,
    ]


def edge_kernel(
    s_ref, owner_ref, column_ref, shift_ref, frac_ref, down_ref, up_ref, top_ref, bottom_ref, words_ref
):
    rows, cols = s_ref.shape[:2]
    top_row = lax.axis_index("lat") * rows
    lat_total = rows * lax.axis_size("lat")
    arrival = lax.broadcasted_iota(jnp.int32, (rows, cols), 0) + top_row
    row = jnp.clip(arrival - 1 + shift_ref[...], 1, lat_total - 3).astype(F32)
    column = (owner_ref[...] * cols + column_ref[...]).astype(F32)
    for k in range(words_ref.shape[0]):
        for w, word in enumerate((column, row, frac_ref[0], frac_ref[1])):
            words_ref[k, w] = jnp.full((rows, LANES), -1.0, F32)
            words_ref[k, w, :, :cols] = word
    first, last = s_ref[0], s_ref[rows - 1]
    far = 1.0 / (1.0 - POLE)

    acc = s_ref[0]
    for r in range(1, rows - UP):
        acc = s_ref[r] + POLE * acc
        if r == rows - 2 - DOWN:
            bottom_ref[DOWN] = 2.0 * far * last - acc
    down_ref[0] = acc
    for k in range(UP):
        down_ref[1 + k] = s_ref[rows - UP + k]
    for k in range(DOWN):
        bottom_ref[k] = 2.0 * last - s_ref[rows - 2 - k]

    acc = s_ref[rows - 1]
    for r in range(rows - 2, DOWN - 1, -1):
        acc = s_ref[r] + POLE * acc
    up_ref[DOWN] = acc
    for k in range(DOWN):
        up_ref[k] = s_ref[k]
    low = s_ref[rows - 1]
    for r in range(rows - 2, UP, -1):
        low = s_ref[r] + POLE * low
    top_ref[0] = 2.0 * far * first - low
    for k in range(UP):
        top_ref[1 + k] = 2.0 * first - s_ref[UP - k]


def edges(s, owner, columns, lat_shift, fractions):
    rows, cols, ch = s.shape
    shape = lambda n: jax.ShapeDtypeStruct((n, cols, ch), F32)
    words = jax.ShapeDtypeStruct((lax.axis_size("lon"), 4, rows, LANES), F32)
    return pl.pallas_call(
        edge_kernel,
        out_shape=(shape(UP + 1), shape(DOWN + 1), shape(UP + 1), shape(DOWN + 1), words),
        cost_estimate=pl.CostEstimate(flops=6 * s.size, bytes_accessed=6 * s.size, transcendentals=0),
        compiler_params=pltpu.CompilerParams(vmem_limit_bytes=VMEM_LIMIT),
        name="edges",
    )(s, owner, columns, lat_shift, fractions)


def lat_kernel(*refs, pieces):
    s_refs, refs = refs[:pieces], refs[pieces:]
    above_ref, below_ref, top_ref, bottom_ref, wr_ref, wl_ref, out_ref, right_ref, left_ref = refs
    depth, cols, _ = s_refs[0].shape
    rows = depth * pieces
    band = lax.axis_index("lat")
    at_top = band == 0
    at_bottom = band == lax.axis_size("lat") - 1
    total = rows + UP + DOWN

    def row(e):
        if e < UP:
            return jnp.where(at_top, top_ref[1 + e], above_ref[1 + e])
        if e >= UP + rows:
            return jnp.where(at_bottom, bottom_ref[e - UP - rows], below_ref[e - UP - rows])
        return s_refs[(e - UP) // depth][(e - UP) % depth]

    acc = jnp.where(at_bottom, bottom_ref[DOWN], below_ref[DOWN])
    for e in range(total - 1, -1, -1):
        acc = POLE * acc
        out_ref[e] = acc
        acc = acc + row(e)
    acc = jnp.where(at_top, top_ref[0], above_ref[0])
    for e in range(total):
        acc = row(e) + POLE * acc
        value = GAIN * (out_ref[e] + acc)
        out_ref[e] = value
        right_ref[0, pl.ds(e, 1)] = jnp.sum(value * wr_ref[...], axis=0, keepdims=True)
        for k in range(LEFT):
            right_ref[1 + k, pl.ds(e, 1)] = value[cols - LEFT + k : cols - LEFT + k + 1]
        for k in range(RIGHT):
            left_ref[k, pl.ds(e, 1)] = value[k : k + 1]
        left_ref[RIGHT, pl.ds(e, 1)] = jnp.sum(value * wl_ref[...], axis=0, keepdims=True)


def lat_solve(pieces, above, below, top, bottom):
    depth, cols, ch = pieces[0].shape
    rows = depth * len(pieces)
    total = rows + UP + DOWN
    place = np.arange(cols)
    wr = np.where(place < cols - LEFT, POLE ** np.maximum(cols - LEFT - 1 - place, 0), 0.0)
    wl = np.where(place >= RIGHT, POLE ** np.maximum(place - RIGHT, 0), 0.0)
    wide = lambda w: jnp.asarray(np.broadcast_to(w[:, None], (cols, ch)).astype(np.float32))
    size = rows * cols * ch
    return pl.pallas_call(
        functools.partial(lat_kernel, pieces=len(pieces)),
        out_shape=(
            jax.ShapeDtypeStruct((total, cols, ch), F32),
            jax.ShapeDtypeStruct((LEFT + 1, total, ch), F32),
            jax.ShapeDtypeStruct((RIGHT + 1, total, ch), F32),
        ),
        cost_estimate=pl.CostEstimate(flops=10 * size, bytes_accessed=10 * size, transcendentals=0),
        compiler_params=pltpu.CompilerParams(vmem_limit_bytes=VMEM_LIMIT),
        name="lat_solve",
    )(*pieces, above, below, top, bottom, wide(wr), wide(wl))


def lon_kernel(x_ref, west_ref, east_ref, green_ref, out_ref):
    total, cols, ch = x_ref.shape
    pad = LANES - cols - (LEFT + RIGHT + 2)
    for e in range(total):
        parts = [x_ref[e]]
        parts += [west_ref[k, pl.ds(e, 1)] for k in range(LEFT + 1)]
        parts += [east_ref[k, pl.ds(e, 1)] for k in range(RIGHT + 1)]
        parts += [jnp.zeros((pad, ch), F32)]
        turned = jnp.concatenate(parts, axis=0).T
        value = dot(thirds(turned), green_ref[...])
        out_ref[e * ch : (e + 1) * ch] = thirds(value)


def lon_solve(x, west, east):
    total, cols, ch = x.shape
    width = cols + LEFT + RIGHT
    j = np.arange(width) - LEFT
    green = np.zeros((LANES, LANES))
    green[:cols, :width] = POLE ** np.abs(np.arange(cols)[:, None] - j[None, :])
    green[cols, :width] = POLE ** (j + LEFT + 1)
    for k in range(LEFT):
        green[cols + 1 + k, :width] = POLE ** np.abs(j - (k - LEFT))
    for k in range(RIGHT):
        green[cols + LEFT + 1 + k, :width] = POLE ** np.abs(j - (cols + k))
    green[cols + LEFT + 1 + RIGHT, :width] = POLE ** (cols + RIGHT - j)
    green = jnp.asarray((GAIN * green).astype(np.float32))
    high, low = split(green)
    return pl.pallas_call(
        lon_kernel,
        out_shape=jax.ShapeDtypeStruct((total * ch, 3 * LANES), BF),
        cost_estimate=pl.CostEstimate(
            flops=6 * total * LANES * LANES * ch, bytes_accessed=8 * x.size, transcendentals=0
        ),
        compiler_params=pltpu.CompilerParams(vmem_limit_bytes=VMEM_LIMIT),
        name="lon_solve",
    )(x, west, east, jnp.concatenate([high, high, low], axis=0))


def tap_kernel(meta_ref, base_ref, *refs, tables, count, cols, cap, span, at):
    meta = lambda k: meta_ref[at + k]
    table_refs, refs = refs[:tables], refs[tables:]
    cells_refs, tri_ref = refs[:count], refs[count]
    out_refs = refs[count + 1 : 2 * count + 1]
    rank, place, lon_w, lat_w, near, later, packed, ct_ref, sems, table_sem = refs[2 * count + 1 :]
    for n, table_ref in enumerate(table_refs):

        @pl.when(meta(count + 1) == n)
        def _(table_ref=table_ref):
            pltpu.make_async_copy(table_ref, ct_ref, table_sem).start()

    rows = rank.shape[1]
    ch = packed.shape[2]
    band = lax.axis_index("lat")
    lat_total = rows * lax.axis_size("lat")
    origin = (meta(count) * cols).astype(F32)

    def window_of(i):
        return i - jnp.where(band * rows + i == lat_total - 1, 1, 0)

    glob = lax.broadcasted_iota(jnp.int32, (rows, LANES), 0) + band * rows
    first = (glob - jnp.where(glob == lat_total - 1, 1, 0) - 1).astype(F32)
    for d in range(count):
        local = cells_refs[d][0, 0] - origin
        mine = (local >= 0.0) & (local < float(cols))
        one = jnp.where(mine, 1.0, 0.0)
        rank[d] = jnp.where(mine, dot(one.astype(BF), tri_ref[...]), -1000.0)
        place[d] = local
        turn = cells_refs[d][0, 1] - first
        a = spline_weights(cells_refs[d][0, 2])
        for n, w in enumerate(spline_weights(cells_refs[d][0, 3])):
            lon_w[d, n] = w * one
        for e in range(TAPS):
            total = jnp.zeros_like(one)
            for t in range(3):
                if 0 <= e - t < 4:
                    total = jnp.where(turn == float(t), a[e - t], total)
            lat_w[d, e] = total
    for buffer in (near, later):
        for k in range(3):
            buffer[k * LANES + span : (k + 1) * LANES] = jnp.zeros((LANES - span, count * LANES), BF)
    column = lax.broadcasted_iota(jnp.int32, (span, LANES), 0).astype(F32)
    step = lax.broadcasted_iota(jnp.int32, (8, LANES), 0)

    def build(i, buffer):
        here = pl.ds(i, 1)
        for d in range(count):
            far = column - place[d, here]
            basis = jnp.where(far == 0.0, lon_w[d, 0, here], 0.0)
            for n in range(1, 4):
                basis = jnp.where(far == float(n), lon_w[d, n, here], basis)
            high, low = split(basis)
            lanes = pl.ds(d * LANES, LANES)
            buffer[0:span, lanes] = high
            buffer[LANES : LANES + span, lanes] = high
            buffer[2 * LANES : 2 * LANES + span, lanes] = low

    def emit(i, buffer):
        half = TAPS // 2
        lines = []
        for part in range(2):
            at = pl.multiple_of((window_of(i) + part * half) * ch, ch)
            lines.append(dot(ct_ref[pl.ds(at, half * ch)], buffer[...]))
        for d in range(count):
            terms = []
            for e in range(TAPS):
                block = lines[e // half][e % half * ch : (e % half + 1) * ch, d * LANES : (d + 1) * LANES]
                terms.append(block * lat_w[d, e, pl.ds(i, 1)])
            value = ((terms[0] + terms[1]) + terms[2]) + ((terms[3] + terms[4]) + terms[5])
            high, low = split(value)
            base = base_ref[meta(count + 2 + d) + i]
            odd = lax.rem(base, 8)
            spot = rank[d, pl.ds(i, 1)] + odd.astype(F32)
            pick = jnp.where(column == spot, 1.0, 0.0).astype(BF)
            got = lax.dot_general(
                jnp.concatenate([pick, pick], axis=1),
                jnp.concatenate([high, low], axis=1),
                (((1,), (1,)), ((), ())),
                preferred_element_type=F32,
            )
            at = pl.multiple_of(base - odd, 8)
            packed[d, pl.ds(at, 8)] = jnp.where(step < odd, packed[d, pl.ds(at, 8)], got[:8])
            packed[d, pl.ds(pl.multiple_of(at + 8, 8), span - 8)] = got[8:]

    build(0, near)
    pltpu.make_async_copy(table_refs[0], ct_ref, table_sem).wait()

    @pl.loop(0, rows // 2)
    def _(pair):
        i = 2 * pair
        emit(i, near)
        build(i + 1, later)
        emit(i + 1, later)
        build(jnp.minimum(i + 2, rows - 1), near)

    copies = [
        pltpu.make_async_copy(packed.at[d, pl.ds(0, cap)], out_refs[d], sems.at[d]) for d in range(count)
    ]
    for copy in copies:
        copy.start()
    for copy in copies:
        copy.wait()


def taps(meta, at, count, base, tables, cells, cols, cap):
    _, words, rows, lanes = cells.shape
    ch = tables[0].shape[0] // (rows + UP + DOWN)
    span = 112
    tri = jnp.asarray(np.triu(np.ones((lanes, lanes)), 1), BF)
    weights = pltpu.VMEM((3 * LANES, count * lanes), BF)
    return pl.pallas_call(
        functools.partial(tap_kernel, tables=len(tables), count=count, cols=cols, cap=cap, span=span, at=at),
        out_shape=[jax.ShapeDtypeStruct((cap, ch), F32)] * count,
        grid_spec=pltpu.PrefetchScalarGridSpec(
            num_scalar_prefetch=2,
            grid=(1,),
            in_specs=[pl.BlockSpec(memory_space=pl.ANY)] * len(tables)
            + [
                pl.BlockSpec((1, words, rows, lanes), functools.partial(lambda g, m, b, k: (m[k], 0, 0, 0), k=at + k))
                for k in range(count)
            ]
            + [pl.BlockSpec(tri.shape, lambda g, m, b: (0, 0))],
            out_specs=[pl.BlockSpec(memory_space=pl.ANY)] * count,
            scratch_shapes=[
                pltpu.VMEM((count, rows, lanes), F32),
                pltpu.VMEM((count, rows, lanes), F32),
                pltpu.VMEM((count, 4, rows, lanes), F32),
                pltpu.VMEM((count, TAPS, rows, lanes), F32),
                weights,
                weights,
                pltpu.VMEM((count, cap + span + 8, ch), F32),
                pltpu.VMEM(tables[0].shape, BF),
                pltpu.SemaphoreType.DMA((count,)),
                pltpu.SemaphoreType.DMA,
            ],
        ),
        cost_estimate=pl.CostEstimate(
            flops=6 * count * rows * TAPS * LANES * ch * LANES, bytes_accessed=2 * tables[0].size, transcendentals=0
        ),
        compiler_params=pltpu.CompilerParams(vmem_limit_bytes=VMEM_LIMIT),
        name="taps",
    )(meta, base, *tables, *([cells] * count), tri)


def place_kernel(target_ref, *refs, cap):
    *parts, out_ref, gathered, sems = refs
    copies = [
        pltpu.make_async_copy(part, gathered.at[pl.ds(k * cap, cap)], sems.at[k]) for k, part in enumerate(parts)
    ]
    for copy in copies:
        copy.start()
    for copy in copies:
        copy.wait()

    @pl.loop(0, out_ref.shape[0] // 8)
    def _(group):
        at = pl.multiple_of(group * 8, 8)
        lines = [gathered[pl.ds(target_ref[at + k], 1)] for k in range(8)]
        out_ref[pl.ds(at, 8)] = jnp.concatenate(lines, axis=0)


def place(target, parts):
    cap, ch = parts[0].shape
    cells = target.shape[0]
    count = len(parts)
    return pl.pallas_call(
        functools.partial(place_kernel, cap=cap),
        out_shape=jax.ShapeDtypeStruct((cells, ch), F32),
        grid_spec=pltpu.PrefetchScalarGridSpec(
            num_scalar_prefetch=1,
            grid=(1,),
            in_specs=[pl.BlockSpec(memory_space=pl.ANY)] * count,
            out_specs=pl.BlockSpec((cells, ch), lambda g, t: (0, 0)),
            scratch_shapes=[pltpu.VMEM((count * cap, ch), F32), pltpu.SemaphoreType.DMA((count,))],
        ),
        cost_estimate=pl.CostEstimate(flops=0, bytes_accessed=8 * count * cap * ch, transcendentals=0),
        compiler_params=pltpu.CompilerParams(vmem_limit_bytes=VMEM_LIMIT),
        name="place",
    )(target, *parts)


def earlier(mask):
    _, cols = mask.shape[1:]
    ones = mask.astype(F32)
    before = lax.dot_general(
        mask.astype(BF),
        jnp.asarray(np.triu(np.ones((cols, cols)), 1), BF),
        (((2,), (0,)), ((), ())),
        preferred_element_type=F32,
    )
    return before, bases(ones)


def bases(ones):
    rows = ones.shape[1]
    totals = jnp.sum(ones, axis=2)
    return jnp.dot(totals, jnp.asarray(np.triu(np.ones((rows, rows)), 1), F32), precision=lax.Precision.HIGHEST)


def transport(tracers, owners, columns, lat_shift, fractions):
    rows, cols, ch = tracers.shape
    bands = lax.axis_size("lat")
    sectors = lax.axis_size("lon")
    band = lax.axis_index("lat")
    me = lax.axis_index("lon")
    cells = rows * cols
    cap = 3 * cells // sectors
    quarter = sectors // 4
    at = lambda q, o: q * quarter + o
    mirror = [(at(q, o), at((0, 2, 1, 3)[q], o)) for q in (1, 2) for o in range(quarter)]
    mine, offset = me // quarter, me % quarter
    middle = (mine == 1) | (mine == 2)

    upper = lax.ppermute(tracers[: rows // 2], "lon", mirror)
    lower = lax.ppermute(tracers[rows // 2 :], "lon", mirror)
    owner = owners.reshape(rows, cols)
    down, up, top, bottom, words = edges(tracers, owner, columns, lat_shift, fractions)
    above = lax.ppermute(down, "lat", [(i, i + 1) for i in range(bands - 1)])
    below = lax.ppermute(up, "lat", [(i + 1, i) for i in range(bands - 1)])
    asked = lax.all_to_all(words, "lon", split_axis=0, concat_axis=0, tiled=True)

    x, right, left = lat_solve([tracers], above, below, top, bottom)
    west = lax.ppermute(right, "lon", [(i, (i + 1) % sectors) for i in range(sectors)])
    east = lax.ppermute(left, "lon", [((i + 1) % sectors, i) for i in range(sectors)])
    above, below, right = lax.optimization_barrier((above, below, right))
    rim = jnp.concatenate(
        [jnp.where(band == 0, top, above), jnp.where(band == bands - 1, bottom, below)], axis=0
    )
    rim = lax.ppermute(rim, "lon", mirror)
    sides = lax.ppermute(jnp.concatenate([west, east], axis=0), "lon", mirror)

    origins = np.array([[s * cols, dict(mirror).get(s, s) * cols] for s in range(sectors)], np.float32)
    local = asked[None, :, 0] - jnp.asarray(origins)[me][:, None, None, None]
    inside = ((local >= 0.0) & (local < float(cols))).astype(F32).reshape(2 * sectors, rows, -1)
    base = bases(inside).astype(jnp.int32).reshape(-1)

    own = lon_solve(x, west, east)
    late_owner, x = lax.optimization_barrier((owner, x))
    every = jnp.arange(sectors, dtype=jnp.int32)
    mask = late_owner[None] == every[:, None, None]
    before, own_base = earlier(mask)
    slot = jnp.sum(jnp.where(mask, before + own_base[:, :, None], 0.0), axis=0).astype(jnp.int32)
    q = late_owner // quarter
    alike = ((q == 1) | (q == 2)) == middle
    early = ((q == 1) | (q == 2)) == (q // 2 == mine // 2)
    part = jnp.where(early, jnp.where(alike, 1, 0), jnp.where(alike, 3, 2)) * quarter
    target = ((part + (offset - late_owner) % quarter) * cap + slot).reshape(cells)

    goals = ((2, 0, 3, 1), (3, 1, 2, 0), (1, 0, 3, 2), (0, 1, 2, 3))
    shifts = list(range(quarter))[::-1]
    calls = [(group, shifts[n : n + 2]) for group in range(4) for n in range(0, quarter, 2)]
    plan = []
    for s in range(sectors):
        k, o = s // quarter, s % quarter
        row = []
        for group, pair in calls:
            which = int(group >= 2 and k in (1, 2))
            dests = [at(goals[group][k], (o + a) % quarter) for a in pair]
            row += dests + [dict(mirror).get(s, s) if which else s, which]
            row += [(which * sectors + dest) * rows for dest in dests]
        plan.append(row)
    meta = jnp.asarray(np.array(plan, np.int32))[me]

    parts = [None] * sectors
    tables, done = [own], 0
    for group, pair in calls:
        if group == 2 and len(tables) == 1:
            other, _, _ = lat_solve([upper, lower], rim[: UP + 1], rim[UP + 1 :], rim[: UP + 1], rim[UP + 1 :])
            tables = [own, lon_solve(other, sides[: LEFT + 1], sides[LEFT + 1 :])]
        values = taps(meta, done, len(pair), base, tables, asked, cols, cap)
        done += 2 * len(pair) + 2
        for a, value in zip(pair, values):
            moves = [(at(k, o), at(goals[group][k], (o + a) % quarter)) for k in range(4) for o in range(quarter)]
            if any(i != j for i, j in moves):
                value = lax.ppermute(value, "lon", moves)
            parts[group * quarter + a] = value
    return place(target, parts).reshape(rows, cols, ch)


def solution(mesh):
    in_specs = (
        P("lat", "lon", None),
        P("lat", "lon", None, None),
        P("lat", "lon"),
        P("lat", "lon"),
        P(None, "lat", "lon"),
    )
    out_specs = P("lat", "lon", None)
    return jax.shard_map(transport, mesh=mesh, in_specs=in_specs, out_specs=out_specs, check_vma=False)
```

```python
import functools
import math

import jax
import jax.numpy as jnp
import numpy as np
from jax import lax
from jax.experimental import pallas as pl
from jax.experimental.pallas import tpu as pltpu
from jax.sharding import PartitionSpec as P


POLE = math.sqrt(3.0) - 2.0
GAIN = math.sqrt(3.0)
LANES = 128
TAPS = 6
UP, DOWN = 2, 3
LEFT, RIGHT = 1, 2
BF = jnp.bfloat16
F32 = jnp.float32
VMEM_LIMIT = 60 * 1024 * 1024


def split(x):
    high = x.astype(BF)
    return high, (x - high.astype(F32)).astype(BF)


def thirds(x):
    high, low = split(x)
    return jnp.concatenate([high, low, high], axis=1)


def dot(a, b):
    return lax.dot_general(a, b, (((1,), (0,)), ((), ())), preferred_element_type=F32)


def spline_weights(shift):
    rest = 1.0 - shift
    cube = shift * shift * shift
    return [
        rest * rest * rest / 6.0,
        (3.0 * cube - 6.0 * shift * shift + 4.0) / 6.0,
        (-3.0 * cube + 3.0 * shift * shift + 3.0 * shift + 1.0) / 6.0,
        cube / 6.0,
    ]


def edge_kernel(
    s_ref, owner_ref, column_ref, shift_ref, frac_ref, down_ref, up_ref, top_ref, bottom_ref, words_ref
):
    rows, cols = s_ref.shape[:2]
    top_row = lax.axis_index("lat") * rows
    lat_total = rows * lax.axis_size("lat")
    arrival = lax.broadcasted_iota(jnp.int32, (rows, cols), 0) + top_row
    row = jnp.clip(arrival - 1 + shift_ref[...], 1, lat_total - 3).astype(F32)
    column = (owner_ref[...] * cols + column_ref[...]).astype(F32)
    for k in range(words_ref.shape[0]):
        for w, word in enumerate((column, row, frac_ref[0], frac_ref[1])):
            words_ref[k, w] = jnp.full((rows, LANES), -1.0, F32)
            words_ref[k, w, :, :cols] = word
    first, last = s_ref[0], s_ref[rows - 1]
    far = 1.0 / (1.0 - POLE)

    acc = s_ref[0]
    for r in range(1, rows - UP):
        acc = s_ref[r] + POLE * acc
        if r == rows - 2 - DOWN:
            bottom_ref[DOWN] = 2.0 * far * last - acc
    down_ref[0] = acc
    for k in range(UP):
        down_ref[1 + k] = s_ref[rows - UP + k]
    for k in range(DOWN):
        bottom_ref[k] = 2.0 * last - s_ref[rows - 2 - k]

    acc = s_ref[rows - 1]
    for r in range(rows - 2, DOWN - 1, -1):
        acc = s_ref[r] + POLE * acc
    up_ref[DOWN] = acc
    for k in range(DOWN):
        up_ref[k] = s_ref[k]
    low = s_ref[rows - 1]
    for r in range(rows - 2, UP, -1):
        low = s_ref[r] + POLE * low
    top_ref[0] = 2.0 * far * first - low
    for k in range(UP):
        top_ref[1 + k] = 2.0 * first - s_ref[UP - k]


def edges(s, owner, columns, lat_shift, fractions):
    rows, cols, ch = s.shape
    shape = lambda n: jax.ShapeDtypeStruct((n, cols, ch), F32)
    words = jax.ShapeDtypeStruct((lax.axis_size("lon"), 4, rows, LANES), F32)
    return pl.pallas_call(
        edge_kernel,
        out_shape=(shape(UP + 1), shape(DOWN + 1), shape(UP + 1), shape(DOWN + 1), words),
        cost_estimate=pl.CostEstimate(flops=6 * s.size, bytes_accessed=6 * s.size, transcendentals=0),
        compiler_params=pltpu.CompilerParams(vmem_limit_bytes=VMEM_LIMIT),
        name="edges",
    )(s, owner, columns, lat_shift, fractions)


def lat_kernel(*refs, pieces, head):
    s_refs, refs = refs[:pieces], refs[pieces:]
    if pieces == 1:
        above_ref, below_ref, top_ref, bottom_ref, wr_ref, wl_ref, out_ref, right_ref, left_ref, rest_ref = refs
        rows, cols, _ = s_refs[0].shape
    else:
        wr_ref, wl_ref, out_ref, right_ref, left_ref = refs
        cols = s_refs[0].shape[1]
        rows = out_ref.shape[0] - UP - DOWN
    band = lax.axis_index("lat")
    at_top = band == 0
    at_bottom = band == lax.axis_size("lat") - 1
    total = rows + UP + DOWN

    def over(k):
        if pieces == 1:
            return jnp.where(at_top, top_ref[k], above_ref[k])
        return s_refs[1][rows - head + k]

    def under(k):
        if pieces == 1:
            return jnp.where(at_bottom, bottom_ref[k], below_ref[k])
        return s_refs[1][rows - head + UP + 1 + k]

    def row(e):
        if e < UP:
            return over(1 + e)
        if e >= UP + rows:
            return under(e - UP - rows)
        if pieces == 1 or e - UP < head:
            return s_refs[0][e - UP]
        return s_refs[1][e - UP - head]

    if pieces == 1:
        for r in range(head, rows):
            rest_ref[r - head] = s_refs[0][r]
        for k in range(UP + 1):
            rest_ref[rows - head + k] = over(k)
        for k in range(DOWN + 1):
            rest_ref[rows - head + UP + 1 + k] = under(k)

    acc = under(DOWN)
    for e in range(total - 1, -1, -1):
        acc = POLE * acc
        out_ref[e] = acc
        acc = acc + row(e)
    acc = over(0)
    for e in range(total):
        acc = row(e) + POLE * acc
        value = GAIN * (out_ref[e] + acc)
        out_ref[e] = value
        right_ref[0, pl.ds(e, 1)] = jnp.sum(value * wr_ref[...], axis=0, keepdims=True)
        for k in range(LEFT):
            right_ref[1 + k, pl.ds(e, 1)] = value[cols - LEFT + k : cols - LEFT + k + 1]
        for k in range(RIGHT):
            left_ref[k, pl.ds(e, 1)] = value[k : k + 1]
        left_ref[RIGHT, pl.ds(e, 1)] = jnp.sum(value * wl_ref[...], axis=0, keepdims=True)


def lat_solve(rows, head, pieces, halos=()):
    _, cols, ch = pieces[0].shape
    total = rows + UP + DOWN
    place = np.arange(cols)
    wr = np.where(place < cols - LEFT, POLE ** np.maximum(cols - LEFT - 1 - place, 0), 0.0)
    wl = np.where(place >= RIGHT, POLE ** np.maximum(place - RIGHT, 0), 0.0)
    wide = lambda w: jnp.asarray(np.broadcast_to(w[:, None], (cols, ch)).astype(np.float32))
    size = rows * cols * ch
    shapes = [
        jax.ShapeDtypeStruct((total, cols, ch), F32),
        jax.ShapeDtypeStruct((LEFT + 1, total, ch), F32),
        jax.ShapeDtypeStruct((RIGHT + 1, total, ch), F32),
    ]
    if halos:
        shapes.append(jax.ShapeDtypeStruct((rows - head + UP + DOWN + 2, cols, ch), F32))
    return pl.pallas_call(
        functools.partial(lat_kernel, pieces=len(pieces), head=head),
        out_shape=shapes,
        cost_estimate=pl.CostEstimate(flops=10 * size, bytes_accessed=10 * size, transcendentals=0),
        compiler_params=pltpu.CompilerParams(vmem_limit_bytes=VMEM_LIMIT),
        name="lat_solve",
    )(*pieces, *halos, wide(wr), wide(wl))


def lon_kernel(x_ref, *refs, packed):
    if packed:
        sides_ref, green_ref, out_ref = refs
    else:
        west_ref, east_ref, green_ref, out_ref, sides_ref = refs
        sides_ref[: LEFT + 1] = west_ref[...]
        sides_ref[LEFT + 1 :] = east_ref[...]
    total, cols, ch = x_ref.shape
    pad = LANES - cols - (LEFT + RIGHT + 2)
    for e in range(total):
        parts = [x_ref[e]]
        if packed:
            parts += [sides_ref[k, pl.ds(e, 1)] for k in range(LEFT + RIGHT + 2)]
        else:
            parts += [west_ref[k, pl.ds(e, 1)] for k in range(LEFT + 1)]
            parts += [east_ref[k, pl.ds(e, 1)] for k in range(RIGHT + 1)]
        parts += [jnp.zeros((pad, ch), F32)]
        turned = jnp.concatenate(parts, axis=0).T
        value = dot(thirds(turned), green_ref[...])
        out_ref[e * ch : (e + 1) * ch] = thirds(value)


def lon_solve(x, *sides):
    total, cols, ch = x.shape
    width = cols + LEFT + RIGHT
    j = np.arange(width) - LEFT
    green = np.zeros((LANES, LANES))
    green[:cols, :width] = POLE ** np.abs(np.arange(cols)[:, None] - j[None, :])
    green[cols, :width] = POLE ** (j + LEFT + 1)
    for k in range(LEFT):
        green[cols + 1 + k, :width] = POLE ** np.abs(j - (k - LEFT))
    for k in range(RIGHT):
        green[cols + LEFT + 1 + k, :width] = POLE ** np.abs(j - (cols + k))
    green[cols + LEFT + 1 + RIGHT, :width] = POLE ** (cols + RIGHT - j)
    green = jnp.asarray((GAIN * green).astype(np.float32))
    high, low = split(green)
    packed = len(sides) == 1
    shapes = [jax.ShapeDtypeStruct((total * ch, 3 * LANES), BF)]
    if not packed:
        shapes.append(jax.ShapeDtypeStruct((LEFT + RIGHT + 2, total, ch), F32))
    return pl.pallas_call(
        functools.partial(lon_kernel, packed=packed),
        out_shape=shapes,
        cost_estimate=pl.CostEstimate(
            flops=6 * total * LANES * LANES * ch, bytes_accessed=8 * x.size, transcendentals=0
        ),
        compiler_params=pltpu.CompilerParams(vmem_limit_bytes=VMEM_LIMIT),
        name="lon_solve",
    )(x, *sides, jnp.concatenate([high, high, low], axis=0))


def tap_kernel(meta_ref, base_ref, *refs, tables, count, cols, cap, span, at):
    meta = lambda k: meta_ref[at + k]
    table_refs, refs = refs[:tables], refs[tables + 1 :]
    cells_refs, tri_ref = refs[:count], refs[count]
    out_refs = refs[count + 1 : 2 * count + 1]
    rank, place, lon_w, lat_w, near, later, packed, ct_ref, sems, table_sem = refs[2 * count + 1 :]
    for n, table_ref in enumerate(table_refs):

        @pl.when(meta(count + 1) == n)
        def _(table_ref=table_ref):
            pltpu.make_async_copy(table_ref, ct_ref, table_sem).start()

    rows = rank.shape[1]
    ch = packed.shape[2]
    band = lax.axis_index("lat")
    lat_total = rows * lax.axis_size("lat")
    origin = (meta(count) * cols).astype(F32)

    def window_of(i):
        return i - jnp.where(band * rows + i == lat_total - 1, 1, 0)

    glob = lax.broadcasted_iota(jnp.int32, (rows, LANES), 0) + band * rows
    first = (glob - jnp.where(glob == lat_total - 1, 1, 0) - 1).astype(F32)
    for d in range(count):
        local = cells_refs[d][0, 0] - origin
        mine = (local >= 0.0) & (local < float(cols))
        one = jnp.where(mine, 1.0, 0.0)
        rank[d] = jnp.where(mine, dot(one.astype(BF), tri_ref[...]), -1000.0)
        place[d] = local
        turn = cells_refs[d][0, 1] - first
        a = spline_weights(cells_refs[d][0, 2])
        for n, w in enumerate(spline_weights(cells_refs[d][0, 3])):
            lon_w[d, n] = w * one
        for e in range(TAPS):
            total = jnp.zeros_like(one)
            for t in range(3):
                if 0 <= e - t < 4:
                    total = jnp.where(turn == float(t), a[e - t], total)
            lat_w[d, e] = total
    for buffer in (near, later):
        for k in range(3):
            buffer[k * LANES + span : (k + 1) * LANES] = jnp.zeros((LANES - span, count * LANES), BF)
    column = lax.broadcasted_iota(jnp.int32, (span, LANES), 0).astype(F32)
    step = lax.broadcasted_iota(jnp.int32, (8, LANES), 0)

    def build(i, buffer):
        here = pl.ds(i, 1)
        for d in range(count):
            far = column - place[d, here]
            basis = jnp.where(far == 0.0, lon_w[d, 0, here], 0.0)
            for n in range(1, 4):
                basis = jnp.where(far == float(n), lon_w[d, n, here], basis)
            high, low = split(basis)
            lanes = pl.ds(d * LANES, LANES)
            buffer[0:span, lanes] = high
            buffer[LANES : LANES + span, lanes] = high
            buffer[2 * LANES : 2 * LANES + span, lanes] = low

    def emit(i, buffer):
        half = TAPS // 2
        lines = []
        for part in range(2):
            at = pl.multiple_of((window_of(i) + part * half) * ch, ch)
            lines.append(dot(ct_ref[pl.ds(at, half * ch)], buffer[...]))
        for d in range(count):
            terms = []
            for e in range(TAPS):
                block = lines[e // half][e % half * ch : (e % half + 1) * ch, d * LANES : (d + 1) * LANES]
                terms.append(block * lat_w[d, e, pl.ds(i, 1)])
            value = ((terms[0] + terms[1]) + terms[2]) + ((terms[3] + terms[4]) + terms[5])
            high, low = split(value)
            base = base_ref[meta(count + 2 + d) + i]
            odd = lax.rem(base, 8)
            spot = rank[d, pl.ds(i, 1)] + odd.astype(F32)
            pick = jnp.where(column == spot, 1.0, 0.0).astype(BF)
            got = lax.dot_general(
                jnp.concatenate([pick, pick], axis=1),
                jnp.concatenate([high, low], axis=1),
                (((1,), (1,)), ((), ())),
                preferred_element_type=F32,
            )
            at = pl.multiple_of(base - odd, 8)
            packed[d, pl.ds(at, 8)] = jnp.where(step < odd, packed[d, pl.ds(at, 8)], got[:8])
            packed[d, pl.ds(pl.multiple_of(at + 8, 8), span - 8)] = got[8:]

    build(0, near)
    pltpu.make_async_copy(table_refs[0], ct_ref, table_sem).wait()

    @pl.loop(0, rows // 2)
    def _(pair):
        i = 2 * pair
        emit(i, near)
        build(i + 1, later)
        emit(i + 1, later)
        build(jnp.minimum(i + 2, rows - 1), near)

    copies = [
        pltpu.make_async_copy(packed.at[d, pl.ds(0, cap)], out_refs[d], sems.at[d]) for d in range(count)
    ]
    for copy in copies:
        copy.start()
    for copy in copies:
        copy.wait()


def taps(meta, at, count, base, tables, cells, cols, cap, after):
    _, words, rows, lanes = cells.shape
    ch = tables[0].shape[0] // (rows + UP + DOWN)
    span = 112
    tri = jnp.asarray(np.triu(np.ones((lanes, lanes)), 1), BF)
    weights = pltpu.VMEM((3 * LANES, count * lanes), BF)
    return pl.pallas_call(
        functools.partial(tap_kernel, tables=len(tables), count=count, cols=cols, cap=cap, span=span, at=at),
        out_shape=[jax.ShapeDtypeStruct((cap, ch), F32)] * count,
        grid_spec=pltpu.PrefetchScalarGridSpec(
            num_scalar_prefetch=2,
            grid=(1,),
            in_specs=[pl.BlockSpec(memory_space=pl.ANY)] * (len(tables) + 1)
            + [
                pl.BlockSpec((1, words, rows, lanes), functools.partial(lambda g, m, b, k: (m[k], 0, 0, 0), k=at + k))
                for k in range(count)
            ]
            + [pl.BlockSpec(tri.shape, lambda g, m, b: (0, 0))],
            out_specs=[pl.BlockSpec(memory_space=pl.ANY)] * count,
            scratch_shapes=[
                pltpu.VMEM((count, rows, lanes), F32),
                pltpu.VMEM((count, rows, lanes), F32),
                pltpu.VMEM((count, 4, rows, lanes), F32),
                pltpu.VMEM((count, TAPS, rows, lanes), F32),
                weights,
                weights,
                pltpu.VMEM((count, cap + span + 8, ch), F32),
                pltpu.VMEM(tables[0].shape, BF),
                pltpu.SemaphoreType.DMA((count,)),
                pltpu.SemaphoreType.DMA,
            ],
        ),
        cost_estimate=pl.CostEstimate(
            flops=6 * count * rows * TAPS * LANES * ch * LANES, bytes_accessed=2 * tables[0].size, transcendentals=0
        ),
        compiler_params=pltpu.CompilerParams(vmem_limit_bytes=VMEM_LIMIT),
        name="taps",
    )(meta, base, *tables, after, *([cells] * count), tri)


def place_kernel(target_ref, *refs, cap):
    *parts, out_ref, gathered, sems = refs
    copies = [
        pltpu.make_async_copy(part, gathered.at[pl.ds(k * cap, cap)], sems.at[k]) for k, part in enumerate(parts)
    ]
    for copy in copies:
        copy.start()
    for copy in copies:
        copy.wait()

    @pl.loop(0, out_ref.shape[0] // 8)
    def _(group):
        at = pl.multiple_of(group * 8, 8)
        lines = [gathered[pl.ds(target_ref[at + k], 1)] for k in range(8)]
        out_ref[pl.ds(at, 8)] = jnp.concatenate(lines, axis=0)


def place(target, parts):
    cap, ch = parts[0].shape
    cells = target.shape[0]
    count = len(parts)
    return pl.pallas_call(
        functools.partial(place_kernel, cap=cap),
        out_shape=jax.ShapeDtypeStruct((cells, ch), F32),
        grid_spec=pltpu.PrefetchScalarGridSpec(
            num_scalar_prefetch=1,
            grid=(1,),
            in_specs=[pl.BlockSpec(memory_space=pl.ANY)] * count,
            out_specs=pl.BlockSpec((cells, ch), lambda g, t: (0, 0)),
            scratch_shapes=[pltpu.VMEM((count * cap, ch), F32), pltpu.SemaphoreType.DMA((count,))],
        ),
        cost_estimate=pl.CostEstimate(flops=0, bytes_accessed=8 * count * cap * ch, transcendentals=0),
        compiler_params=pltpu.CompilerParams(vmem_limit_bytes=VMEM_LIMIT),
        name="place",
    )(target, *parts)


def earlier(mask):
    _, cols = mask.shape[1:]
    ones = mask.astype(F32)
    before = lax.dot_general(
        mask.astype(BF),
        jnp.asarray(np.triu(np.ones((cols, cols)), 1), BF),
        (((2,), (0,)), ((), ())),
        preferred_element_type=F32,
    )
    return before, bases(ones)


def bases(ones):
    rows = ones.shape[1]
    totals = jnp.sum(ones, axis=2)
    return jnp.dot(totals, jnp.asarray(np.triu(np.ones((rows, rows)), 1), F32), precision=lax.Precision.HIGHEST)


def transport(tracers, owners, columns, lat_shift, fractions):
    rows, cols, ch = tracers.shape
    bands = lax.axis_size("lat")
    sectors = lax.axis_size("lon")
    me = lax.axis_index("lon")
    cells = rows * cols
    cap = 3 * cells // sectors
    quarter = sectors // 4
    at = lambda q, o: q * quarter + o
    mirror = [(at(q, o), at((0, 2, 1, 3)[q], o)) for q in (1, 2) for o in range(quarter)]
    mine, offset = me // quarter, me % quarter
    middle = (mine == 1) | (mine == 2)

    head = rows // 4
    first = lax.ppermute(tracers[:head], "lon", mirror)
    owner = owners.reshape(rows, cols)
    down, up, top, bottom, words = edges(tracers, owner, columns, lat_shift, fractions)
    above = lax.ppermute(down, "lat", [(i, i + 1) for i in range(bands - 1)])
    below = lax.ppermute(up, "lat", [(i + 1, i) for i in range(bands - 1)])
    asked = lax.all_to_all(words, "lon", split_axis=0, concat_axis=0, tiled=True)

    x, right, left, rest = lat_solve(rows, head, [tracers], (above, below, top, bottom))
    west = lax.ppermute(right, "lon", [(i, (i + 1) % sectors) for i in range(sectors)])
    east = lax.ppermute(left, "lon", [((i + 1) % sectors, i) for i in range(sectors)])
    origins = np.array([[s * cols, dict(mirror).get(s, s) * cols] for s in range(sectors)], np.float32)
    local = asked[None, :, 0] - jnp.asarray(origins)[me][:, None, None, None]
    inside = ((local >= 0.0) & (local < float(cols))).astype(F32).reshape(2 * sectors, rows, -1)
    base = bases(inside).astype(jnp.int32).reshape(-1)

    own, sides = lon_solve(x, west, east)
    rest = lax.ppermute(rest, "lon", mirror)
    sides = lax.ppermute(sides, "lon", mirror)
    late_owner, x = lax.optimization_barrier((owner, x))
    every = jnp.arange(sectors, dtype=jnp.int32)
    mask = late_owner[None] == every[:, None, None]
    before, own_base = earlier(mask)
    slot = jnp.sum(jnp.where(mask, before + own_base[:, :, None], 0.0), axis=0).astype(jnp.int32)
    q = late_owner // quarter
    alike = ((q == 1) | (q == 2)) == middle
    early = ((q == 1) | (q == 2)) == (q // 2 == mine // 2)
    part = jnp.where(early, jnp.where(alike, 1, 0), jnp.where(alike, 3, 2)) * quarter
    target = ((part + (offset - late_owner) % quarter) * cap + slot).reshape(cells)

    goals = ((2, 0, 3, 1), (3, 1, 2, 0), (1, 0, 3, 2), (0, 1, 2, 3))
    shifts = list(range(quarter))[::-1]
    calls = [(group, shifts[n : n + 2]) for group in range(4) for n in range(0, quarter, 2)]
    plan = []
    for s in range(sectors):
        k, o = s // quarter, s % quarter
        row = []
        for group, pair in calls:
            which = int(group >= 2 and k in (1, 2))
            dests = [at(goals[group][k], (o + a) % quarter) for a in pair]
            row += dests + [dict(mirror).get(s, s) if which else s, which]
            row += [(which * sectors + dest) * rows for dest in dests]
        plan.append(row)
    meta = jnp.asarray(np.array(plan, np.int32))[me]

    parts = [None] * sectors
    tables, done, values = [own], 0, [own]
    for group, pair in calls:
        if group == 2 and len(tables) == 1:
            other = lat_solve(rows, head, [first, rest])[0]
            tables = [own, lon_solve(other, sides)[0]]
        values = taps(meta, done, len(pair), base, tables, asked, cols, cap, values[0])
        done += 2 * len(pair) + 2
        for a, value in zip(pair, values):
            moves = [(at(k, o), at(goals[group][k], (o + a) % quarter)) for k in range(4) for o in range(quarter)]
            if any(i != j for i, j in moves):
                value = lax.ppermute(value, "lon", moves)
            parts[group * quarter + a] = value
    return place(target, parts).reshape(rows, cols, ch)


def solution(mesh):
    in_specs = (
        P("lat", "lon", None),
        P("lat", "lon", None, None),
        P("lat", "lon"),
        P("lat", "lon"),
        P(None, "lat", "lon"),
    )
    out_specs = P("lat", "lon", None)
    return jax.shard_map(transport, mesh=mesh, in_specs=in_specs, out_specs=out_specs, check_vma=False)
```

```python
import functools
import math

import jax
import jax.numpy as jnp
import numpy as np
from jax import lax
from jax.experimental import pallas as pl
from jax.experimental.pallas import tpu as pltpu
from jax.sharding import PartitionSpec as P


POLE = math.sqrt(3.0) - 2.0
GAIN = math.sqrt(3.0)
LANES = 128
TAPS = 6
UP, DOWN = 2, 3
LEFT, RIGHT = 1, 2
BF = jnp.bfloat16
F32 = jnp.float32
VMEM_LIMIT = 60 * 1024 * 1024


def split(x):
    high = x.astype(BF)
    return high, (x - high.astype(F32)).astype(BF)


def thirds(x):
    high, low = split(x)
    return jnp.concatenate([high, low, high], axis=1)


def dot(a, b):
    return lax.dot_general(a, b, (((1,), (0,)), ((), ())), preferred_element_type=F32)


def spline_weights(shift):
    rest = 1.0 - shift
    cube = shift * shift * shift
    return [
        rest * rest * rest / 6.0,
        (3.0 * cube - 6.0 * shift * shift + 4.0) / 6.0,
        (-3.0 * cube + 3.0 * shift * shift + 3.0 * shift + 1.0) / 6.0,
        cube / 6.0,
    ]


def edge_kernel(
    s_ref, owner_ref, column_ref, shift_ref, frac_ref, down_ref, up_ref, top_ref, bottom_ref, words_ref
):
    rows, cols = s_ref.shape[:2]
    top_row = lax.axis_index("lat") * rows
    lat_total = rows * lax.axis_size("lat")
    arrival = lax.broadcasted_iota(jnp.int32, (rows, cols), 0) + top_row
    row = jnp.clip(arrival - 1 + shift_ref[...], 1, lat_total - 3).astype(F32)
    column = (owner_ref[...] * cols + column_ref[...]).astype(F32)
    for k in range(words_ref.shape[0]):
        for w, word in enumerate((column, row, frac_ref[0], frac_ref[1])):
            words_ref[k, w] = jnp.full((rows, LANES), -1.0, F32)
            words_ref[k, w, :, :cols] = word
    first, last = s_ref[0], s_ref[rows - 1]
    far = 1.0 / (1.0 - POLE)

    acc = s_ref[0]
    for r in range(1, rows - UP):
        acc = s_ref[r] + POLE * acc
        if r == rows - 2 - DOWN:
            bottom_ref[DOWN] = 2.0 * far * last - acc
    down_ref[0] = acc
    for k in range(UP):
        down_ref[1 + k] = s_ref[rows - UP + k]
    for k in range(DOWN):
        bottom_ref[k] = 2.0 * last - s_ref[rows - 2 - k]

    acc = s_ref[rows - 1]
    for r in range(rows - 2, DOWN - 1, -1):
        acc = s_ref[r] + POLE * acc
    up_ref[DOWN] = acc
    for k in range(DOWN):
        up_ref[k] = s_ref[k]
    low = s_ref[rows - 1]
    for r in range(rows - 2, UP, -1):
        low = s_ref[r] + POLE * low
    top_ref[0] = 2.0 * far * first - low
    for k in range(UP):
        top_ref[1 + k] = 2.0 * first - s_ref[UP - k]


def edges(s, owner, columns, lat_shift, fractions):
    rows, cols, ch = s.shape
    shape = lambda n: jax.ShapeDtypeStruct((n, cols, ch), F32)
    words = jax.ShapeDtypeStruct((lax.axis_size("lon"), 4, rows, LANES), F32)
    return pl.pallas_call(
        edge_kernel,
        out_shape=(shape(UP + 1), shape(DOWN + 1), shape(UP + 1), shape(DOWN + 1), words),
        cost_estimate=pl.CostEstimate(flops=6 * s.size, bytes_accessed=6 * s.size, transcendentals=0),
        compiler_params=pltpu.CompilerParams(vmem_limit_bytes=VMEM_LIMIT),
        name="edges",
    )(s, owner, columns, lat_shift, fractions)


def lat_kernel(*refs, pieces, head):
    s_refs, refs = refs[:pieces], refs[pieces:]
    if pieces == 1:
        above_ref, below_ref, top_ref, bottom_ref, wr_ref, wl_ref, out_ref, right_ref, left_ref, rest_ref = refs
        rows, cols, _ = s_refs[0].shape
    else:
        wr_ref, wl_ref, out_ref, right_ref, left_ref = refs
        cols = s_refs[0].shape[1]
        rows = out_ref.shape[0] - UP - DOWN
    band = lax.axis_index("lat")
    at_top = band == 0
    at_bottom = band == lax.axis_size("lat") - 1
    total = rows + UP + DOWN

    def over(k):
        if pieces == 1:
            return jnp.where(at_top, top_ref[k], above_ref[k])
        return s_refs[1][rows - head + k]

    def under(k):
        if pieces == 1:
            return jnp.where(at_bottom, bottom_ref[k], below_ref[k])
        return s_refs[1][rows - head + UP + 1 + k]

    def row(e):
        if e < UP:
            return over(1 + e)
        if e >= UP + rows:
            return under(e - UP - rows)
        if pieces == 1 or e - UP < head:
            return s_refs[0][e - UP]
        return s_refs[1][e - UP - head]

    if pieces == 1:
        for r in range(head, rows):
            rest_ref[r - head] = s_refs[0][r]
        for k in range(UP + 1):
            rest_ref[rows - head + k] = over(k)
        for k in range(DOWN + 1):
            rest_ref[rows - head + UP + 1 + k] = under(k)

    acc = under(DOWN)
    for e in range(total - 1, -1, -1):
        acc = POLE * acc
        out_ref[e] = acc
        acc = acc + row(e)
    acc = over(0)
    for e in range(total):
        acc = row(e) + POLE * acc
        value = GAIN * (out_ref[e] + acc)
        out_ref[e] = value
        right_ref[0, pl.ds(e, 1)] = jnp.sum(value * wr_ref[...], axis=0, keepdims=True)
        for k in range(LEFT):
            right_ref[1 + k, pl.ds(e, 1)] = value[cols - LEFT + k : cols - LEFT + k + 1]
        for k in range(RIGHT):
            left_ref[k, pl.ds(e, 1)] = value[k : k + 1]
        left_ref[RIGHT, pl.ds(e, 1)] = jnp.sum(value * wl_ref[...], axis=0, keepdims=True)


def lat_solve(rows, head, pieces, halos=()):
    _, cols, ch = pieces[0].shape
    total = rows + UP + DOWN
    place = np.arange(cols)
    wr = np.where(place < cols - LEFT, POLE ** np.maximum(cols - LEFT - 1 - place, 0), 0.0)
    wl = np.where(place >= RIGHT, POLE ** np.maximum(place - RIGHT, 0), 0.0)
    wide = lambda w: jnp.asarray(np.broadcast_to(w[:, None], (cols, ch)).astype(np.float32))
    size = rows * cols * ch
    shapes = [
        jax.ShapeDtypeStruct((total, cols, ch), F32),
        jax.ShapeDtypeStruct((LEFT + 1, total, ch), F32),
        jax.ShapeDtypeStruct((RIGHT + 1, total, ch), F32),
    ]
    if halos:
        shapes.append(jax.ShapeDtypeStruct((rows - head + UP + DOWN + 2, cols, ch), F32))
    return pl.pallas_call(
        functools.partial(lat_kernel, pieces=len(pieces), head=head),
        out_shape=shapes,
        cost_estimate=pl.CostEstimate(flops=10 * size, bytes_accessed=10 * size, transcendentals=0),
        compiler_params=pltpu.CompilerParams(vmem_limit_bytes=VMEM_LIMIT),
        name="lat_solve",
    )(*pieces, *halos, wide(wr), wide(wl))


def lon_kernel(x_ref, *refs, packed):
    if packed:
        sides_ref, green_ref, out_ref = refs
    else:
        west_ref, east_ref, green_ref, out_ref, sides_ref = refs
        sides_ref[: LEFT + 1] = west_ref[...]
        sides_ref[LEFT + 1 :] = east_ref[...]
    total, cols, ch = x_ref.shape
    pad = LANES - cols - (LEFT + RIGHT + 2)
    for e in range(total):
        parts = [x_ref[e]]
        if packed:
            parts += [sides_ref[k, pl.ds(e, 1)] for k in range(LEFT + RIGHT + 2)]
        else:
            parts += [west_ref[k, pl.ds(e, 1)] for k in range(LEFT + 1)]
            parts += [east_ref[k, pl.ds(e, 1)] for k in range(RIGHT + 1)]
        parts += [jnp.zeros((pad, ch), F32)]
        turned = jnp.concatenate(parts, axis=0).T
        value = dot(thirds(turned), green_ref[...])
        out_ref[e * ch : (e + 1) * ch] = thirds(value)


def lon_solve(x, *sides):
    total, cols, ch = x.shape
    width = cols + LEFT + RIGHT
    j = np.arange(width) - LEFT
    green = np.zeros((LANES, LANES))
    green[:cols, :width] = POLE ** np.abs(np.arange(cols)[:, None] - j[None, :])
    green[cols, :width] = POLE ** (j + LEFT + 1)
    for k in range(LEFT):
        green[cols + 1 + k, :width] = POLE ** np.abs(j - (k - LEFT))
    for k in range(RIGHT):
        green[cols + LEFT + 1 + k, :width] = POLE ** np.abs(j - (cols + k))
    green[cols + LEFT + 1 + RIGHT, :width] = POLE ** (cols + RIGHT - j)
    green = jnp.asarray((GAIN * green).astype(np.float32))
    high, low = split(green)
    packed = len(sides) == 1
    shapes = [jax.ShapeDtypeStruct((total * ch, 3 * LANES), BF)]
    if not packed:
        shapes.append(jax.ShapeDtypeStruct((LEFT + RIGHT + 2, total, ch), F32))
    return pl.pallas_call(
        functools.partial(lon_kernel, packed=packed),
        out_shape=shapes,
        cost_estimate=pl.CostEstimate(
            flops=6 * total * LANES * LANES * ch, bytes_accessed=8 * x.size, transcendentals=0
        ),
        compiler_params=pltpu.CompilerParams(vmem_limit_bytes=VMEM_LIMIT),
        name="lon_solve",
    )(x, *sides, jnp.concatenate([high, high, low], axis=0))


def tap_kernel(meta_ref, base_ref, *refs, tables, count, cols, cap, span, at):
    meta = lambda k: meta_ref[at + k]
    table_refs, refs = refs[:tables], refs[tables + 1 :]
    cells_refs, tri_ref = refs[:count], refs[count]
    out_refs = refs[count + 1 : 2 * count + 1]
    rank, place, lon_w, lat_w, near, later, packed, ct_ref, sems, table_sem = refs[2 * count + 1 :]
    for n, table_ref in enumerate(table_refs):

        @pl.when(meta(count + 1) == n)
        def _(table_ref=table_ref):
            pltpu.make_async_copy(table_ref, ct_ref, table_sem).start()

    rows = rank.shape[1]
    ch = packed.shape[2]
    band = lax.axis_index("lat")
    lat_total = rows * lax.axis_size("lat")
    origin = (meta(count) * cols).astype(F32)

    def window_of(i):
        return i - jnp.where(band * rows + i == lat_total - 1, 1, 0)

    glob = lax.broadcasted_iota(jnp.int32, (rows, LANES), 0) + band * rows
    first = (glob - jnp.where(glob == lat_total - 1, 1, 0) - 1).astype(F32)
    for d in range(count):
        local = cells_refs[d][0, 0] - origin
        mine = (local >= 0.0) & (local < float(cols))
        one = jnp.where(mine, 1.0, 0.0)
        rank[d] = jnp.where(mine, dot(one.astype(BF), tri_ref[...]), -1000.0)
        place[d] = local
        turn = cells_refs[d][0, 1] - first
        a = spline_weights(cells_refs[d][0, 2])
        for n, w in enumerate(spline_weights(cells_refs[d][0, 3])):
            lon_w[d, n] = w * one
        for e in range(TAPS):
            total = jnp.zeros_like(one)
            for t in range(3):
                if 0 <= e - t < 4:
                    total = jnp.where(turn == float(t), a[e - t], total)
            lat_w[d, e] = total
    for buffer in (near, later):
        for k in range(3):
            buffer[k * LANES + span : (k + 1) * LANES] = jnp.zeros((LANES - span, count * LANES), BF)
    column = lax.broadcasted_iota(jnp.int32, (span, LANES), 0).astype(F32)
    step = lax.broadcasted_iota(jnp.int32, (8, LANES), 0)

    def build(i, buffer):
        here = pl.ds(i, 1)
        for d in range(count):
            far = column - place[d, here]
            basis = jnp.where(far == 0.0, lon_w[d, 0, here], 0.0)
            for n in range(1, 4):
                basis = jnp.where(far == float(n), lon_w[d, n, here], basis)
            high, low = split(basis)
            lanes = pl.ds(d * LANES, LANES)
            buffer[0:span, lanes] = high
            buffer[LANES : LANES + span, lanes] = high
            buffer[2 * LANES : 2 * LANES + span, lanes] = low

    def emit(i, buffer):
        half = TAPS // 2
        lines = []
        for part in range(2):
            at = pl.multiple_of((window_of(i) + part * half) * ch, ch)
            lines.append(dot(ct_ref[pl.ds(at, half * ch)], buffer[...]))
        for d in range(count):
            terms = []
            for e in range(TAPS):
                block = lines[e // half][e % half * ch : (e % half + 1) * ch, d * LANES : (d + 1) * LANES]
                terms.append(block * lat_w[d, e, pl.ds(i, 1)])
            value = ((terms[0] + terms[1]) + terms[2]) + ((terms[3] + terms[4]) + terms[5])
            high, low = split(value)
            base = base_ref[meta(count + 2 + d) + i]
            odd = lax.rem(base, 8)
            spot = rank[d, pl.ds(i, 1)] + odd.astype(F32)
            pick = jnp.where(column == spot, 1.0, 0.0).astype(BF)
            got = lax.dot_general(
                jnp.concatenate([pick, pick], axis=1),
                jnp.concatenate([high, low], axis=1),
                (((1,), (1,)), ((), ())),
                preferred_element_type=F32,
            )
            at = pl.multiple_of(base - odd, 8)
            packed[d, pl.ds(at, 8)] = jnp.where(step < odd, packed[d, pl.ds(at, 8)], got[:8])
            packed[d, pl.ds(pl.multiple_of(at + 8, 8), span - 8)] = got[8:]

    build(0, near)
    pltpu.make_async_copy(table_refs[0], ct_ref, table_sem).wait()

    @pl.loop(0, rows // 2)
    def _(pair):
        i = 2 * pair
        emit(i, near)
        build(i + 1, later)
        emit(i + 1, later)
        build(jnp.minimum(i + 2, rows - 1), near)

    copies = [
        pltpu.make_async_copy(packed.at[d, pl.ds(0, cap)], out_refs[d], sems.at[d]) for d in range(count)
    ]
    for copy in copies:
        copy.start()
    for copy in copies:
        copy.wait()


def taps(meta, at, count, base, tables, cells, cols, cap, after):
    _, words, rows, lanes = cells.shape
    ch = tables[0].shape[0] // (rows + UP + DOWN)
    span = 112
    tri = jnp.asarray(np.triu(np.ones((lanes, lanes)), 1), BF)
    weights = pltpu.VMEM((3 * LANES, count * lanes), BF)
    return pl.pallas_call(
        functools.partial(tap_kernel, tables=len(tables), count=count, cols=cols, cap=cap, span=span, at=at),
        out_shape=[jax.ShapeDtypeStruct((cap, ch), F32)] * count,
        grid_spec=pltpu.PrefetchScalarGridSpec(
            num_scalar_prefetch=2,
            grid=(1,),
            in_specs=[pl.BlockSpec(memory_space=pl.ANY)] * (len(tables) + 1)
            + [
                pl.BlockSpec((1, words, rows, lanes), functools.partial(lambda g, m, b, k: (m[k], 0, 0, 0), k=at + k))
                for k in range(count)
            ]
            + [pl.BlockSpec(tri.shape, lambda g, m, b: (0, 0))],
            out_specs=[pl.BlockSpec(memory_space=pl.ANY)] * count,
            scratch_shapes=[
                pltpu.VMEM((count, rows, lanes), F32),
                pltpu.VMEM((count, rows, lanes), F32),
                pltpu.VMEM((count, 4, rows, lanes), F32),
                pltpu.VMEM((count, TAPS, rows, lanes), F32),
                weights,
                weights,
                pltpu.VMEM((count, cap + span + 8, ch), F32),
                pltpu.VMEM(tables[0].shape, BF),
                pltpu.SemaphoreType.DMA((count,)),
                pltpu.SemaphoreType.DMA,
            ],
        ),
        cost_estimate=pl.CostEstimate(
            flops=6 * count * rows * TAPS * LANES * ch * LANES, bytes_accessed=2 * tables[0].size, transcendentals=0
        ),
        compiler_params=pltpu.CompilerParams(vmem_limit_bytes=VMEM_LIMIT),
        name="taps",
    )(meta, base, *tables, after, *([cells] * count), tri)


def place_kernel(target_ref, *refs, cap):
    *parts, out_ref, gathered, sems = refs
    copies = [
        pltpu.make_async_copy(part, gathered.at[pl.ds(k * cap, cap)], sems.at[k]) for k, part in enumerate(parts)
    ]
    for copy in copies:
        copy.start()
    for copy in copies:
        copy.wait()

    @pl.loop(0, out_ref.shape[0] // 32)
    def _(group):
        at = pl.multiple_of(group * 32, 32)
        for k in range(32):
            out_ref[pl.ds(at + k, 1)] = gathered[pl.ds(target_ref[at + k], 1)]


def place(target, parts):
    cap, ch = parts[0].shape
    cells = target.shape[0]
    count = len(parts)
    return pl.pallas_call(
        functools.partial(place_kernel, cap=cap),
        out_shape=jax.ShapeDtypeStruct((cells, ch), F32),
        grid_spec=pltpu.PrefetchScalarGridSpec(
            num_scalar_prefetch=1,
            grid=(1,),
            in_specs=[pl.BlockSpec(memory_space=pl.ANY)] * count,
            out_specs=pl.BlockSpec((cells, ch), lambda g, t: (0, 0)),
            scratch_shapes=[pltpu.VMEM((count * cap, ch), F32), pltpu.SemaphoreType.DMA((count,))],
        ),
        cost_estimate=pl.CostEstimate(flops=0, bytes_accessed=8 * count * cap * ch, transcendentals=0),
        compiler_params=pltpu.CompilerParams(vmem_limit_bytes=16 * 1024 * 1024),
        name="place",
    )(target, *parts)


def earlier(mask):
    _, cols = mask.shape[1:]
    ones = mask.astype(F32)
    before = lax.dot_general(
        mask.astype(BF),
        jnp.asarray(np.triu(np.ones((cols, cols)), 1), BF),
        (((2,), (0,)), ((), ())),
        preferred_element_type=F32,
    )
    return before, bases(ones)


def bases(ones):
    rows = ones.shape[1]
    totals = jnp.sum(ones, axis=2)
    return jnp.dot(totals, jnp.asarray(np.triu(np.ones((rows, rows)), 1), F32), precision=lax.Precision.HIGHEST)


def transport(tracers, owners, columns, lat_shift, fractions):
    rows, cols, ch = tracers.shape
    bands = lax.axis_size("lat")
    sectors = lax.axis_size("lon")
    me = lax.axis_index("lon")
    cells = rows * cols
    cap = 3 * cells // sectors
    quarter = sectors // 4
    at = lambda q, o: q * quarter + o
    mirror = [(at(q, o), at((0, 2, 1, 3)[q], o)) for q in (1, 2) for o in range(quarter)]
    mine, offset = me // quarter, me % quarter
    middle = (mine == 1) | (mine == 2)

    head = rows // 2
    first = lax.ppermute(tracers[:head], "lon", mirror)
    owner = owners.reshape(rows, cols)
    down, up, top, bottom, words = edges(tracers, owner, columns, lat_shift, fractions)
    above = lax.ppermute(down, "lat", [(i, i + 1) for i in range(bands - 1)])
    below = lax.ppermute(up, "lat", [(i + 1, i) for i in range(bands - 1)])
    asked = lax.all_to_all(words, "lon", split_axis=0, concat_axis=0, tiled=True)

    x, right, left, rest = lat_solve(rows, head, [tracers], (above, below, top, bottom))
    west = lax.ppermute(right, "lon", [(i, (i + 1) % sectors) for i in range(sectors)])
    east = lax.ppermute(left, "lon", [((i + 1) % sectors, i) for i in range(sectors)])
    origins = np.array([[s * cols, dict(mirror).get(s, s) * cols] for s in range(sectors)], np.float32)
    local = asked[None, :, 0] - jnp.asarray(origins)[me][:, None, None, None]
    inside = ((local >= 0.0) & (local < float(cols))).astype(F32).reshape(2 * sectors, rows, -1)
    base = bases(inside).astype(jnp.int32).reshape(-1)

    own, sides = lon_solve(x, west, east)
    rest = lax.ppermute(rest, "lon", mirror)
    sides = lax.ppermute(sides, "lon", mirror)
    late_owner, x = lax.optimization_barrier((owner, x))
    every = jnp.arange(sectors, dtype=jnp.int32)
    mask = late_owner[None] == every[:, None, None]
    before, own_base = earlier(mask)
    slot = jnp.sum(jnp.where(mask, before + own_base[:, :, None], 0.0), axis=0).astype(jnp.int32)
    q = late_owner // quarter
    alike = ((q == 1) | (q == 2)) == middle
    early = ((q == 1) | (q == 2)) == (q // 2 == mine // 2)
    part = jnp.where(early, jnp.where(alike, 1, 0), jnp.where(alike, 3, 2)) * quarter
    target = ((part + (offset - late_owner) % quarter) * cap + slot).reshape(cells)

    goals = ((2, 0, 3, 1), (3, 1, 2, 0), (1, 0, 3, 2), (0, 1, 2, 3))
    shifts = list(range(quarter))[::-1]
    calls = [(group, shifts[n : n + 2]) for group in range(4) for n in range(0, quarter, 2)]
    plan = []
    for s in range(sectors):
        k, o = s // quarter, s % quarter
        row = []
        for group, pair in calls:
            which = int(group >= 2 and k in (1, 2))
            dests = [at(goals[group][k], (o + a) % quarter) for a in pair]
            row += dests + [dict(mirror).get(s, s) if which else s, which]
            row += [(which * sectors + dest) * rows for dest in dests]
        plan.append(row)
    meta = jnp.asarray(np.array(plan, np.int32))[me]

    parts = [None] * sectors
    tables, done, values = [own], 0, [own]
    for group, pair in calls:
        if group == 2 and len(tables) == 1:
            other = lat_solve(rows, head, [first, rest])[0]
            tables = [own, lon_solve(other, sides)[0]]
        values = taps(meta, done, len(pair), base, tables, asked, cols, cap, values[0])
        done += 2 * len(pair) + 2
        for a, value in zip(pair, values):
            moves = [(at(k, o), at(goals[group][k], (o + a) % quarter)) for k in range(4) for o in range(quarter)]
            if any(i != j for i, j in moves):
                value = lax.ppermute(value, "lon", moves)
            parts[group * quarter + a] = value
    return place(target, parts).reshape(rows, cols, ch)


def solution(mesh):
    in_specs = (
        P("lat", "lon", None),
        P("lat", "lon", None, None),
        P("lat", "lon"),
        P("lat", "lon"),
        P(None, "lat", "lon"),
    )
    out_specs = P("lat", "lon", None)
    return jax.shard_map(transport, mesh=mesh, in_specs=in_specs, out_specs=out_specs, check_vma=False)
```

```python
import functools
import math

import jax
import jax.numpy as jnp
import numpy as np
from jax import lax
from jax.experimental import pallas as pl
from jax.experimental.pallas import tpu as pltpu
from jax.sharding import PartitionSpec as P


POLE = math.sqrt(3.0) - 2.0
GAIN = math.sqrt(3.0)
LANES = 128
TAPS = 6
UP, DOWN = 2, 3
LEFT, RIGHT = 1, 2
BF = jnp.bfloat16
F32 = jnp.float32
VMEM_LIMIT = 60 * 1024 * 1024


def split(x):
    high = x.astype(BF)
    return high, (x - high.astype(F32)).astype(BF)


def thirds(x):
    high, low = split(x)
    return jnp.concatenate([high, low, high], axis=1)


def dot(a, b):
    return lax.dot_general(a, b, (((1,), (0,)), ((), ())), preferred_element_type=F32)


def spline_weights(shift):
    rest = 1.0 - shift
    cube = shift * shift * shift
    return [
        rest * rest * rest / 6.0,
        (3.0 * cube - 6.0 * shift * shift + 4.0) / 6.0,
        (-3.0 * cube + 3.0 * shift * shift + 3.0 * shift + 1.0) / 6.0,
        cube / 6.0,
    ]


def edge_kernel(
    s_ref, owner_ref, column_ref, shift_ref, frac_ref, down_ref, up_ref, top_ref, bottom_ref, words_ref
):
    rows, cols = s_ref.shape[:2]
    top_row = lax.axis_index("lat") * rows
    lat_total = rows * lax.axis_size("lat")
    arrival = lax.broadcasted_iota(jnp.int32, (rows, cols), 0) + top_row
    row = jnp.clip(arrival - 1 + shift_ref[...], 1, lat_total - 3).astype(F32)
    column = (owner_ref[...] * cols + column_ref[...]).astype(F32)
    for k in range(words_ref.shape[0]):
        for w, word in enumerate((column, row, frac_ref[0], frac_ref[1])):
            words_ref[k, w] = jnp.full((rows, LANES), -1.0, F32)
            words_ref[k, w, :, :cols] = word
    first, last = s_ref[0], s_ref[rows - 1]
    far = 1.0 / (1.0 - POLE)

    acc = s_ref[0]
    for r in range(1, rows - UP):
        acc = s_ref[r] + POLE * acc
        if r == rows - 2 - DOWN:
            bottom_ref[DOWN] = 2.0 * far * last - acc
    down_ref[0] = acc
    for k in range(UP):
        down_ref[1 + k] = s_ref[rows - UP + k]
    for k in range(DOWN):
        bottom_ref[k] = 2.0 * last - s_ref[rows - 2 - k]

    acc = s_ref[rows - 1]
    for r in range(rows - 2, DOWN - 1, -1):
        acc = s_ref[r] + POLE * acc
    up_ref[DOWN] = acc
    for k in range(DOWN):
        up_ref[k] = s_ref[k]
    low = s_ref[rows - 1]
    for r in range(rows - 2, UP, -1):
        low = s_ref[r] + POLE * low
    top_ref[0] = 2.0 * far * first - low
    for k in range(UP):
        top_ref[1 + k] = 2.0 * first - s_ref[UP - k]


def edges(s, owner, columns, lat_shift, fractions):
    rows, cols, ch = s.shape
    shape = lambda n: jax.ShapeDtypeStruct((n, cols, ch), F32)
    words = jax.ShapeDtypeStruct((lax.axis_size("lon"), 4, rows, LANES), F32)
    return pl.pallas_call(
        edge_kernel,
        out_shape=(shape(UP + 1), shape(DOWN + 1), shape(UP + 1), shape(DOWN + 1), words),
        cost_estimate=pl.CostEstimate(flops=6 * s.size, bytes_accessed=6 * s.size, transcendentals=0),
        compiler_params=pltpu.CompilerParams(vmem_limit_bytes=VMEM_LIMIT),
        name="edges",
    )(s, owner, columns, lat_shift, fractions)


def lat_kernel(*refs, pieces, head):
    s_refs, refs = refs[:pieces], refs[pieces:]
    if pieces == 1:
        above_ref, below_ref, top_ref, bottom_ref, wr_ref, wl_ref, out_ref, right_ref, left_ref, rest_ref = refs
        rows, cols, _ = s_refs[0].shape
    else:
        wr_ref, wl_ref, out_ref, right_ref, left_ref = refs
        cols = s_refs[0].shape[1]
        rows = out_ref.shape[0] - UP - DOWN
    band = lax.axis_index("lat")
    at_top = band == 0
    at_bottom = band == lax.axis_size("lat") - 1
    total = rows + UP + DOWN

    def over(k):
        if pieces == 1:
            return jnp.where(at_top, top_ref[k], above_ref[k])
        return s_refs[1][rows - head + k]

    def under(k):
        if pieces == 1:
            return jnp.where(at_bottom, bottom_ref[k], below_ref[k])
        return s_refs[1][rows - head + UP + 1 + k]

    def row(e):
        if e < UP:
            return over(1 + e)
        if e >= UP + rows:
            return under(e - UP - rows)
        if pieces == 1 or e - UP < head:
            return s_refs[0][e - UP]
        return s_refs[1][e - UP - head]

    if pieces == 1:
        for r in range(head, rows):
            rest_ref[r - head] = s_refs[0][r]
        for k in range(UP + 1):
            rest_ref[rows - head + k] = over(k)
        for k in range(DOWN + 1):
            rest_ref[rows - head + UP + 1 + k] = under(k)

    acc = under(DOWN)
    for e in range(total - 1, -1, -1):
        acc = POLE * acc
        out_ref[e] = acc
        acc = acc + row(e)
    acc = over(0)
    for e in range(total):
        acc = row(e) + POLE * acc
        value = GAIN * (out_ref[e] + acc)
        out_ref[e] = value
        right_ref[0, pl.ds(e, 1)] = jnp.sum(value * wr_ref[...], axis=0, keepdims=True)
        for k in range(LEFT):
            right_ref[1 + k, pl.ds(e, 1)] = value[cols - LEFT + k : cols - LEFT + k + 1]
        for k in range(RIGHT):
            left_ref[k, pl.ds(e, 1)] = value[k : k + 1]
        left_ref[RIGHT, pl.ds(e, 1)] = jnp.sum(value * wl_ref[...], axis=0, keepdims=True)


def lat_solve(rows, head, pieces, halos=()):
    _, cols, ch = pieces[0].shape
    total = rows + UP + DOWN
    place = np.arange(cols)
    wr = np.where(place < cols - LEFT, POLE ** np.maximum(cols - LEFT - 1 - place, 0), 0.0)
    wl = np.where(place >= RIGHT, POLE ** np.maximum(place - RIGHT, 0), 0.0)
    wide = lambda w: jnp.asarray(np.broadcast_to(w[:, None], (cols, ch)).astype(np.float32))
    size = rows * cols * ch
    shapes = [
        jax.ShapeDtypeStruct((total, cols, ch), F32),
        jax.ShapeDtypeStruct((LEFT + 1, total, ch), F32),
        jax.ShapeDtypeStruct((RIGHT + 1, total, ch), F32),
    ]
    if halos:
        shapes.append(jax.ShapeDtypeStruct((rows - head + UP + DOWN + 2, cols, ch), F32))
    return pl.pallas_call(
        functools.partial(lat_kernel, pieces=len(pieces), head=head),
        out_shape=shapes,
        cost_estimate=pl.CostEstimate(flops=10 * size, bytes_accessed=10 * size, transcendentals=0),
        compiler_params=pltpu.CompilerParams(vmem_limit_bytes=VMEM_LIMIT),
        name="lat_solve",
    )(*pieces, *halos, wide(wr), wide(wl))


def lon_kernel(x_ref, *refs, packed):
    if packed:
        sides_ref, green_ref, out_ref = refs
    else:
        west_ref, east_ref, green_ref, out_ref, sides_ref = refs
        sides_ref[: LEFT + 1] = west_ref[...]
        sides_ref[LEFT + 1 :] = east_ref[...]
    total, cols, ch = x_ref.shape
    pad = LANES - cols - (LEFT + RIGHT + 2)
    for e in range(total):
        parts = [x_ref[e]]
        if packed:
            parts += [sides_ref[k, pl.ds(e, 1)] for k in range(LEFT + RIGHT + 2)]
        else:
            parts += [west_ref[k, pl.ds(e, 1)] for k in range(LEFT + 1)]
            parts += [east_ref[k, pl.ds(e, 1)] for k in range(RIGHT + 1)]
        parts += [jnp.zeros((pad, ch), F32)]
        turned = jnp.concatenate(parts, axis=0).T
        value = dot(thirds(turned), green_ref[...])
        out_ref[e * ch : (e + 1) * ch] = thirds(value)


def lon_solve(x, *sides):
    total, cols, ch = x.shape
    width = cols + LEFT + RIGHT
    j = np.arange(width) - LEFT
    green = np.zeros((LANES, LANES))
    green[:cols, :width] = POLE ** np.abs(np.arange(cols)[:, None] - j[None, :])
    green[cols, :width] = POLE ** (j + LEFT + 1)
    for k in range(LEFT):
        green[cols + 1 + k, :width] = POLE ** np.abs(j - (k - LEFT))
    for k in range(RIGHT):
        green[cols + LEFT + 1 + k, :width] = POLE ** np.abs(j - (cols + k))
    green[cols + LEFT + 1 + RIGHT, :width] = POLE ** (cols + RIGHT - j)
    green = jnp.asarray((GAIN * green).astype(np.float32))
    high, low = split(green)
    packed = len(sides) == 1
    shapes = [jax.ShapeDtypeStruct((total * ch, 3 * LANES), BF)]
    if not packed:
        shapes.append(jax.ShapeDtypeStruct((LEFT + RIGHT + 2, total, ch), F32))
    return pl.pallas_call(
        functools.partial(lon_kernel, packed=packed),
        out_shape=shapes,
        cost_estimate=pl.CostEstimate(
            flops=6 * total * LANES * LANES * ch, bytes_accessed=8 * x.size, transcendentals=0
        ),
        compiler_params=pltpu.CompilerParams(vmem_limit_bytes=VMEM_LIMIT),
        name="lon_solve",
    )(x, *sides, jnp.concatenate([high, high, low], axis=0))


def tap_kernel(meta_ref, base_ref, *refs, tables, count, cols, cap, span, at):
    meta = lambda k: meta_ref[at + k]
    table_refs, refs = refs[:tables], refs[tables + 1 :]
    cells_refs, tri_ref = refs[:count], refs[count]
    out_refs = refs[count + 1 : 2 * count + 1]
    rank, words, got, tab, near, later, packed, ct_ref, sems, table_sem = refs[2 * count + 1 :]
    for n, table_ref in enumerate(table_refs):

        @pl.when(meta(count + 1) == n)
        def _(table_ref=table_ref):
            pltpu.make_async_copy(table_ref, ct_ref, table_sem).start()

    rows = rank.shape[1]
    pairs = rows // 2
    ch = packed.shape[2]
    window = TAPS + 1
    band = lax.axis_index("lat")
    origin = (meta(count) * cols).astype(F32)
    for d in range(count):
        local = cells_refs[d][0, 0] - origin
        mine = (local >= 0.0) & (local < float(cols))
        one = jnp.where(mine, 1.0, 0.0)
        rank[d] = jnp.where(mine, dot(one.astype(BF), tri_ref[...]), -1000.0)
        parts = [local, cells_refs[d][0, 1] - (band * rows - UP).astype(F32)]
        for w in (2, 3):
            left = cells_refs[d][0, w]
            for _ in range(3):
                part = left.astype(BF).astype(F32)
                parts.append(part)
                left = left - part
        for w, part in enumerate(parts):
            words[d, :, w, :] = part
    for buffer in (near, later):
        for k in range(3):
            buffer[k * LANES + span : (k + 1) * LANES] = jnp.zeros((LANES - span, count * LANES), BF)
    column = lax.broadcasted_iota(jnp.int32, (span, count * LANES), 0).astype(F32)
    slot = lax.broadcasted_iota(jnp.int32, (LANES, LANES), 0)
    place = slot.astype(F32)

    def spot(j, d):
        start = meta(count + 2 + d) + 2 * j
        base = base_ref[start]
        return base, lax.rem(base, 8), base_ref[start + 1] - base, base_ref[start + 2] - base

    def gather(j, lap):
        i = 2 * j
        found = []
        for d in range(count):
            _, odd, count_first, _ = spot(j, d)
            skip = odd - lap * LANES
            picks = [
                jnp.where(place == rank[d, pl.ds(i, 1)] + skip.astype(F32), 1.0, 0.0),
                jnp.where(place == rank[d, pl.ds(i + 1, 1)] + (skip + count_first).astype(F32), 1.0, 0.0),
            ]
            found.append(
                lax.dot_general(
                    jnp.concatenate([words[d, i], words[d, i + 1]], axis=1).astype(BF),
                    jnp.concatenate(picks, axis=1).astype(BF),
                    (((1,), (1,)), ((), ())),
                    preferred_element_type=F32,
                )
            )
        return found

    def keep(j, found):
        for d in range(count):
            got[j, :, d * LANES : (d + 1) * LANES] = found[d]

    def weigh(read, write, first):
        a = spline_weights(read(2) + read(3) + read(4))
        b = spline_weights(read(5) + read(6) + read(7))
        turn = read(1) - 1.0 - first
        write(0, read(0))
        for n in range(4):
            write(1 + n, b[n])
        for e in range(window):
            total = jnp.zeros_like(turn)
            for t in range(4):
                if 0 <= e - t < 4:
                    total = jnp.where(turn == float(t), a[e - t], total)
            write(5 + e, total)

    def write_all(n, value):
        tab[:, n, :] = value

    def build(j, buffer):
        far = column - tab[j, 0:1]
        basis = jnp.where(far == 0.0, tab[j, 1:2], 0.0)
        for n in range(1, 4):
            basis = jnp.where(far == float(n), tab[j, 1 + n : 2 + n], basis)
        high, low = split(basis)
        buffer[0:span] = high
        buffer[LANES : LANES + span] = high
        buffer[2 * LANES : 2 * LANES + span] = low

    def emit(j, buffer, lap):
        half = window * ch // 2
        lines = []
        for part in range(2):
            first = pl.multiple_of(2 * j * ch + part * half, half)
            lines.append(dot(ct_ref[pl.ds(first, half)], buffer[...]))
        lines = jnp.concatenate(lines, axis=0)
        terms = [lines[e * ch : (e + 1) * ch] * tab[j, 5 + e : 6 + e] for e in range(window)]
        value = ((terms[0] + terms[1]) + (terms[2] + terms[3])) + ((terms[4] + terms[5]) + terms[6])
        for d in range(count):
            turned = value[:, d * LANES : (d + 1) * LANES].T
            base, odd, _, total = spot(j, d)
            to = pl.multiple_of(base - odd + lap * LANES, 8)
            if lap:
                whole = pl.ds(to, LANES)
                packed[d, whole] = jnp.where(slot < odd + total - lap * LANES, turned, packed[d, whole])
            else:
                packed[d, pl.ds(to, 8)] = jnp.where(slot[:8] < odd, packed[d, pl.ds(to, 8)], turned[:8])
                packed[d, pl.ds(pl.multiple_of(to + 8, 8), LANES - 8)] = turned[8:]

    @pl.loop(0, pairs // 2)
    def _(k):
        found = [gather(2 * k, 0), gather(2 * k + 1, 0)]
        keep(2 * k, found[0])
        keep(2 * k + 1, found[1])

    even = 2 * lax.broadcasted_iota(jnp.int32, (pairs, count * LANES), 0)
    weigh(lambda w: got[:, w, :], write_all, even.astype(F32))
    build(0, near)
    pltpu.make_async_copy(table_refs[0], ct_ref, table_sem).wait()

    @pl.loop(0, pairs // 2)
    def _(k):
        emit(2 * k, near, 0)
        build(2 * k + 1, later)
        emit(2 * k + 1, later, 0)
        build(jnp.minimum(2 * k + 2, pairs - 1), near)

    @pl.loop(0, pairs)
    def _(j):
        over = False
        for d in range(count):
            _, odd, _, total = spot(j, d)
            over = over | (odd + total > LANES)

        @pl.when(over)
        def _():
            keep(j, gather(j, 1))

            def write_one(n, value):
                tab[j, n : n + 1] = value

            weigh(lambda w: got[j, w : w + 1], write_one, (2 * j).astype(F32))
            build(j, near)
            emit(j, near, 1)

    copies = [
        pltpu.make_async_copy(packed.at[d, pl.ds(0, cap)], out_refs[d], sems.at[d]) for d in range(count)
    ]
    for copy in copies:
        copy.start()
    for copy in copies:
        copy.wait()


def taps(meta, at, count, base, tables, cells, cols, cap, after):
    _, words, rows, lanes = cells.shape
    ch = tables[0].shape[0] // (rows + UP + DOWN)
    span = 112
    tri = jnp.asarray(np.triu(np.ones((lanes, lanes)), 1), BF)
    weights = pltpu.VMEM((3 * LANES, count * lanes), BF)
    return pl.pallas_call(
        functools.partial(tap_kernel, tables=len(tables), count=count, cols=cols, cap=cap, span=span, at=at),
        out_shape=[jax.ShapeDtypeStruct((cap, ch), F32)] * count,
        grid_spec=pltpu.PrefetchScalarGridSpec(
            num_scalar_prefetch=2,
            grid=(1,),
            in_specs=[pl.BlockSpec(memory_space=pl.ANY)] * (len(tables) + 1)
            + [
                pl.BlockSpec((1, words, rows, lanes), functools.partial(lambda g, m, b, k: (m[k], 0, 0, 0), k=at + k))
                for k in range(count)
            ]
            + [pl.BlockSpec(tri.shape, lambda g, m, b: (0, 0))],
            out_specs=[pl.BlockSpec(memory_space=pl.ANY)] * count,
            scratch_shapes=[
                pltpu.VMEM((count, rows, lanes), F32),
                pltpu.VMEM((count, rows, 8, lanes), F32),
                pltpu.VMEM((rows // 2, 8, count * lanes), F32),
                pltpu.VMEM((rows // 2, 16, count * lanes), F32),
                weights,
                weights,
                pltpu.VMEM((count, cap + 2 * lanes + 8, ch), F32),
                pltpu.VMEM(tables[0].shape, BF),
                pltpu.SemaphoreType.DMA((count,)),
                pltpu.SemaphoreType.DMA,
            ],
        ),
        cost_estimate=pl.CostEstimate(
            flops=6 * count * rows * TAPS * LANES * ch * LANES, bytes_accessed=2 * tables[0].size, transcendentals=0
        ),
        compiler_params=pltpu.CompilerParams(vmem_limit_bytes=VMEM_LIMIT),
        name="taps",
    )(meta, base, *tables, after, *([cells] * count), tri)


def place_kernel(target_ref, *refs, cap):
    *parts, out_ref, gathered, sems = refs
    copies = [
        pltpu.make_async_copy(part, gathered.at[pl.ds(k * cap, cap)], sems.at[k]) for k, part in enumerate(parts)
    ]
    for copy in copies:
        copy.start()
    for copy in copies:
        copy.wait()

    @pl.loop(0, out_ref.shape[0] // 32)
    def _(group):
        at = pl.multiple_of(group * 32, 32)
        for k in range(32):
            out_ref[pl.ds(at + k, 1)] = gathered[pl.ds(target_ref[at + k], 1)]


def place(target, parts):
    cap, ch = parts[0].shape
    cells = target.shape[0]
    count = len(parts)
    return pl.pallas_call(
        functools.partial(place_kernel, cap=cap),
        out_shape=jax.ShapeDtypeStruct((cells, ch), F32),
        grid_spec=pltpu.PrefetchScalarGridSpec(
            num_scalar_prefetch=1,
            grid=(1,),
            in_specs=[pl.BlockSpec(memory_space=pl.ANY)] * count,
            out_specs=pl.BlockSpec((cells, ch), lambda g, t: (0, 0)),
            scratch_shapes=[pltpu.VMEM((count * cap, ch), F32), pltpu.SemaphoreType.DMA((count,))],
        ),
        cost_estimate=pl.CostEstimate(flops=0, bytes_accessed=8 * count * cap * ch, transcendentals=0),
        compiler_params=pltpu.CompilerParams(vmem_limit_bytes=16 * 1024 * 1024),
        name="place",
    )(target, *parts)


def earlier(mask):
    _, cols = mask.shape[1:]
    ones = mask.astype(F32)
    before = lax.dot_general(
        mask.astype(BF),
        jnp.asarray(np.triu(np.ones((cols, cols)), 1), BF),
        (((2,), (0,)), ((), ())),
        preferred_element_type=F32,
    )
    return before, bases(ones)


def bases(ones):
    rows = ones.shape[1]
    totals = jnp.sum(ones, axis=2)
    return jnp.dot(totals, jnp.asarray(np.triu(np.ones((rows, rows + 1)), 1), F32), precision=lax.Precision.HIGHEST)


def transport(tracers, owners, columns, lat_shift, fractions):
    rows, cols, ch = tracers.shape
    bands = lax.axis_size("lat")
    sectors = lax.axis_size("lon")
    me = lax.axis_index("lon")
    cells = rows * cols
    cap = 3 * cells // sectors
    quarter = sectors // 4
    at = lambda q, o: q * quarter + o
    mirror = [(at(q, o), at((0, 2, 1, 3)[q], o)) for q in (1, 2) for o in range(quarter)]
    mine, offset = me // quarter, me % quarter
    middle = (mine == 1) | (mine == 2)

    head = rows // 2
    first = lax.ppermute(tracers[:head], "lon", mirror)
    owner = owners.reshape(rows, cols)
    down, up, top, bottom, words = edges(tracers, owner, columns, lat_shift, fractions)
    above = lax.ppermute(down, "lat", [(i, i + 1) for i in range(bands - 1)])
    below = lax.ppermute(up, "lat", [(i + 1, i) for i in range(bands - 1)])
    asked = lax.all_to_all(words, "lon", split_axis=0, concat_axis=0, tiled=True)

    x, right, left, rest = lat_solve(rows, head, [tracers], (above, below, top, bottom))
    west = lax.ppermute(right, "lon", [(i, (i + 1) % sectors) for i in range(sectors)])
    east = lax.ppermute(left, "lon", [((i + 1) % sectors, i) for i in range(sectors)])
    origins = np.array([[s * cols, dict(mirror).get(s, s) * cols] for s in range(sectors)], np.float32)
    local = asked[None, :, 0] - jnp.asarray(origins)[me][:, None, None, None]
    inside = ((local >= 0.0) & (local < float(cols))).astype(F32).reshape(2 * sectors, rows, -1)
    base = bases(inside).astype(jnp.int32).reshape(-1)

    own, sides = lon_solve(x, west, east)
    rest = lax.ppermute(rest, "lon", mirror)
    sides = lax.ppermute(sides, "lon", mirror)
    late_owner, x = lax.optimization_barrier((owner, x))
    every = jnp.arange(sectors, dtype=jnp.int32)
    mask = late_owner[None] == every[:, None, None]
    before, own_base = earlier(mask)
    slot = jnp.sum(jnp.where(mask, before + own_base[:, :-1, None], 0.0), axis=0).astype(jnp.int32)
    q = late_owner // quarter
    alike = ((q == 1) | (q == 2)) == middle
    early = ((q == 1) | (q == 2)) == (q // 2 == mine // 2)
    part = jnp.where(early, jnp.where(alike, 1, 0), jnp.where(alike, 3, 2)) * quarter
    target = ((part + (offset - late_owner) % quarter) * cap + slot).reshape(cells)

    goals = ((2, 0, 3, 1), (3, 1, 2, 0), (1, 0, 3, 2), (0, 1, 2, 3))
    shifts = list(range(quarter))[::-1]
    calls = [(group, shifts[n : n + 2]) for group in range(4) for n in range(0, quarter, 2)]
    plan = []
    for s in range(sectors):
        k, o = s // quarter, s % quarter
        row = []
        for group, pair in calls:
            which = int(group >= 2 and k in (1, 2))
            dests = [at(goals[group][k], (o + a) % quarter) for a in pair]
            row += dests + [dict(mirror).get(s, s) if which else s, which]
            row += [(which * sectors + dest) * (rows + 1) for dest in dests]
        plan.append(row)
    meta = jnp.asarray(np.array(plan, np.int32))[me]

    parts = [None] * sectors
    tables, done, values = [own], 0, [own]
    for group, pair in calls:
        if group == 2 and len(tables) == 1:
            other = lat_solve(rows, head, [first, rest])[0]
            tables = [own, lon_solve(other, sides)[0]]
        values = taps(meta, done, len(pair), base, tables, asked, cols, cap, values[0])
        done += 2 * len(pair) + 2
        for a, value in zip(pair, values):
            moves = [(at(k, o), at(goals[group][k], (o + a) % quarter)) for k in range(4) for o in range(quarter)]
            if any(i != j for i, j in moves):
                value = lax.ppermute(value, "lon", moves)
            parts[group * quarter + a] = value
    return place(target, parts).reshape(rows, cols, ch)


def solution(mesh):
    in_specs = (
        P("lat", "lon", None),
        P("lat", "lon", None, None),
        P("lat", "lon"),
        P("lat", "lon"),
        P(None, "lat", "lon"),
    )
    out_specs = P("lat", "lon", None)
    return jax.shard_map(transport, mesh=mesh, in_specs=in_specs, out_specs=out_specs, check_vma=False)
```

```python
import functools
import math

import jax
import jax.numpy as jnp
import numpy as np
from jax import lax
from jax.experimental import pallas as pl
from jax.experimental.pallas import tpu as pltpu
from jax.sharding import PartitionSpec as P


POLE = math.sqrt(3.0) - 2.0
GAIN = math.sqrt(3.0)
LANES = 128
TAPS = 6
UP, DOWN = 2, 3
LEFT, RIGHT = 1, 2
BF = jnp.bfloat16
F32 = jnp.float32
VMEM_LIMIT = 60 * 1024 * 1024


def split(x):
    high = x.astype(BF)
    return high, (x - high.astype(F32)).astype(BF)


def thirds(x):
    high, low = split(x)
    return jnp.concatenate([high, low, high], axis=1)


def dot(a, b):
    return lax.dot_general(a, b, (((1,), (0,)), ((), ())), preferred_element_type=F32)


def spline_weights(shift):
    rest = 1.0 - shift
    cube = shift * shift * shift
    return [
        rest * rest * rest / 6.0,
        (3.0 * cube - 6.0 * shift * shift + 4.0) / 6.0,
        (-3.0 * cube + 3.0 * shift * shift + 3.0 * shift + 1.0) / 6.0,
        cube / 6.0,
    ]


def edge_kernel(
    s_ref, owner_ref, column_ref, shift_ref, frac_ref, down_ref, up_ref, top_ref, bottom_ref, words_ref
):
    rows, cols = s_ref.shape[:2]
    top_row = lax.axis_index("lat") * rows
    lat_total = rows * lax.axis_size("lat")
    arrival = lax.broadcasted_iota(jnp.int32, (rows, cols), 0) + top_row
    row = jnp.clip(arrival - 1 + shift_ref[...], 1, lat_total - 3).astype(F32)
    column = (owner_ref[...] * cols + column_ref[...]).astype(F32)
    for k in range(words_ref.shape[0]):
        for w, word in enumerate((column, row, frac_ref[0], frac_ref[1])):
            words_ref[k, w] = jnp.full((rows, LANES), -1.0, F32)
            words_ref[k, w, :, :cols] = word
    first, last = s_ref[0], s_ref[rows - 1]
    far = 1.0 / (1.0 - POLE)

    acc = s_ref[0]
    for r in range(1, rows - UP):
        acc = s_ref[r] + POLE * acc
        if r == rows - 2 - DOWN:
            bottom_ref[DOWN] = 2.0 * far * last - acc
    down_ref[0] = acc
    for k in range(UP):
        down_ref[1 + k] = s_ref[rows - UP + k]
    for k in range(DOWN):
        bottom_ref[k] = 2.0 * last - s_ref[rows - 2 - k]

    acc = s_ref[rows - 1]
    for r in range(rows - 2, DOWN - 1, -1):
        acc = s_ref[r] + POLE * acc
    up_ref[DOWN] = acc
    for k in range(DOWN):
        up_ref[k] = s_ref[k]
    low = s_ref[rows - 1]
    for r in range(rows - 2, UP, -1):
        low = s_ref[r] + POLE * low
    top_ref[0] = 2.0 * far * first - low
    for k in range(UP):
        top_ref[1 + k] = 2.0 * first - s_ref[UP - k]


def edges(s, owner, columns, lat_shift, fractions):
    rows, cols, ch = s.shape
    shape = lambda n: jax.ShapeDtypeStruct((n, cols, ch), F32)
    words = jax.ShapeDtypeStruct((lax.axis_size("lon"), 4, rows, LANES), F32)
    return pl.pallas_call(
        edge_kernel,
        out_shape=(shape(UP + 1), shape(DOWN + 1), shape(UP + 1), shape(DOWN + 1), words),
        cost_estimate=pl.CostEstimate(flops=6 * s.size, bytes_accessed=6 * s.size, transcendentals=0),
        compiler_params=pltpu.CompilerParams(vmem_limit_bytes=VMEM_LIMIT),
        name="edges",
    )(s, owner, columns, lat_shift, fractions)


def lat_kernel(*refs, pieces, head):
    s_refs, refs = refs[:pieces], refs[pieces:]
    if pieces == 1:
        above_ref, below_ref, top_ref, bottom_ref, wr_ref, wl_ref, out_ref, right_ref, left_ref, rest_ref = refs
        rows, cols, _ = s_refs[0].shape
    else:
        wr_ref, wl_ref, out_ref, right_ref, left_ref = refs
        cols = s_refs[0].shape[1]
        rows = out_ref.shape[0] - UP - DOWN
    band = lax.axis_index("lat")
    at_top = band == 0
    at_bottom = band == lax.axis_size("lat") - 1
    total = rows + UP + DOWN

    def over(k):
        if pieces == 1:
            return jnp.where(at_top, top_ref[k], above_ref[k])
        return s_refs[1][rows - head + k]

    def under(k):
        if pieces == 1:
            return jnp.where(at_bottom, bottom_ref[k], below_ref[k])
        return s_refs[1][rows - head + UP + 1 + k]

    def row(e):
        if e < UP:
            return over(1 + e)
        if e >= UP + rows:
            return under(e - UP - rows)
        if pieces == 1 or e - UP < head:
            return s_refs[0][e - UP]
        return s_refs[1][e - UP - head]

    if pieces == 1:
        for r in range(head, rows):
            rest_ref[r - head] = s_refs[0][r]
        for k in range(UP + 1):
            rest_ref[rows - head + k] = over(k)
        for k in range(DOWN + 1):
            rest_ref[rows - head + UP + 1 + k] = under(k)

    acc = under(DOWN)
    for e in range(total - 1, -1, -1):
        acc = POLE * acc
        out_ref[e] = acc
        acc = acc + row(e)
    acc = over(0)
    for e in range(total):
        acc = row(e) + POLE * acc
        value = GAIN * (out_ref[e] + acc)
        out_ref[e] = value
        right_ref[0, pl.ds(e, 1)] = jnp.sum(value * wr_ref[...], axis=0, keepdims=True)
        for k in range(LEFT):
            right_ref[1 + k, pl.ds(e, 1)] = value[cols - LEFT + k : cols - LEFT + k + 1]
        for k in range(RIGHT):
            left_ref[k, pl.ds(e, 1)] = value[k : k + 1]
        left_ref[RIGHT, pl.ds(e, 1)] = jnp.sum(value * wl_ref[...], axis=0, keepdims=True)


def lat_solve(rows, head, pieces, halos=()):
    _, cols, ch = pieces[0].shape
    total = rows + UP + DOWN
    place = np.arange(cols)
    wr = np.where(place < cols - LEFT, POLE ** np.maximum(cols - LEFT - 1 - place, 0), 0.0)
    wl = np.where(place >= RIGHT, POLE ** np.maximum(place - RIGHT, 0), 0.0)
    wide = lambda w: jnp.asarray(np.broadcast_to(w[:, None], (cols, ch)).astype(np.float32))
    size = rows * cols * ch
    shapes = [
        jax.ShapeDtypeStruct((total, cols, ch), F32),
        jax.ShapeDtypeStruct((LEFT + 1, total, ch), F32),
        jax.ShapeDtypeStruct((RIGHT + 1, total, ch), F32),
    ]
    if halos:
        shapes.append(jax.ShapeDtypeStruct((rows - head + UP + DOWN + 2, cols, ch), F32))
    return pl.pallas_call(
        functools.partial(lat_kernel, pieces=len(pieces), head=head),
        out_shape=shapes,
        cost_estimate=pl.CostEstimate(flops=10 * size, bytes_accessed=10 * size, transcendentals=0),
        compiler_params=pltpu.CompilerParams(vmem_limit_bytes=VMEM_LIMIT),
        name="lat_solve",
    )(*pieces, *halos, wide(wr), wide(wl))


def lon_kernel(x_ref, *refs, packed):
    if packed:
        sides_ref, green_ref, out_ref = refs
    else:
        west_ref, east_ref, green_ref, out_ref, sides_ref = refs
        sides_ref[: LEFT + 1] = west_ref[...]
        sides_ref[LEFT + 1 :] = east_ref[...]
    total, cols, ch = x_ref.shape
    pad = LANES - cols - (LEFT + RIGHT + 2)
    for e in range(total):
        parts = [x_ref[e]]
        if packed:
            parts += [sides_ref[k, pl.ds(e, 1)] for k in range(LEFT + RIGHT + 2)]
        else:
            parts += [west_ref[k, pl.ds(e, 1)] for k in range(LEFT + 1)]
            parts += [east_ref[k, pl.ds(e, 1)] for k in range(RIGHT + 1)]
        parts += [jnp.zeros((pad, ch), F32)]
        turned = jnp.concatenate(parts, axis=0).T
        value = dot(thirds(turned), green_ref[...])
        out_ref[e * ch : (e + 1) * ch] = thirds(value)


def lon_solve(x, *sides):
    total, cols, ch = x.shape
    width = cols + LEFT + RIGHT
    j = np.arange(width) - LEFT
    green = np.zeros((LANES, LANES))
    green[:cols, :width] = POLE ** np.abs(np.arange(cols)[:, None] - j[None, :])
    green[cols, :width] = POLE ** (j + LEFT + 1)
    for k in range(LEFT):
        green[cols + 1 + k, :width] = POLE ** np.abs(j - (k - LEFT))
    for k in range(RIGHT):
        green[cols + LEFT + 1 + k, :width] = POLE ** np.abs(j - (cols + k))
    green[cols + LEFT + 1 + RIGHT, :width] = POLE ** (cols + RIGHT - j)
    green = jnp.asarray((GAIN * green).astype(np.float32))
    high, low = split(green)
    packed = len(sides) == 1
    shapes = [jax.ShapeDtypeStruct((total * ch, 3 * LANES), BF)]
    if not packed:
        shapes.append(jax.ShapeDtypeStruct((LEFT + RIGHT + 2, total, ch), F32))
    return pl.pallas_call(
        functools.partial(lon_kernel, packed=packed),
        out_shape=shapes,
        cost_estimate=pl.CostEstimate(
            flops=6 * total * LANES * LANES * ch, bytes_accessed=8 * x.size, transcendentals=0
        ),
        compiler_params=pltpu.CompilerParams(vmem_limit_bytes=VMEM_LIMIT),
        name="lon_solve",
    )(x, *sides, jnp.concatenate([high, high, low], axis=0))


def tap_kernel(meta_ref, base_ref, *refs, tables, count, cols, cap, span, width, at):
    mine_at = lax.axis_index("lon") * width + at
    meta = lambda k: meta_ref[mine_at + k]
    table_refs, refs = refs[:tables], refs[tables + 1 :]
    cells_refs, tri_ref = refs[:count], refs[count]
    out_refs = refs[count + 1 : 2 * count + 1]
    rank, words, got, tab, near, later, packed, ct_ref, sems, table_sem = refs[2 * count + 1 :]
    for n, table_ref in enumerate(table_refs):

        @pl.when(meta(count + 1) == n)
        def _(table_ref=table_ref):
            pltpu.make_async_copy(table_ref, ct_ref, table_sem).start()

    rows = rank.shape[1]
    pairs = rows // 2
    ch = packed.shape[2]
    window = TAPS + 1
    band = lax.axis_index("lat")
    origin = (meta(count) * cols).astype(F32)
    for d in range(count):
        local = cells_refs[d][0, 0] - origin
        mine = (local >= 0.0) & (local < float(cols))
        one = jnp.where(mine, 1.0, 0.0)
        rank[d] = jnp.where(mine, dot(one.astype(BF), tri_ref[...]), -1000.0)
        parts = [local, cells_refs[d][0, 1] - (band * rows - UP).astype(F32)]
        for w in (2, 3):
            left = cells_refs[d][0, w]
            for _ in range(3):
                part = left.astype(BF).astype(F32)
                parts.append(part)
                left = left - part
        for w, part in enumerate(parts):
            words[d, :, w, :] = part
    for buffer in (near, later):
        for k in range(3):
            buffer[k * LANES + span : (k + 1) * LANES] = jnp.zeros((LANES - span, count * LANES), BF)
    column = lax.broadcasted_iota(jnp.int32, (span, count * LANES), 0).astype(F32)
    slot = lax.broadcasted_iota(jnp.int32, (LANES, LANES), 0)
    place = slot.astype(F32)

    def spot(j, d):
        start = meta(count + 2 + d) + 2 * j
        base = base_ref[start]
        return base, lax.rem(base, 8), base_ref[start + 1] - base, base_ref[start + 2] - base

    def gather(j, lap):
        i = 2 * j
        found = []
        for d in range(count):
            _, odd, count_first, _ = spot(j, d)
            skip = odd - lap * LANES
            picks = [
                jnp.where(place == rank[d, pl.ds(i, 1)] + skip.astype(F32), 1.0, 0.0),
                jnp.where(place == rank[d, pl.ds(i + 1, 1)] + (skip + count_first).astype(F32), 1.0, 0.0),
            ]
            found.append(
                lax.dot_general(
                    jnp.concatenate([words[d, i], words[d, i + 1]], axis=1).astype(BF),
                    jnp.concatenate(picks, axis=1).astype(BF),
                    (((1,), (1,)), ((), ())),
                    preferred_element_type=F32,
                )
            )
        return found

    def keep(j, found):
        for d in range(count):
            got[j, :, d * LANES : (d + 1) * LANES] = found[d]

    def weigh(read, write, first):
        a = spline_weights(read(2) + read(3) + read(4))
        b = spline_weights(read(5) + read(6) + read(7))
        turn = read(1) - 1.0 - first
        write(0, read(0))
        for n in range(4):
            write(1 + n, b[n])
        for e in range(window):
            total = jnp.zeros_like(turn)
            for t in range(4):
                if 0 <= e - t < 4:
                    total = jnp.where(turn == float(t), a[e - t], total)
            write(5 + e, total)

    def write_all(n, value):
        tab[:, n, :] = value

    def build(j, buffer):
        far = column - tab[j, 0:1]
        basis = jnp.where(far == 0.0, tab[j, 1:2], 0.0)
        for n in range(1, 4):
            basis = jnp.where(far == float(n), tab[j, 1 + n : 2 + n], basis)
        high, low = split(basis)
        buffer[0:span] = high
        buffer[LANES : LANES + span] = high
        buffer[2 * LANES : 2 * LANES + span] = low

    def emit(j, buffer, lap):
        half = window * ch // 2
        lines = []
        for part in range(2):
            first = pl.multiple_of(2 * j * ch + part * half, half)
            lines.append(dot(ct_ref[pl.ds(first, half)], buffer[...]))
        lines = jnp.concatenate(lines, axis=0)
        terms = [lines[e * ch : (e + 1) * ch] * tab[j, 5 + e : 6 + e] for e in range(window)]
        value = ((terms[0] + terms[1]) + (terms[2] + terms[3])) + ((terms[4] + terms[5]) + terms[6])
        for d in range(count):
            turned = value[:, d * LANES : (d + 1) * LANES].T
            base, odd, _, total = spot(j, d)
            to = pl.multiple_of(base - odd + lap * LANES, 8)
            if lap:
                whole = pl.ds(to, LANES)
                packed[d, whole] = jnp.where(slot < odd + total - lap * LANES, turned, packed[d, whole])
            else:
                packed[d, pl.ds(to, 8)] = jnp.where(slot[:8] < odd, packed[d, pl.ds(to, 8)], turned[:8])
                packed[d, pl.ds(pl.multiple_of(to + 8, 8), LANES - 8)] = turned[8:]

    @pl.loop(0, pairs // 2)
    def _(k):
        found = [gather(2 * k, 0), gather(2 * k + 1, 0)]
        keep(2 * k, found[0])
        keep(2 * k + 1, found[1])

    even = 2 * lax.broadcasted_iota(jnp.int32, (pairs, count * LANES), 0)
    weigh(lambda w: got[:, w, :], write_all, even.astype(F32))
    build(0, near)
    pltpu.make_async_copy(table_refs[0], ct_ref, table_sem).wait()

    @pl.loop(0, pairs // 2)
    def _(k):
        emit(2 * k, near, 0)
        build(2 * k + 1, later)
        emit(2 * k + 1, later, 0)
        build(jnp.minimum(2 * k + 2, pairs - 1), near)

    @pl.loop(0, pairs)
    def _(j):
        over = False
        for d in range(count):
            _, odd, _, total = spot(j, d)
            over = over | (odd + total > LANES)

        @pl.when(over)
        def _():
            keep(j, gather(j, 1))

            def write_one(n, value):
                tab[j, n : n + 1] = value

            weigh(lambda w: got[j, w : w + 1], write_one, (2 * j).astype(F32))
            build(j, near)
            emit(j, near, 1)

    copies = [
        pltpu.make_async_copy(packed.at[d, pl.ds(0, cap)], out_refs[d], sems.at[d]) for d in range(count)
    ]
    for copy in copies:
        copy.start()
    for copy in copies:
        copy.wait()


def taps(meta, width, at, count, base, tables, cells, cols, cap, after):
    _, words, rows, lanes = cells.shape
    ch = tables[0].shape[0] // (rows + UP + DOWN)
    span = 112
    tri = jnp.asarray(np.triu(np.ones((lanes, lanes)), 1), BF)
    weights = pltpu.VMEM((3 * LANES, count * lanes), BF)
    return pl.pallas_call(
        functools.partial(
            tap_kernel, tables=len(tables), count=count, cols=cols, cap=cap, span=span, width=width, at=at
        ),
        out_shape=[jax.ShapeDtypeStruct((cap, ch), F32)] * count,
        grid_spec=pltpu.PrefetchScalarGridSpec(
            num_scalar_prefetch=2,
            grid=(1,),
            in_specs=[pl.BlockSpec(memory_space=pl.ANY)] * (len(tables) + 1)
            + [
                pl.BlockSpec((1, words, rows, lanes), functools.partial(lambda g, m, b, k: (m[lax.axis_index("lon") * width + k], 0, 0, 0), k=at + k))
                for k in range(count)
            ]
            + [pl.BlockSpec(tri.shape, lambda g, m, b: (0, 0))],
            out_specs=[pl.BlockSpec(memory_space=pl.ANY)] * count,
            scratch_shapes=[
                pltpu.VMEM((count, rows, lanes), F32),
                pltpu.VMEM((count, rows, 8, lanes), F32),
                pltpu.VMEM((rows // 2, 8, count * lanes), F32),
                pltpu.VMEM((rows // 2, 16, count * lanes), F32),
                weights,
                weights,
                pltpu.VMEM((count, cap + 2 * lanes + 8, ch), F32),
                pltpu.VMEM(tables[0].shape, BF),
                pltpu.SemaphoreType.DMA((count,)),
                pltpu.SemaphoreType.DMA,
            ],
        ),
        cost_estimate=pl.CostEstimate(
            flops=6 * count * rows * TAPS * LANES * ch * LANES, bytes_accessed=2 * tables[0].size, transcendentals=0
        ),
        compiler_params=pltpu.CompilerParams(vmem_limit_bytes=VMEM_LIMIT),
        name="taps",
    )(meta, base, *tables, after, *([cells] * count), tri)


def place_kernel(target_ref, *refs, cap):
    *parts, out_ref, gathered, sems = refs
    copies = [
        pltpu.make_async_copy(part, gathered.at[pl.ds(k * cap, cap)], sems.at[k]) for k, part in enumerate(parts)
    ]
    for copy in copies:
        copy.start()
    for copy in copies:
        copy.wait()

    @pl.loop(0, out_ref.shape[0] // 32)
    def _(group):
        at = pl.multiple_of(group * 32, 32)
        for k in range(32):
            out_ref[pl.ds(at + k, 1)] = gathered[pl.ds(target_ref[at + k], 1)]


def place(target, parts):
    cap, ch = parts[0].shape
    cells = target.shape[0]
    count = len(parts)
    return pl.pallas_call(
        functools.partial(place_kernel, cap=cap),
        out_shape=jax.ShapeDtypeStruct((cells, ch), F32),
        grid_spec=pltpu.PrefetchScalarGridSpec(
            num_scalar_prefetch=1,
            grid=(1,),
            in_specs=[pl.BlockSpec(memory_space=pl.ANY)] * count,
            out_specs=pl.BlockSpec((cells, ch), lambda g, t: (0, 0)),
            scratch_shapes=[pltpu.VMEM((count * cap, ch), F32), pltpu.SemaphoreType.DMA((count,))],
        ),
        cost_estimate=pl.CostEstimate(flops=0, bytes_accessed=8 * count * cap * ch, transcendentals=0),
        compiler_params=pltpu.CompilerParams(vmem_limit_bytes=16 * 1024 * 1024),
        name="place",
    )(target, *parts)


def earlier(mask):
    _, cols = mask.shape[1:]
    ones = mask.astype(F32)
    before = lax.dot_general(
        mask.astype(BF),
        jnp.asarray(np.triu(np.ones((cols, cols)), 1), BF),
        (((2,), (0,)), ((), ())),
        preferred_element_type=F32,
    )
    return before, bases(ones)


def bases(ones):
    rows = ones.shape[1]
    totals = jnp.sum(ones, axis=2)
    return jnp.dot(totals, jnp.asarray(np.triu(np.ones((rows, rows + 1)), 1), F32), precision=lax.Precision.HIGHEST)


def transport(tracers, owners, columns, lat_shift, fractions):
    rows, cols, ch = tracers.shape
    bands = lax.axis_size("lat")
    sectors = lax.axis_size("lon")
    me = lax.axis_index("lon")
    cells = rows * cols
    cap = 3 * cells // sectors
    quarter = sectors // 4
    at = lambda q, o: q * quarter + o
    mirror = [(at(q, o), at((0, 2, 1, 3)[q], o)) for q in (1, 2) for o in range(quarter)]
    mine, offset = me // quarter, me % quarter
    middle = (mine == 1) | (mine == 2)

    head = 5 * rows // 8
    first = lax.ppermute(tracers[:head], "lon", mirror)
    owner = owners.reshape(rows, cols)
    down, up, top, bottom, words = edges(tracers, owner, columns, lat_shift, fractions)
    above = lax.ppermute(down, "lat", [(i, i + 1) for i in range(bands - 1)])
    below = lax.ppermute(up, "lat", [(i + 1, i) for i in range(bands - 1)])
    asked = lax.all_to_all(words, "lon", split_axis=0, concat_axis=0, tiled=True)

    x, right, left, rest = lat_solve(rows, head, [tracers], (above, below, top, bottom))
    west = lax.ppermute(right, "lon", [(i, (i + 1) % sectors) for i in range(sectors)])
    east = lax.ppermute(left, "lon", [((i + 1) % sectors, i) for i in range(sectors)])
    origins = np.array([[s * cols, dict(mirror).get(s, s) * cols] for s in range(sectors)], np.float32)
    local = asked[None, :, 0] - jnp.asarray(origins)[me][:, None, None, None]
    inside = ((local >= 0.0) & (local < float(cols))).astype(F32).reshape(2 * sectors, rows, -1)
    base = bases(inside).astype(jnp.int32).reshape(-1)

    own, sides = lon_solve(x, west, east)
    rest = lax.ppermute(rest, "lon", mirror)
    sides = lax.ppermute(sides, "lon", mirror)
    late_owner, x = lax.optimization_barrier((owner, x))
    every = jnp.arange(sectors, dtype=jnp.int32)
    mask = late_owner[None] == every[:, None, None]
    before, own_base = earlier(mask)
    slot = jnp.sum(jnp.where(mask, before + own_base[:, :-1, None], 0.0), axis=0).astype(jnp.int32)
    q = late_owner // quarter
    alike = ((q == 1) | (q == 2)) == middle
    early = ((q == 1) | (q == 2)) == (q // 2 == mine // 2)
    part = jnp.where(early, jnp.where(alike, 1, 0), jnp.where(alike, 3, 2)) * quarter
    target = ((part + (offset - late_owner) % quarter) * cap + slot).reshape(cells)

    goals = ((2, 0, 3, 1), (3, 1, 2, 0), (1, 0, 3, 2), (0, 1, 2, 3))
    shifts = list(range(quarter))[::-1]
    calls = [(group, shifts[n : n + 2]) for group in range(4) for n in range(0, quarter, 2)]
    plan = []
    for s in range(sectors):
        k, o = s // quarter, s % quarter
        row = []
        for group, pair in calls:
            which = int(group >= 2 and k in (1, 2))
            dests = [at(goals[group][k], (o + a) % quarter) for a in pair]
            row += dests + [dict(mirror).get(s, s) if which else s, which]
            row += [(which * sectors + dest) * (rows + 1) for dest in dests]
        plan.append(row)
    meta, width = jnp.asarray(np.array(plan, np.int32).reshape(-1)), len(plan[0])

    parts = [None] * sectors
    tables, done, values = [own], 0, [own]
    for group, pair in calls:
        if group == 2 and len(tables) == 1:
            other = lat_solve(rows, head, [first, rest])[0]
            tables = [own, lon_solve(other, sides)[0]]
        values = taps(meta, width, done, len(pair), base, tables, asked, cols, cap, values[0])
        done += 2 * len(pair) + 2
        for a, value in zip(pair, values):
            moves = [(at(k, o), at(goals[group][k], (o + a) % quarter)) for k in range(4) for o in range(quarter)]
            if any(i != j for i, j in moves):
                value = lax.ppermute(value, "lon", moves)
            parts[group * quarter + a] = value
    return place(target, parts).reshape(rows, cols, ch)


def solution(mesh):
    in_specs = (
        P("lat", "lon", None),
        P("lat", "lon", None, None),
        P("lat", "lon"),
        P("lat", "lon"),
        P(None, "lat", "lon"),
    )
    out_specs = P("lat", "lon", None)
    return jax.shard_map(transport, mesh=mesh, in_specs=in_specs, out_specs=out_specs, check_vma=False)
```

```python
import functools
import math

import jax
import jax.numpy as jnp
import numpy as np
from jax import lax
from jax.experimental import pallas as pl
from jax.experimental.pallas import tpu as pltpu
from jax.sharding import PartitionSpec as P


POLE = math.sqrt(3.0) - 2.0
GAIN = math.sqrt(3.0)
LANES = 128
TAPS = 6
UP, DOWN = 2, 3
LEFT, RIGHT = 1, 2
BF = jnp.bfloat16
F32 = jnp.float32
VMEM_LIMIT = 60 * 1024 * 1024


def split(x):
    high = x.astype(BF)
    return high, (x - high.astype(F32)).astype(BF)


def thirds(x):
    high, low = split(x)
    return jnp.concatenate([high, low, high], axis=1)


def dot(a, b):
    return lax.dot_general(a, b, (((1,), (0,)), ((), ())), preferred_element_type=F32)


def spline_weights(shift):
    rest = 1.0 - shift
    cube = shift * shift * shift
    return [
        rest * rest * rest / 6.0,
        (3.0 * cube - 6.0 * shift * shift + 4.0) / 6.0,
        (-3.0 * cube + 3.0 * shift * shift + 3.0 * shift + 1.0) / 6.0,
        cube / 6.0,
    ]


def edge_kernel(
    s_ref, owner_ref, column_ref, shift_ref, frac_ref, down_ref, up_ref, top_ref, bottom_ref, words_ref
):
    rows, cols = s_ref.shape[:2]
    top_row = lax.axis_index("lat") * rows
    lat_total = rows * lax.axis_size("lat")
    arrival = lax.broadcasted_iota(jnp.int32, (rows, cols), 0) + top_row
    row = jnp.clip(arrival - 1 + shift_ref[...], 1, lat_total - 3).astype(F32)
    column = (owner_ref[...] * cols + column_ref[...]).astype(F32)
    for k in range(words_ref.shape[0]):
        for w, word in enumerate((column, row, frac_ref[0], frac_ref[1])):
            words_ref[k, w] = jnp.full((rows, LANES), -1.0, F32)
            words_ref[k, w, :, :cols] = word
    first, last = s_ref[0], s_ref[rows - 1]
    far = 1.0 / (1.0 - POLE)

    acc = s_ref[0]
    for r in range(1, rows - UP):
        acc = s_ref[r] + POLE * acc
        if r == rows - 2 - DOWN:
            bottom_ref[DOWN] = 2.0 * far * last - acc
    down_ref[0] = acc
    for k in range(UP):
        down_ref[1 + k] = s_ref[rows - UP + k]
    for k in range(DOWN):
        bottom_ref[k] = 2.0 * last - s_ref[rows - 2 - k]

    acc = s_ref[rows - 1]
    for r in range(rows - 2, DOWN - 1, -1):
        acc = s_ref[r] + POLE * acc
    up_ref[DOWN] = acc
    for k in range(DOWN):
        up_ref[k] = s_ref[k]
    low = s_ref[rows - 1]
    for r in range(rows - 2, UP, -1):
        low = s_ref[r] + POLE * low
    top_ref[0] = 2.0 * far * first - low
    for k in range(UP):
        top_ref[1 + k] = 2.0 * first - s_ref[UP - k]


def edges(s, owner, columns, lat_shift, fractions):
    rows, cols, ch = s.shape
    shape = lambda n: jax.ShapeDtypeStruct((n, cols, ch), F32)
    words = jax.ShapeDtypeStruct((lax.axis_size("lon"), 4, rows, LANES), F32)
    return pl.pallas_call(
        edge_kernel,
        out_shape=(shape(UP + 1), shape(DOWN + 1), shape(UP + 1), shape(DOWN + 1), words),
        cost_estimate=pl.CostEstimate(flops=6 * s.size, bytes_accessed=6 * s.size, transcendentals=0),
        compiler_params=pltpu.CompilerParams(vmem_limit_bytes=VMEM_LIMIT),
        name="edges",
    )(s, owner, columns, lat_shift, fractions)


def lat_kernel(*refs, pieces, head):
    s_refs, refs = refs[:pieces], refs[pieces:]
    if pieces == 1:
        above_ref, below_ref, top_ref, bottom_ref, wr_ref, wl_ref, out_ref, right_ref, left_ref, rest_ref = refs
        rows, cols, _ = s_refs[0].shape
    else:
        wr_ref, wl_ref, out_ref, right_ref, left_ref = refs
        cols = s_refs[0].shape[1]
        rows = out_ref.shape[0] - UP - DOWN
    band = lax.axis_index("lat")
    at_top = band == 0
    at_bottom = band == lax.axis_size("lat") - 1
    total = rows + UP + DOWN

    def over(k):
        if pieces == 1:
            return jnp.where(at_top, top_ref[k], above_ref[k])
        return s_refs[1][rows - head + k]

    def under(k):
        if pieces == 1:
            return jnp.where(at_bottom, bottom_ref[k], below_ref[k])
        return s_refs[1][rows - head + UP + 1 + k]

    def row(e):
        if e < UP:
            return over(1 + e)
        if e >= UP + rows:
            return under(e - UP - rows)
        if pieces == 1 or e - UP < head:
            return s_refs[0][e - UP]
        return s_refs[1][e - UP - head]

    if pieces == 1:
        for r in range(head, rows):
            rest_ref[r - head] = s_refs[0][r]
        for k in range(UP + 1):
            rest_ref[rows - head + k] = over(k)
        for k in range(DOWN + 1):
            rest_ref[rows - head + UP + 1 + k] = under(k)

    acc = under(DOWN)
    for e in range(total - 1, -1, -1):
        acc = POLE * acc
        out_ref[e] = acc
        acc = acc + row(e)
    acc = over(0)
    for e in range(total):
        acc = row(e) + POLE * acc
        value = GAIN * (out_ref[e] + acc)
        out_ref[e] = value
        right_ref[0, pl.ds(e, 1)] = jnp.sum(value * wr_ref[...], axis=0, keepdims=True)
        for k in range(LEFT):
            right_ref[1 + k, pl.ds(e, 1)] = value[cols - LEFT + k : cols - LEFT + k + 1]
        for k in range(RIGHT):
            left_ref[k, pl.ds(e, 1)] = value[k : k + 1]
        left_ref[RIGHT, pl.ds(e, 1)] = jnp.sum(value * wl_ref[...], axis=0, keepdims=True)


def lat_solve(rows, head, pieces, halos=()):
    _, cols, ch = pieces[0].shape
    total = rows + UP + DOWN
    place = np.arange(cols)
    wr = np.where(place < cols - LEFT, POLE ** np.maximum(cols - LEFT - 1 - place, 0), 0.0)
    wl = np.where(place >= RIGHT, POLE ** np.maximum(place - RIGHT, 0), 0.0)
    wide = lambda w: jnp.asarray(np.broadcast_to(w[:, None], (cols, ch)).astype(np.float32))
    size = rows * cols * ch
    shapes = [
        jax.ShapeDtypeStruct((total, cols, ch), F32),
        jax.ShapeDtypeStruct((LEFT + 1, total, ch), F32),
        jax.ShapeDtypeStruct((RIGHT + 1, total, ch), F32),
    ]
    if halos:
        shapes.append(jax.ShapeDtypeStruct((rows - head + UP + DOWN + 2, cols, ch), F32))
    return pl.pallas_call(
        functools.partial(lat_kernel, pieces=len(pieces), head=head),
        out_shape=shapes,
        cost_estimate=pl.CostEstimate(flops=10 * size, bytes_accessed=10 * size, transcendentals=0),
        compiler_params=pltpu.CompilerParams(vmem_limit_bytes=VMEM_LIMIT),
        name="lat_solve",
    )(*pieces, *halos, wide(wr), wide(wl))


def lon_kernel(x_ref, *refs, packed):
    if packed:
        sides_ref, green_ref, out_ref = refs
    else:
        west_ref, east_ref, green_ref, out_ref, sides_ref = refs
        sides_ref[: LEFT + 1] = west_ref[...]
        sides_ref[LEFT + 1 :] = east_ref[...]
    total, cols, ch = x_ref.shape
    pad = LANES - cols - (LEFT + RIGHT + 2)
    for e in range(total):
        parts = [x_ref[e]]
        if packed:
            parts += [sides_ref[k, pl.ds(e, 1)] for k in range(LEFT + RIGHT + 2)]
        else:
            parts += [west_ref[k, pl.ds(e, 1)] for k in range(LEFT + 1)]
            parts += [east_ref[k, pl.ds(e, 1)] for k in range(RIGHT + 1)]
        parts += [jnp.zeros((pad, ch), F32)]
        turned = jnp.concatenate(parts, axis=0).T
        value = dot(thirds(turned), green_ref[...])
        out_ref[e * ch : (e + 1) * ch] = thirds(value)


def lon_solve(x, *sides):
    total, cols, ch = x.shape
    width = cols + LEFT + RIGHT
    j = np.arange(width) - LEFT
    green = np.zeros((LANES, LANES))
    green[:cols, :width] = POLE ** np.abs(np.arange(cols)[:, None] - j[None, :])
    green[cols, :width] = POLE ** (j + LEFT + 1)
    for k in range(LEFT):
        green[cols + 1 + k, :width] = POLE ** np.abs(j - (k - LEFT))
    for k in range(RIGHT):
        green[cols + LEFT + 1 + k, :width] = POLE ** np.abs(j - (cols + k))
    green[cols + LEFT + 1 + RIGHT, :width] = POLE ** (cols + RIGHT - j)
    green = jnp.asarray((GAIN * green).astype(np.float32))
    high, low = split(green)
    packed = len(sides) == 1
    shapes = [jax.ShapeDtypeStruct((total * ch, 3 * LANES), BF)]
    if not packed:
        shapes.append(jax.ShapeDtypeStruct((LEFT + RIGHT + 2, total, ch), F32))
    return pl.pallas_call(
        functools.partial(lon_kernel, packed=packed),
        out_shape=shapes,
        cost_estimate=pl.CostEstimate(
            flops=6 * total * LANES * LANES * ch, bytes_accessed=8 * x.size, transcendentals=0
        ),
        compiler_params=pltpu.CompilerParams(vmem_limit_bytes=VMEM_LIMIT),
        name="lon_solve",
    )(x, *sides, jnp.concatenate([high, high, low], axis=0))


def tap_kernel(meta_ref, base_ref, *refs, tables, count, cols, cap, span, width, at):
    mine_at = lax.axis_index("lon") * width + at
    meta = lambda k: meta_ref[mine_at + k]
    table_refs, refs = refs[:tables], refs[tables + 1 :]
    cells_refs, tri_ref = refs[:count], refs[count]
    out_refs = refs[count + 1 : 2 * count + 1]
    rank, words, got, tab, near, later, packed, ct_ref, sems, table_sem = refs[2 * count + 1 :]
    for n, table_ref in enumerate(table_refs):

        @pl.when(meta(count + 1) == n)
        def _(table_ref=table_ref):
            pltpu.make_async_copy(table_ref, ct_ref, table_sem).start()

    rows = rank.shape[1]
    pairs = rows // 2
    ch = packed.shape[2]
    window = TAPS + 1
    band = lax.axis_index("lat")
    origin = (meta(count) * cols).astype(F32)
    for d in range(count):
        local = cells_refs[d][0, 0] - origin
        mine = (local >= 0.0) & (local < float(cols))
        one = jnp.where(mine, 1.0, 0.0)
        rank[d] = jnp.where(mine, dot(one.astype(BF), tri_ref[...]), -1000.0)
        parts = [local, cells_refs[d][0, 1] - (band * rows - UP).astype(F32)]
        for w in (2, 3):
            left = cells_refs[d][0, w]
            for _ in range(3):
                part = left.astype(BF).astype(F32)
                parts.append(part)
                left = left - part
        for w, part in enumerate(parts):
            words[d, :, w, :] = part
    for buffer in (near, later):
        for k in range(3):
            buffer[k * LANES + span : (k + 1) * LANES] = jnp.zeros((LANES - span, count * LANES), BF)
    column = lax.broadcasted_iota(jnp.int32, (span, count * LANES), 0).astype(F32)
    slot = lax.broadcasted_iota(jnp.int32, (LANES, LANES), 0)
    place = slot.astype(F32)

    def spot(j, d):
        start = meta(count + 2 + d) + 2 * j
        base = base_ref[start]
        return base, lax.rem(base, 8), base_ref[start + 1] - base, base_ref[start + 2] - base

    def gather(j, lap):
        i = 2 * j
        found = []
        for d in range(count):
            _, odd, count_first, _ = spot(j, d)
            skip = odd - lap * LANES
            picks = [
                jnp.where(place == rank[d, pl.ds(i, 1)] + skip.astype(F32), 1.0, 0.0),
                jnp.where(place == rank[d, pl.ds(i + 1, 1)] + (skip + count_first).astype(F32), 1.0, 0.0),
            ]
            found.append(
                lax.dot_general(
                    jnp.concatenate([words[d, i], words[d, i + 1]], axis=1).astype(BF),
                    jnp.concatenate(picks, axis=1).astype(BF),
                    (((1,), (1,)), ((), ())),
                    preferred_element_type=F32,
                )
            )
        return found

    def keep(j, found):
        for d in range(count):
            got[j, :, d * LANES : (d + 1) * LANES] = found[d]

    def weigh(read, write, first):
        a = spline_weights(read(2) + read(3) + read(4))
        b = spline_weights(read(5) + read(6) + read(7))
        turn = read(1) - 1.0 - first
        write(0, read(0))
        for n in range(4):
            write(1 + n, b[n])
        for e in range(window):
            total = jnp.zeros_like(turn)
            for t in range(4):
                if 0 <= e - t < 4:
                    total = jnp.where(turn == float(t), a[e - t], total)
            write(5 + e, total)

    def write_all(n, value):
        tab[:, n, :] = value

    def build(j, buffer):
        far = column - tab[j, 0:1]
        basis = jnp.where(far == 0.0, tab[j, 1:2], 0.0)
        for n in range(1, 4):
            basis = jnp.where(far == float(n), tab[j, 1 + n : 2 + n], basis)
        high, low = split(basis)
        buffer[0:span] = high
        buffer[LANES : LANES + span] = high
        buffer[2 * LANES : 2 * LANES + span] = low

    def emit(j, buffer, lap):
        half = window * ch // 2
        lines = []
        for part in range(2):
            first = pl.multiple_of(2 * j * ch + part * half, half)
            lines.append(dot(ct_ref[pl.ds(first, half)], buffer[...]))
        lines = jnp.concatenate(lines, axis=0)
        terms = [lines[e * ch : (e + 1) * ch] * tab[j, 5 + e : 6 + e] for e in range(window)]
        value = ((terms[0] + terms[1]) + (terms[2] + terms[3])) + ((terms[4] + terms[5]) + terms[6])
        for d in range(count):
            turned = value[:, d * LANES : (d + 1) * LANES].T
            base, odd, _, total = spot(j, d)
            to = pl.multiple_of(base - odd + lap * LANES, 8)
            if lap:
                whole = pl.ds(to, LANES)
                packed[d, whole] = jnp.where(slot < odd + total - lap * LANES, turned, packed[d, whole])
            else:
                packed[d, pl.ds(to, 8)] = jnp.where(slot[:8] < odd, packed[d, pl.ds(to, 8)], turned[:8])
                packed[d, pl.ds(pl.multiple_of(to + 8, 8), LANES - 8)] = turned[8:]

    @pl.loop(0, pairs // 2)
    def _(k):
        found = [gather(2 * k, 0), gather(2 * k + 1, 0)]
        keep(2 * k, found[0])
        keep(2 * k + 1, found[1])

    even = 2 * lax.broadcasted_iota(jnp.int32, (pairs, count * LANES), 0)
    weigh(lambda w: got[:, w, :], write_all, even.astype(F32))
    build(0, near)
    pltpu.make_async_copy(table_refs[0], ct_ref, table_sem).wait()

    @pl.loop(0, pairs // 2)
    def _(k):
        emit(2 * k, near, 0)
        build(2 * k + 1, later)
        emit(2 * k + 1, later, 0)
        build(jnp.minimum(2 * k + 2, pairs - 1), near)

    @pl.loop(0, pairs)
    def _(j):
        over = False
        for d in range(count):
            _, odd, _, total = spot(j, d)
            over = over | (odd + total > LANES)

        @pl.when(over)
        def _():
            keep(j, gather(j, 1))

            def write_one(n, value):
                tab[j, n : n + 1] = value

            weigh(lambda w: got[j, w : w + 1], write_one, (2 * j).astype(F32))
            build(j, near)
            emit(j, near, 1)

    copies = [
        pltpu.make_async_copy(packed.at[d, pl.ds(0, cap)], out_refs[d], sems.at[d]) for d in range(count)
    ]
    for copy in copies:
        copy.start()
    for copy in copies:
        copy.wait()


def taps(meta, width, at, count, base, tables, cells, cols, cap, after):
    _, words, rows, lanes = cells.shape
    ch = tables[0].shape[0] // (rows + UP + DOWN)
    span = 112
    tri = jnp.asarray(np.triu(np.ones((lanes, lanes)), 1), BF)
    weights = pltpu.VMEM((3 * LANES, count * lanes), BF)
    return pl.pallas_call(
        functools.partial(
            tap_kernel, tables=len(tables), count=count, cols=cols, cap=cap, span=span, width=width, at=at
        ),
        out_shape=[jax.ShapeDtypeStruct((cap, ch), F32)] * count,
        grid_spec=pltpu.PrefetchScalarGridSpec(
            num_scalar_prefetch=2,
            grid=(1,),
            in_specs=[pl.BlockSpec(memory_space=pl.ANY)] * (len(tables) + 1)
            + [
                pl.BlockSpec((1, words, rows, lanes), functools.partial(lambda g, m, b, k: (m[lax.axis_index("lon") * width + k], 0, 0, 0), k=at + k))
                for k in range(count)
            ]
            + [pl.BlockSpec(tri.shape, lambda g, m, b: (0, 0))],
            out_specs=[pl.BlockSpec(memory_space=pl.ANY)] * count,
            scratch_shapes=[
                pltpu.VMEM((count, rows, lanes), F32),
                pltpu.VMEM((count, rows, 8, lanes), F32),
                pltpu.VMEM((rows // 2, 8, count * lanes), F32),
                pltpu.VMEM((rows // 2, 16, count * lanes), F32),
                weights,
                weights,
                pltpu.VMEM((count, cap + 2 * lanes + 8, ch), F32),
                pltpu.VMEM(tables[0].shape, BF),
                pltpu.SemaphoreType.DMA((count,)),
                pltpu.SemaphoreType.DMA,
            ],
        ),
        cost_estimate=pl.CostEstimate(
            flops=6 * count * rows * TAPS * LANES * ch * LANES, bytes_accessed=2 * tables[0].size, transcendentals=0
        ),
        compiler_params=pltpu.CompilerParams(vmem_limit_bytes=VMEM_LIMIT),
        name="taps",
    )(meta, base, *tables, after, *([cells] * count), tri)


def place_kernel(target_ref, *refs, cap):
    *parts, out_ref, gathered, sems = refs
    copies = [
        pltpu.make_async_copy(part, gathered.at[pl.ds(k * cap, cap)], sems.at[k]) for k, part in enumerate(parts)
    ]
    for copy in copies:
        copy.start()
    for copy in copies:
        copy.wait()

    @pl.loop(0, out_ref.shape[0] // 32)
    def _(group):
        at = pl.multiple_of(group * 32, 32)
        for k in range(32):
            out_ref[pl.ds(at + k, 1)] = gathered[pl.ds(target_ref[at + k], 1)]


def place(target, parts):
    cap, ch = parts[0].shape
    cells = target.shape[0]
    count = len(parts)
    return pl.pallas_call(
        functools.partial(place_kernel, cap=cap),
        out_shape=jax.ShapeDtypeStruct((cells, ch), F32),
        grid_spec=pltpu.PrefetchScalarGridSpec(
            num_scalar_prefetch=1,
            grid=(1,),
            in_specs=[pl.BlockSpec(memory_space=pltpu.HBM)] * count,
            out_specs=pl.BlockSpec((cells, ch), lambda g, t: (0, 0)),
            scratch_shapes=[pltpu.VMEM((count * cap, ch), F32), pltpu.SemaphoreType.DMA((count,))],
        ),
        cost_estimate=pl.CostEstimate(flops=0, bytes_accessed=8 * count * cap * ch, transcendentals=0),
        compiler_params=pltpu.CompilerParams(vmem_limit_bytes=16 * 1024 * 1024),
        name="place",
    )(target, *parts)


def earlier(mask):
    _, cols = mask.shape[1:]
    ones = mask.astype(F32)
    before = lax.dot_general(
        mask.astype(BF),
        jnp.asarray(np.triu(np.ones((cols, cols)), 1), BF),
        (((2,), (0,)), ((), ())),
        preferred_element_type=F32,
    )
    return before, bases(ones)


def bases(ones):
    rows = ones.shape[1]
    totals = jnp.sum(ones, axis=2)
    return jnp.dot(totals, jnp.asarray(np.triu(np.ones((rows, rows + 1)), 1), F32), precision=lax.Precision.HIGHEST)


def transport(tracers, owners, columns, lat_shift, fractions):
    rows, cols, ch = tracers.shape
    bands = lax.axis_size("lat")
    sectors = lax.axis_size("lon")
    me = lax.axis_index("lon")
    cells = rows * cols
    cap = 3 * cells // sectors
    quarter = sectors // 4
    at = lambda q, o: q * quarter + o
    mirror = [(at(q, o), at((0, 2, 1, 3)[q], o)) for q in (1, 2) for o in range(quarter)]
    mine, offset = me // quarter, me % quarter
    middle = (mine == 1) | (mine == 2)

    head = 5 * rows // 8
    first = lax.ppermute(tracers[:head], "lon", mirror)
    owner = owners.reshape(rows, cols)
    down, up, top, bottom, words = edges(tracers, owner, columns, lat_shift, fractions)
    above = lax.ppermute(down, "lat", [(i, i + 1) for i in range(bands - 1)])
    below = lax.ppermute(up, "lat", [(i + 1, i) for i in range(bands - 1)])
    asked = lax.all_to_all(words, "lon", split_axis=0, concat_axis=0, tiled=True)

    x, right, left, rest = lat_solve(rows, head, [tracers], (above, below, top, bottom))
    west = lax.ppermute(right, "lon", [(i, (i + 1) % sectors) for i in range(sectors)])
    east = lax.ppermute(left, "lon", [((i + 1) % sectors, i) for i in range(sectors)])
    origins = np.array([[s * cols, dict(mirror).get(s, s) * cols] for s in range(sectors)], np.float32)
    local = asked[None, :, 0] - jnp.asarray(origins)[me][:, None, None, None]
    inside = ((local >= 0.0) & (local < float(cols))).astype(F32).reshape(2 * sectors, rows, -1)
    base = bases(inside).astype(jnp.int32).reshape(-1)

    own, sides = lon_solve(x, west, east)
    rest = lax.ppermute(rest, "lon", mirror)
    sides = lax.ppermute(sides, "lon", mirror)
    late_owner, x = lax.optimization_barrier((owner, x))
    every = jnp.arange(sectors, dtype=jnp.int32)
    mask = late_owner[None] == every[:, None, None]
    before, own_base = earlier(mask)
    slot = jnp.sum(jnp.where(mask, before + own_base[:, :-1, None], 0.0), axis=0).astype(jnp.int32)
    q = late_owner // quarter
    alike = ((q == 1) | (q == 2)) == middle
    near = q // 2 == mine // 2
    part = jnp.where(near, jnp.where(q == mine, 3, 0), jnp.where(alike, 2, 1)) * quarter
    target = ((part + (offset - late_owner) % quarter) * cap + slot).reshape(cells)

    goals = ((1, 0, 3, 2), (2, 0, 3, 1), (3, 1, 2, 0), (0, 1, 2, 3))
    shifts = list(range(quarter))[::-1]
    calls = [(group, shifts[n : n + 2]) for group in range(4) for n in range(0, quarter, 2)]
    plan = []
    for s in range(sectors):
        k, o = s // quarter, s % quarter
        row = []
        for group, pair in calls:
            which = int(group in (1, 2) and k in (1, 2))
            dests = [at(goals[group][k], (o + a) % quarter) for a in pair]
            row += dests + [dict(mirror).get(s, s) if which else s, which]
            row += [(which * sectors + dest) * (rows + 1) for dest in dests]
        plan.append(row)
    meta, width = jnp.asarray(np.array(plan, np.int32).reshape(-1)), len(plan[0])

    parts = [None] * sectors
    tables, done, values = [own], 0, [own]
    for group, pair in calls:
        if group == 1 and len(tables) == 1:
            other = lat_solve(rows, head, [first, rest])[0]
            tables = [own, lon_solve(other, sides)[0]]
        values = taps(meta, width, done, len(pair), base, tables, asked, cols, cap, values[0])
        done += 2 * len(pair) + 2
        for a, value in zip(pair, values):
            moves = [(at(k, o), at(goals[group][k], (o + a) % quarter)) for k in range(4) for o in range(quarter)]
            if any(i != j for i, j in moves):
                value = lax.ppermute(value, "lon", moves)
            parts[group * quarter + a] = value
    return place(target, parts).reshape(rows, cols, ch)


def solution(mesh):
    in_specs = (
        P("lat", "lon", None),
        P("lat", "lon", None, None),
        P("lat", "lon"),
        P("lat", "lon"),
        P(None, "lat", "lon"),
    )
    out_specs = P("lat", "lon", None)
    return jax.shard_map(transport, mesh=mesh, in_specs=in_specs, out_specs=out_specs, check_vma=False)
```

```python
import functools
import math

import jax
import jax.numpy as jnp
import numpy as np
from jax import lax
from jax.experimental import pallas as pl
from jax.experimental.pallas import tpu as pltpu
from jax.sharding import PartitionSpec as P


POLE = math.sqrt(3.0) - 2.0
GAIN = math.sqrt(3.0)
LANES = 128
TAPS = 6
UP, DOWN = 2, 3
LEFT, RIGHT = 1, 2
BF = jnp.bfloat16
F32 = jnp.float32
VMEM_LIMIT = 60 * 1024 * 1024


def split(x):
    high = x.astype(BF)
    return high, (x - high.astype(F32)).astype(BF)


def thirds(x):
    high, low = split(x)
    return jnp.concatenate([high, low, high], axis=1)


def dot(a, b):
    return lax.dot_general(a, b, (((1,), (0,)), ((), ())), preferred_element_type=F32)


def spline_weights(shift):
    rest = 1.0 - shift
    cube = shift * shift * shift
    return [
        rest * rest * rest / 6.0,
        (3.0 * cube - 6.0 * shift * shift + 4.0) / 6.0,
        (-3.0 * cube + 3.0 * shift * shift + 3.0 * shift + 1.0) / 6.0,
        cube / 6.0,
    ]


def edge_kernel(
    s_ref, owner_ref, column_ref, shift_ref, frac_ref, down_ref, up_ref, top_ref, bottom_ref, words_ref
):
    rows, cols = s_ref.shape[:2]
    top_row = lax.axis_index("lat") * rows
    lat_total = rows * lax.axis_size("lat")
    arrival = lax.broadcasted_iota(jnp.int32, (rows, cols), 0) + top_row
    row = jnp.clip(arrival - 1 + shift_ref[...], 1, lat_total - 3).astype(F32)
    column = (owner_ref[...] * cols + column_ref[...]).astype(F32)
    for w, word in enumerate((column, row, frac_ref[0], frac_ref[1])):
        words_ref[w] = jnp.full((rows, LANES), -1.0, F32)
        words_ref[w, :, :cols] = word
    first, last = s_ref[0], s_ref[rows - 1]
    far = 1.0 / (1.0 - POLE)

    acc = s_ref[0]
    for r in range(1, rows - UP):
        acc = s_ref[r] + POLE * acc
        if r == rows - 2 - DOWN:
            bottom_ref[DOWN] = 2.0 * far * last - acc
    down_ref[0] = acc
    for k in range(UP):
        down_ref[1 + k] = s_ref[rows - UP + k]
    for k in range(DOWN):
        bottom_ref[k] = 2.0 * last - s_ref[rows - 2 - k]

    acc = s_ref[rows - 1]
    for r in range(rows - 2, DOWN - 1, -1):
        acc = s_ref[r] + POLE * acc
    up_ref[DOWN] = acc
    for k in range(DOWN):
        up_ref[k] = s_ref[k]
    low = s_ref[rows - 1]
    for r in range(rows - 2, UP, -1):
        low = s_ref[r] + POLE * low
    top_ref[0] = 2.0 * far * first - low
    for k in range(UP):
        top_ref[1 + k] = 2.0 * first - s_ref[UP - k]


def edges(s, owner, columns, lat_shift, fractions):
    rows, cols, ch = s.shape
    shape = lambda n: jax.ShapeDtypeStruct((n, cols, ch), F32)
    words = jax.ShapeDtypeStruct((4, rows, LANES), F32)
    return pl.pallas_call(
        edge_kernel,
        out_shape=(shape(UP + 1), shape(DOWN + 1), shape(UP + 1), shape(DOWN + 1), words),
        cost_estimate=pl.CostEstimate(flops=6 * s.size, bytes_accessed=6 * s.size, transcendentals=0),
        compiler_params=pltpu.CompilerParams(vmem_limit_bytes=VMEM_LIMIT),
        name="edges",
    )(s, owner, columns, lat_shift, fractions)


def lat_kernel(*refs, pieces, head):
    s_refs, refs = refs[:pieces], refs[pieces:]
    if pieces == 1:
        above_ref, below_ref, top_ref, bottom_ref, wr_ref, wl_ref, out_ref, right_ref, left_ref, rest_ref = refs
        rows, cols, _ = s_refs[0].shape
    else:
        wr_ref, wl_ref, out_ref, right_ref, left_ref = refs
        cols = s_refs[0].shape[1]
        rows = out_ref.shape[0] - UP - DOWN
    band = lax.axis_index("lat")
    at_top = band == 0
    at_bottom = band == lax.axis_size("lat") - 1
    total = rows + UP + DOWN

    def over(k):
        if pieces == 1:
            return jnp.where(at_top, top_ref[k], above_ref[k])
        return s_refs[1][rows - head + k]

    def under(k):
        if pieces == 1:
            return jnp.where(at_bottom, bottom_ref[k], below_ref[k])
        return s_refs[1][rows - head + UP + 1 + k]

    def row(e):
        if e < UP:
            return over(1 + e)
        if e >= UP + rows:
            return under(e - UP - rows)
        if pieces == 1 or e - UP < head:
            return s_refs[0][e - UP]
        return s_refs[1][e - UP - head]

    if pieces == 1:
        for r in range(head, rows):
            rest_ref[r - head] = s_refs[0][r]
        for k in range(UP + 1):
            rest_ref[rows - head + k] = over(k)
        for k in range(DOWN + 1):
            rest_ref[rows - head + UP + 1 + k] = under(k)

    acc = under(DOWN)
    for e in range(total - 1, -1, -1):
        acc = POLE * acc
        out_ref[e] = acc
        acc = acc + row(e)
    acc = over(0)
    for e in range(total):
        acc = row(e) + POLE * acc
        value = GAIN * (out_ref[e] + acc)
        out_ref[e] = value
        right_ref[0, pl.ds(e, 1)] = jnp.sum(value * wr_ref[...], axis=0, keepdims=True)
        for k in range(LEFT):
            right_ref[1 + k, pl.ds(e, 1)] = value[cols - LEFT + k : cols - LEFT + k + 1]
        for k in range(RIGHT):
            left_ref[k, pl.ds(e, 1)] = value[k : k + 1]
        left_ref[RIGHT, pl.ds(e, 1)] = jnp.sum(value * wl_ref[...], axis=0, keepdims=True)


def lat_solve(rows, head, pieces, halos=()):
    _, cols, ch = pieces[0].shape
    total = rows + UP + DOWN
    place = np.arange(cols)
    wr = np.where(place < cols - LEFT, POLE ** np.maximum(cols - LEFT - 1 - place, 0), 0.0)
    wl = np.where(place >= RIGHT, POLE ** np.maximum(place - RIGHT, 0), 0.0)
    wide = lambda w: jnp.asarray(np.broadcast_to(w[:, None], (cols, ch)).astype(np.float32))
    size = rows * cols * ch
    shapes = [
        jax.ShapeDtypeStruct((total, cols, ch), F32),
        jax.ShapeDtypeStruct((LEFT + 1, total, ch), F32),
        jax.ShapeDtypeStruct((RIGHT + 1, total, ch), F32),
    ]
    if halos:
        shapes.append(jax.ShapeDtypeStruct((rows - head + UP + DOWN + 2, cols, ch), F32))
    return pl.pallas_call(
        functools.partial(lat_kernel, pieces=len(pieces), head=head),
        out_shape=shapes,
        cost_estimate=pl.CostEstimate(flops=10 * size, bytes_accessed=10 * size, transcendentals=0),
        compiler_params=pltpu.CompilerParams(vmem_limit_bytes=VMEM_LIMIT),
        name="lat_solve",
    )(*pieces, *halos, wide(wr), wide(wl))


def lon_kernel(x_ref, *refs, packed):
    if packed:
        sides_ref, green_ref, out_ref = refs
    else:
        west_ref, east_ref, green_ref, out_ref, sides_ref = refs
        sides_ref[: LEFT + 1] = west_ref[...]
        sides_ref[LEFT + 1 :] = east_ref[...]
    total, cols, ch = x_ref.shape
    pad = LANES - cols - (LEFT + RIGHT + 2)
    for e in range(total):
        parts = [x_ref[e]]
        if packed:
            parts += [sides_ref[k, pl.ds(e, 1)] for k in range(LEFT + RIGHT + 2)]
        else:
            parts += [west_ref[k, pl.ds(e, 1)] for k in range(LEFT + 1)]
            parts += [east_ref[k, pl.ds(e, 1)] for k in range(RIGHT + 1)]
        parts += [jnp.zeros((pad, ch), F32)]
        turned = jnp.concatenate(parts, axis=0).T
        value = dot(thirds(turned), green_ref[...])
        out_ref[e * ch : (e + 1) * ch] = thirds(value)


def lon_solve(x, *sides):
    total, cols, ch = x.shape
    width = cols + LEFT + RIGHT
    j = np.arange(width) - LEFT
    green = np.zeros((LANES, LANES))
    green[:cols, :width] = POLE ** np.abs(np.arange(cols)[:, None] - j[None, :])
    green[cols, :width] = POLE ** (j + LEFT + 1)
    for k in range(LEFT):
        green[cols + 1 + k, :width] = POLE ** np.abs(j - (k - LEFT))
    for k in range(RIGHT):
        green[cols + LEFT + 1 + k, :width] = POLE ** np.abs(j - (cols + k))
    green[cols + LEFT + 1 + RIGHT, :width] = POLE ** (cols + RIGHT - j)
    green = jnp.asarray((GAIN * green).astype(np.float32))
    high, low = split(green)
    packed = len(sides) == 1
    shapes = [jax.ShapeDtypeStruct((total * ch, 3 * LANES), BF)]
    if not packed:
        shapes.append(jax.ShapeDtypeStruct((LEFT + RIGHT + 2, total, ch), F32))
    return pl.pallas_call(
        functools.partial(lon_kernel, packed=packed),
        out_shape=shapes,
        cost_estimate=pl.CostEstimate(
            flops=6 * total * LANES * LANES * ch, bytes_accessed=8 * x.size, transcendentals=0
        ),
        compiler_params=pltpu.CompilerParams(vmem_limit_bytes=VMEM_LIMIT),
        name="lon_solve",
    )(x, *sides, jnp.concatenate([high, high, low], axis=0))


def tap_kernel(meta_ref, base_ref, *refs, tables, count, cols, cap, span, width, at):
    mine_at = lax.axis_index("lon") * width + at
    meta = lambda k: meta_ref[mine_at + k]
    table_refs, refs = refs[:tables], refs[tables + 1 :]
    cells_refs, tri_ref = refs[:count], refs[count]
    out_refs = refs[count + 1 : 2 * count + 1]
    rank, words, got, tab, near, later, packed, ct_ref, sems, table_sem = refs[2 * count + 1 :]
    for n, table_ref in enumerate(table_refs):

        @pl.when(meta(count + 1) == n)
        def _(table_ref=table_ref):
            pltpu.make_async_copy(table_ref, ct_ref, table_sem).start()

    rows = rank.shape[1]
    pairs = rows // 2
    ch = packed.shape[2]
    window = TAPS + 1
    band = lax.axis_index("lat")
    origin = (meta(count) * cols).astype(F32)
    for d in range(count):
        local = cells_refs[d][0] - origin
        mine = (local >= 0.0) & (local < float(cols))
        one = jnp.where(mine, 1.0, 0.0)
        rank[d] = jnp.where(mine, dot(one.astype(BF), tri_ref[...]), -1000.0)
        parts = [local, cells_refs[d][1] - (band * rows - UP).astype(F32)]
        for w in (2, 3):
            left = cells_refs[d][w]
            for _ in range(3):
                part = left.astype(BF).astype(F32)
                parts.append(part)
                left = left - part
        for w, part in enumerate(parts):
            words[d, :, w, :] = part
    for buffer in (near, later):
        for k in range(3):
            buffer[k * LANES + span : (k + 1) * LANES] = jnp.zeros((LANES - span, count * LANES), BF)
    column = lax.broadcasted_iota(jnp.int32, (span, count * LANES), 0).astype(F32)
    slot = lax.broadcasted_iota(jnp.int32, (LANES, LANES), 0)
    place = slot.astype(F32)

    def spot(j, d):
        start = meta(count + 2 + d) + 2 * j
        base = base_ref[start]
        return base, lax.rem(base, 8), base_ref[start + 1] - base, base_ref[start + 2] - base

    def gather(j, lap):
        i = 2 * j
        found = []
        for d in range(count):
            _, odd, count_first, _ = spot(j, d)
            skip = odd - lap * LANES
            picks = [
                jnp.where(place == rank[d, pl.ds(i, 1)] + skip.astype(F32), 1.0, 0.0),
                jnp.where(place == rank[d, pl.ds(i + 1, 1)] + (skip + count_first).astype(F32), 1.0, 0.0),
            ]
            found.append(
                lax.dot_general(
                    jnp.concatenate([words[d, i], words[d, i + 1]], axis=1).astype(BF),
                    jnp.concatenate(picks, axis=1).astype(BF),
                    (((1,), (1,)), ((), ())),
                    preferred_element_type=F32,
                )
            )
        return found

    def keep(j, found):
        for d in range(count):
            got[j, :, d * LANES : (d + 1) * LANES] = found[d]

    def weigh(read, write, first):
        a = spline_weights(read(2) + read(3) + read(4))
        b = spline_weights(read(5) + read(6) + read(7))
        turn = read(1) - 1.0 - first
        write(0, read(0))
        for n in range(4):
            write(1 + n, b[n])
        for e in range(window):
            total = jnp.zeros_like(turn)
            for t in range(4):
                if 0 <= e - t < 4:
                    total = jnp.where(turn == float(t), a[e - t], total)
            write(5 + e, total)

    def write_all(n, value):
        tab[:, n, :] = value

    def build(j, buffer):
        far = column - tab[j, 0:1]
        basis = jnp.where(far == 0.0, tab[j, 1:2], 0.0)
        for n in range(1, 4):
            basis = jnp.where(far == float(n), tab[j, 1 + n : 2 + n], basis)
        high, low = split(basis)
        buffer[0:span] = high
        buffer[LANES : LANES + span] = high
        buffer[2 * LANES : 2 * LANES + span] = low

    def emit(j, buffer, lap):
        half = window * ch // 2
        lines = []
        for part in range(2):
            first = pl.multiple_of(2 * j * ch + part * half, half)
            lines.append(dot(ct_ref[pl.ds(first, half)], buffer[...]))
        lines = jnp.concatenate(lines, axis=0)
        terms = [lines[e * ch : (e + 1) * ch] * tab[j, 5 + e : 6 + e] for e in range(window)]
        value = ((terms[0] + terms[1]) + (terms[2] + terms[3])) + ((terms[4] + terms[5]) + terms[6])
        for d in range(count):
            turned = value[:, d * LANES : (d + 1) * LANES].T
            base, odd, _, total = spot(j, d)
            to = pl.multiple_of(base - odd + lap * LANES, 8)
            if lap:
                whole = pl.ds(to, LANES)
                packed[d, whole] = jnp.where(slot < odd + total - lap * LANES, turned, packed[d, whole])
            else:
                packed[d, pl.ds(to, 8)] = jnp.where(slot[:8] < odd, packed[d, pl.ds(to, 8)], turned[:8])
                packed[d, pl.ds(pl.multiple_of(to + 8, 8), LANES - 8)] = turned[8:]

    @pl.loop(0, pairs // 2)
    def _(k):
        found = [gather(2 * k, 0), gather(2 * k + 1, 0)]
        keep(2 * k, found[0])
        keep(2 * k + 1, found[1])

    even = 2 * lax.broadcasted_iota(jnp.int32, (pairs, count * LANES), 0)
    weigh(lambda w: got[:, w, :], write_all, even.astype(F32))
    build(0, near)
    pltpu.make_async_copy(table_refs[0], ct_ref, table_sem).wait()

    @pl.loop(0, pairs // 2)
    def _(k):
        emit(2 * k, near, 0)
        build(2 * k + 1, later)
        emit(2 * k + 1, later, 0)
        build(jnp.minimum(2 * k + 2, pairs - 1), near)

    @pl.loop(0, pairs)
    def _(j):
        over = False
        for d in range(count):
            _, odd, _, total = spot(j, d)
            over = over | (odd + total > LANES)

        @pl.when(over)
        def _():
            keep(j, gather(j, 1))

            def write_one(n, value):
                tab[j, n : n + 1] = value

            weigh(lambda w: got[j, w : w + 1], write_one, (2 * j).astype(F32))
            build(j, near)
            emit(j, near, 1)

    copies = [
        pltpu.make_async_copy(packed.at[d, pl.ds(0, cap)], out_refs[d], sems.at[d]) for d in range(count)
    ]
    for copy in copies:
        copy.start()
    for copy in copies:
        copy.wait()


def taps(meta, width, at, count, base, tables, cells, cols, cap, after):
    words, rows, lanes = cells[0].shape
    ch = tables[0].shape[0] // (rows + UP + DOWN)
    span = 112
    tri = jnp.asarray(np.triu(np.ones((lanes, lanes)), 1), BF)
    weights = pltpu.VMEM((3 * LANES, count * lanes), BF)
    return pl.pallas_call(
        functools.partial(
            tap_kernel, tables=len(tables), count=count, cols=cols, cap=cap, span=span, width=width, at=at
        ),
        out_shape=[jax.ShapeDtypeStruct((cap, ch), F32)] * count,
        grid_spec=pltpu.PrefetchScalarGridSpec(
            num_scalar_prefetch=2,
            grid=(1,),
            in_specs=[pl.BlockSpec(memory_space=pl.ANY)] * (len(tables) + 1)
            + [pl.BlockSpec((words, rows, lanes), lambda g, m, b: (0, 0, 0))] * count
            + [pl.BlockSpec(tri.shape, lambda g, m, b: (0, 0))],
            out_specs=[pl.BlockSpec(memory_space=pl.ANY)] * count,
            scratch_shapes=[
                pltpu.VMEM((count, rows, lanes), F32),
                pltpu.VMEM((count, rows, 8, lanes), F32),
                pltpu.VMEM((rows // 2, 8, count * lanes), F32),
                pltpu.VMEM((rows // 2, 16, count * lanes), F32),
                weights,
                weights,
                pltpu.VMEM((count, cap + 2 * lanes + 8, ch), F32),
                pltpu.VMEM(tables[0].shape, BF),
                pltpu.SemaphoreType.DMA((count,)),
                pltpu.SemaphoreType.DMA,
            ],
        ),
        cost_estimate=pl.CostEstimate(
            flops=6 * count * rows * TAPS * LANES * ch * LANES, bytes_accessed=2 * tables[0].size, transcendentals=0
        ),
        compiler_params=pltpu.CompilerParams(vmem_limit_bytes=VMEM_LIMIT),
        name="taps",
    )(meta, base, *tables, after, *cells, tri)


def place_kernel(target_ref, *refs, cap):
    *parts, out_ref, gathered, sems = refs
    copies = [
        pltpu.make_async_copy(part, gathered.at[pl.ds(k * cap, cap)], sems.at[k]) for k, part in enumerate(parts)
    ]
    for copy in copies:
        copy.start()
    for copy in copies:
        copy.wait()

    @pl.loop(0, out_ref.shape[0] // 32)
    def _(group):
        at = pl.multiple_of(group * 32, 32)
        for k in range(32):
            out_ref[pl.ds(at + k, 1)] = gathered[pl.ds(target_ref[at + k], 1)]


def place(target, parts):
    cap, ch = parts[0].shape
    cells = target.shape[0]
    count = len(parts)
    return pl.pallas_call(
        functools.partial(place_kernel, cap=cap),
        out_shape=jax.ShapeDtypeStruct((cells, ch), F32),
        grid_spec=pltpu.PrefetchScalarGridSpec(
            num_scalar_prefetch=1,
            grid=(1,),
            in_specs=[pl.BlockSpec(memory_space=pltpu.HBM)] * count,
            out_specs=pl.BlockSpec((cells, ch), lambda g, t: (0, 0)),
            scratch_shapes=[pltpu.VMEM((count * cap, ch), F32), pltpu.SemaphoreType.DMA((count,))],
        ),
        cost_estimate=pl.CostEstimate(flops=0, bytes_accessed=8 * count * cap * ch, transcendentals=0),
        compiler_params=pltpu.CompilerParams(vmem_limit_bytes=16 * 1024 * 1024),
        name="place",
    )(target, *parts)


def earlier(mask):
    _, cols = mask.shape[1:]
    ones = mask.astype(F32)
    before = lax.dot_general(
        mask.astype(BF),
        jnp.asarray(np.triu(np.ones((cols, cols)), 1), BF),
        (((2,), (0,)), ((), ())),
        preferred_element_type=F32,
    )
    return before, bases(ones)


def bases(ones):
    rows = ones.shape[1]
    totals = jnp.sum(ones, axis=2)
    return jnp.dot(totals, jnp.asarray(np.triu(np.ones((rows, rows + 1)), 1), F32), precision=lax.Precision.HIGHEST)


def transport(tracers, owners, columns, lat_shift, fractions):
    rows, cols, ch = tracers.shape
    bands = lax.axis_size("lat")
    sectors = lax.axis_size("lon")
    me = lax.axis_index("lon")
    cells = rows * cols
    cap = 3 * cells // sectors
    quarter = sectors // 4
    at = lambda q, o: q * quarter + o
    mirror = [(at(q, o), at((0, 2, 1, 3)[q], o)) for q in (1, 2) for o in range(quarter)]
    mine, offset = me // quarter, me % quarter
    middle = (mine == 1) | (mine == 2)

    head = 5 * rows // 8
    first = lax.ppermute(tracers[:head], "lon", mirror)
    owner = owners.reshape(rows, cols)
    down, up, top, bottom, words = edges(tracers, owner, columns, lat_shift, fractions)
    above = lax.ppermute(down, "lat", [(i, i + 1) for i in range(bands - 1)])
    below = lax.ppermute(up, "lat", [(i + 1, i) for i in range(bands - 1)])
    goals = ((1, 0, 3, 2), (2, 0, 3, 1), (3, 1, 2, 0), (0, 1, 2, 3))
    shifts = list(range(quarter))[::-1]
    calls = [(group, shifts[n : n + 2]) for group in range(4) for n in range(0, quarter, 2)]
    plan = []
    for s in range(sectors):
        k, o = s // quarter, s % quarter
        row = []
        for group, pair in calls:
            which = int(group in (1, 2) and k in (1, 2))
            dests = [at(goals[group][k], (o + a) % quarter) for a in pair]
            row += dests + [dict(mirror).get(s, s) if which else s, which]
            row += [d * (rows + 1) for d in range(len(pair))]
        plan.append(row)
    meta, width = jnp.asarray(np.array(plan, np.int32).reshape(-1)), len(plan[0])

    def moves_of(group, a):
        return [(at(k, o), at(goals[group][k], (o + a) % quarter)) for k in range(4) for o in range(quarter)]

    asked = {}
    for group, pair in calls:
        for a in pair:
            back = [(j, i) for i, j in moves_of(group, a)]
            asked[group, a] = words
            if any(i != j for i, j in back):
                asked[group, a] = lax.ppermute(words, "lon", back)
    served = [[row[sum(2 * len(p) + 2 for _, p in calls[:n]) + len(pair)] for n, (_, pair) in enumerate(calls)] for row in plan]
    origins = jnp.asarray(np.array(served, np.float32) * cols)[me]

    x, right, left, rest = lat_solve(rows, head, [tracers], (above, below, top, bottom))
    west = lax.ppermute(right, "lon", [(i, (i + 1) % sectors) for i in range(sectors)])
    east = lax.ppermute(left, "lon", [((i + 1) % sectors, i) for i in range(sectors)])
    own, sides = lon_solve(x, west, east)
    rest = lax.ppermute(rest, "lon", mirror)
    sides = lax.ppermute(sides, "lon", mirror)
    late_owner, x = lax.optimization_barrier((owner, x))
    every = jnp.arange(sectors, dtype=jnp.int32)
    mask = late_owner[None] == every[:, None, None]
    before, own_base = earlier(mask)
    slot = jnp.sum(jnp.where(mask, before + own_base[:, :-1, None], 0.0), axis=0).astype(jnp.int32)
    q = late_owner // quarter
    alike = ((q == 1) | (q == 2)) == middle
    near = q // 2 == mine // 2
    part = jnp.where(near, jnp.where(q == mine, 3, 0), jnp.where(alike, 2, 1)) * quarter
    target = ((part + (offset - late_owner) % quarter) * cap + slot).reshape(cells)

    parts = [None] * sectors
    tables, done, values = [own], 0, [own]
    for group, pair in calls:
        if group == 1 and len(tables) == 1:
            other = lat_solve(rows, head, [first, rest])[0]
            tables = [own, lon_solve(other, sides)[0]]
        cells_of = [asked[group, a] for a in pair]
        local = jnp.stack([cells[0] for cells in cells_of]) - origins[calls.index((group, pair))]
        base = bases(((local >= 0.0) & (local < float(cols))).astype(F32)).astype(jnp.int32).reshape(-1)
        values = taps(meta, width, done, len(pair), base, tables, cells_of, cols, cap, values[0])
        done += 2 * len(pair) + 2
        for a, value in zip(pair, values):
            moves = moves_of(group, a)
            if any(i != j for i, j in moves):
                value = lax.ppermute(value, "lon", moves)
            parts[group * quarter + a] = value
    return place(target, parts).reshape(rows, cols, ch)


def solution(mesh):
    in_specs = (
        P("lat", "lon", None),
        P("lat", "lon", None, None),
        P("lat", "lon"),
        P("lat", "lon"),
        P(None, "lat", "lon"),
    )
    out_specs = P("lat", "lon", None)
    return jax.shard_map(transport, mesh=mesh, in_specs=in_specs, out_specs=out_specs, check_vma=False)
```
